32 devices in a mesh: expert: 4 (over z), fsdp: 8 (over y, x, core).
Axes of the slice: x: 2, y: 2, z: 4, core: 2. Of those that a mesh axis runs over, the one named last changes fastest.
Arguments:
- tokens: bfloat16 [25216, 512], P(('expert', 'fsdp')), may hold values from -6 to 6
- routes: int32 [25216, 2], P(('expert', 'fsdp')), may hold values from 0 to 7, all different within a row; in each aligned block of 788 rows (0 to 787, 788 to 1575, ...) at most 394 rows name the same one
- cotangent: bfloat16 [25216, 512], P(('expert', 'fsdp')), may hold values from -6 to 6
- attend_gain: float32 [512], P('fsdp'), may hold values from 0.5 to 1.5
- attend_bias: float32 [512], P('fsdp'), may hold values from -1.25 to 1.25
- triple_weight: float32 [512, 1536], P('fsdp'), may hold values from -0.25 to 0.25
- merge_weight: float32 [512, 512], P('fsdp'), may hold values from -2 to 2
- mixture_gain: float32 [512], P('fsdp'), may hold values from 0.5 to 1.5
- mixture_bias: float32 [512], P('fsdp'), may hold values from -1.25 to 1.25
- router_weight: float32 [512, 8], P('fsdp'), may hold values from -0.125 to 0.125
- expert_up: float32 [8, 512, 2048], P('expert', 'fsdp'), may hold values from -0.25 to 0.25
- expert_down: float32 [8, 2048, 512], P('expert', 'fsdp'), may hold values from -0.75 to 0.75
Outputs:
- block_out: bfloat16 [25216, 512], P(('expert', 'fsdp'))
- tokens_grad: float32 [25216, 512], P(('expert', 'fsdp'))
- attendgain_grad: float32 [512], P('fsdp')
- attendbias_grad: float32 [512], P('fsdp')
- triple_grad: float32 [512, 1536], P('fsdp')
- merge_grad: float32 [512, 512], P('fsdp')
- mixturegain_grad: float32 [512], P('fsdp')
- mixturebias_grad: float32 [512], P('fsdp')
- router_grad: float32 [512, 8], P('fsdp')
- expertup_grad: float32 [8, 512, 2048], P('expert', 'fsdp')
- expertdown_grad: float32 [8, 2048, 512], P('expert', 'fsdp')
The draws below stay inside these ranges and needn't reach their ends.
Inputs may be any that keep to these rules, and one draw needn't show every extreme that they name: `routes`: each token names 2 different experts. Among the 788 tokens of one device no expert is named by more than 394 tokens, a bound that some block reaches of them; every expert is named by some token.
All inputs are finite; a program needn't handle non-finite values.
Results may differ from the reference program's by a relative error of at most 0.02.
Values may be sent and summed in bfloat16 or wider, within the bound.
A program may use at most 192 MiB of HBM per device.

```python
import math
import jax
import jax.numpy as jnp
import numpy as np
from jax import lax

D = 512
HEADS = 8
HEAD_DIM = 64
FF = 2048
TOP = 2
SEQ = 197
IMG_DEV = 4
EXPERTS = 8
TOK_DEV = 788
CAP = 394
IMAGES = 128
TOKENS = 25216


def shard_levels(rng, extent, shards, smallest, top_value):
    factor_of, own = 1.0, jax.random.fold_in(rng, 6)
    for position, parts in shards:
        draws = jnp.exp(jax.random.uniform(jax.random.fold_in(own, position), (parts,), jnp.float32, smallest / len(shards), top_value / len(shards)))
        factor_of = factor_of * jnp.repeat(draws, extent[position] // parts).reshape([-1 if axis == position else 1 for axis in range(len(extent))])
    return factor_of


def shared_out(stream_key, own, number, rows, number_of, top, reach, skew):
    order = jax.random.permutation(stream_key, number_of)
    heavy_load, common = load_shares(number_of, rows * top, reach, skew, True), load_shares(number_of, rows * top, reach, skew, False)
    places = jnp.arange(number_of)

    def named(lengths, turn):
        used = int((lengths > 0).sum())
        fixed = max(1, used // 4)
        shifted = fixed + (places - fixed + turn * (used - fixed)) % max(1, number_of - fixed)
        return jnp.zeros((number_of,), jnp.int32).at[order[jnp.where(places < fixed, places, shifted)]].set(jnp.asarray(lengths, jnp.int32))

    lengths = jnp.where(number % 4 == 0, named(heavy_load, number // 4), named(common, number - number // 4 - 1))
    mixed = jax.random.permutation(jax.random.fold_in(own, 3), number_of)
    donor, receiver = mixed[0:number_of // 2 * 2:2], mixed[1:number_of // 2 * 2:2]
    slack = jnp.minimum(lengths[donor] - 1, reach - lengths[receiver]) // 2
    slack = jnp.where((donor == order[0]) | (receiver == order[0]) | (lengths[receiver] == 0), 0, jnp.maximum(slack, 0))
    shifted = jax.random.randint(jax.random.fold_in(own, 4), (number_of // 2,), 0, 1 << 20) % (slack + 1)
    lengths = lengths.at[donor].add(-shifted).at[receiver].add(shifted)
    members = jnp.searchsorted(jnp.cumsum(lengths), jnp.arange(rows * top), side="right").astype(jnp.int32)
    table = members.reshape(top, rows).T
    table = table[jax.random.permutation(jax.random.fold_in(own, 1), rows)]
    turn = jax.random.randint(jax.random.fold_in(own, 2), (rows, 1), 0, top)
    return jnp.take_along_axis(table, (jnp.arange(top)[None, :] + turn) % top, axis=1)


def load_shares(count, total, most, slope, full):
    loads = [(1 << 20) // math.isqrt(grade ** slope) + 1 for grade in range(1, count + 1)]
    largest = most if full else min(most, max(-(-total // count), total * loads[0] // sum(loads)))
    least = 1 if total - largest >= count - 1 else 0
    holding, surplus = [largest] + [least] * (count - 1), total - largest - least * (count - 1)
    while surplus > 0:
        movable = [i for i in range(1, count) if holding[i] < largest] or [i for i in range(1, count) if holding[i] < most]
        pool, remaining = sum([loads[i] for i in movable]), surplus
        for i in movable:
            more = min(most - holding[i], max(1, remaining * loads[i] // pool), surplus)
            holding[i] = holding[i] + more
            surplus = surplus - more
    return np.array(holding)


def scatter_about(own_key, extent, scale, reach, pieces=(), kind=jnp.bfloat16):
    values = jax.random.normal(own_key, extent, jnp.float32) * scale
    if len(pieces) > 0:
        values = shard_levels(own_key, extent, pieces, -0.22, 0.18) * values
    return jnp.clip(values, min=-reach, max=reach).astype(kind)


def setup_inputs(seed: int = 0) -> dict:
    key_of = jax.random.split(jax.random.key(seed), 13)
    tokens = scatter_about(key_of[0], (TOKENS, D), 1.0, 6.0, ((0, 32),))
    routes_keys = jax.random.split(jax.random.fold_in(key_of[1], 1), TOKENS // TOK_DEV)
    routes_turns = jax.random.permutation(jax.random.fold_in(key_of[1], 3), TOKENS // TOK_DEV)
    routes = jax.vmap(lambda own, number: shared_out(jax.random.fold_in(key_of[1], 2), own, number, TOK_DEV, EXPERTS, TOP, CAP, 1))(routes_keys, routes_turns).reshape((TOKENS, TOP))
    cotangent = scatter_about(key_of[2], (TOKENS, D), 1.0, 6.0, ((0, 32),))
    attend_gain = jnp.clip(1.0 + 0.1 * jax.random.normal(key_of[3], (D,), jnp.float32), 0.5, 1.5)
    attend_bias = scatter_about(key_of[4], (D,), 0.2, 1.25, ((0, 8),), jnp.float32)
    triple_weight = scatter_about(key_of[5], (D, 3 * D), D ** -0.5, 0.25, ((0, 8),), jnp.float32)
    merge_weight = scatter_about(key_of[6], (D, D), (D // 64) ** -0.5, 2.0, ((0, 8),), jnp.float32)
    mixture_gain = jnp.clip(1.0 + 0.1 * jax.random.normal(key_of[7], (D,), jnp.float32), 0.5, 1.5)
    mixture_bias = scatter_about(key_of[8], (D,), 0.2, 1.25, ((0, 8),), jnp.float32)
    router_weight = scatter_about(key_of[9], (D, EXPERTS), (4 * D) ** -0.5, 0.125, ((0, 8),), jnp.float32)
    expert_up = scatter_about(key_of[10], (EXPERTS, D, FF), D ** -0.5, 0.25, ((0, 4), (1, 8)), jnp.float32)
    expert_down = scatter_about(key_of[11], (EXPERTS, FF, D), (max(1, FF * TOP // (EXPERTS * EXPERTS))) ** -0.5, 0.75, ((0, 4), (1, 8)), jnp.float32)
    return {"tokens": tokens, "routes": routes, "cotangent": cotangent, "attend_gain": attend_gain, "attend_bias": attend_bias, "triple_weight": triple_weight, "merge_weight": merge_weight, "mixture_gain": mixture_gain, "mixture_bias": mixture_bias, "router_weight": router_weight, "expert_up": expert_up, "expert_down": expert_down}


@jax.custom_vjp
def low(v):
    return lax.optimization_barrier(v.astype(jnp.bfloat16)).astype(jnp.float32)

@jax.custom_vjp
def low_back(v):
    return v

def low_keep(v):
    return (low(v), None)

def low_pass(kept, grad):
    return (grad,)

def back_keep(v):
    return (v, None)

def back_low(kept, grad):
    return (low(grad),)
low.defvjp(low_keep, low_pass)
low_back.defvjp(back_keep, back_low)
EPSILON = 1e-06
HIGHEST = lax.Precision.HIGHEST

def layer_norm(values, gain, bias):
    center = values - lax.optimization_barrier(jnp.mean(values, -1, keepdims=True))
    spread = lax.optimization_barrier(jnp.mean(center * center, -1, keepdims=True))
    return center * lax.rsqrt(spread + EPSILON) * gain + bias

def reference(tokens, routes, cotangent, attend_gain, attend_bias, triple_weight, merge_weight, mixture_gain, mixture_bias, router_weight, expert_up, expert_down):
    blocks = TOKENS // TOK_DEV
    chosen = routes.reshape(blocks, TOK_DEV * TOP)
    expert_ids = jnp.arange(EXPERTS, dtype=jnp.int32)
    onehot = (chosen[:, :, None] == expert_ids).astype(jnp.int32)
    before = jnp.cumsum(onehot, 1) - onehot
    ranking = lax.optimization_barrier(jnp.sum(before * onehot, 2))
    block_ids = jnp.arange(blocks, dtype=jnp.int32)[:, None]
    slots = (chosen * (blocks * CAP) + block_ids * CAP + ranking).reshape(-1).astype(jnp.int32)
    pair_ids = jnp.arange(TOKENS * TOP, dtype=jnp.int32)
    filler = jnp.zeros((EXPERTS * blocks * CAP,), jnp.int32).at[slots].set(pair_ids + 1)
    token_source = jnp.where(filler > 0, (filler - 1) // TOP + 1, 0).astype(jnp.int32)
    picked = (routes[:, :, None] == expert_ids).astype(jnp.float32)
    group_images = IMG_DEV * 4
    scale = 1.0 / HEAD_DIM ** 0.5

    def forward(inputs, gain_one, bias_one, triple, merge_full, gain_two, bias_two, router, up_all, down_all):
        gain_one, bias_one, gain_two, bias_two = (low(gain_one), low(bias_one), low(gain_two), low(bias_two))
        triple, merge_full, router = (low(triple), low(merge_full), low(router))
        up_all, down_all = (low(up_all), low(down_all))
        normed = low(layer_norm(inputs, gain_one, bias_one))

        def attend(group):
            count = group.shape[0]
            joined = jnp.einsum('gsd,de->gse', group, triple, precision=HIGHEST)
            joined = low_back(low(joined)).reshape(count, SEQ, 3, HEADS, HEAD_DIM)
            query_rows = joined[:, :, 0]
            key_rows = joined[:, :, 1]
            value_rows = joined[:, :, 2]
            scores = low_back(jnp.einsum('gqhd,gkhd->ghqk', query_rows, key_rows, precision=HIGHEST) * scale)
            weights = jax.nn.softmax(scores, -1)
            mixed = jnp.einsum('ghqk,gkhd->gqhd', low(weights), value_rows, precision=HIGHEST)
            mixed = low_back(low(mixed)).reshape(count, SEQ, D)
            return low_back(jnp.einsum('gsd,de->gse', mixed, merge_full, precision=HIGHEST))
        grouped = normed.reshape(IMAGES // group_images, group_images, SEQ, D)
        branch = lax.map(jax.checkpoint(attend), grouped).reshape(TOKENS, D)
        hidden_one = inputs + branch
        normed_two = low(layer_norm(hidden_one, gain_two, bias_two))
        logits = low_back(jnp.dot(normed_two, router, precision=HIGHEST))
        probs = jax.nn.softmax(logits, -1)
        gates = lax.optimization_barrier(jnp.sum(picked * probs[:, None, :], 2))
        padded = jnp.concatenate([jnp.zeros((1, D), normed_two.dtype), normed_two], 0)
        rows = low_back(padded[token_source]).reshape(EXPERTS, blocks * CAP, D)

        def expert_apply(operands):
            rows_here, up_here, down_here = operands
            hidden = low_back(jnp.dot(rows_here, up_here, precision=HIGHEST))
            active = low(jax.nn.gelu(hidden, approximate=False))
            return low_back(low(jnp.dot(active, down_here, precision=HIGHEST)))
        outputs = lax.map(jax.checkpoint(expert_apply), (rows, up_all, down_all))
        pair_out = outputs.reshape(EXPERTS * blocks * CAP, D)[slots].reshape(TOKENS, TOP, D)
        return hidden_one + lax.optimization_barrier(jnp.sum(gates[:, :, None] * pair_out, 1))
    primals = (tokens.astype(jnp.float32), attend_gain, attend_bias, triple_weight, merge_weight, mixture_gain, mixture_bias, router_weight, expert_up, expert_down)
    result, pullback = jax.vjp(forward, *primals)
    grads = pullback(cotangent.astype(jnp.float32))
    return (result.astype(jnp.bfloat16), grads[0], grads[1], grads[2], grads[3], grads[4], grads[5], grads[6], grads[7], grads[8], grads[9])
```

```python
from functools import partial

import jax
import jax.numpy as jnp
from jax import lax
from jax.experimental import pallas as pl
from jax.experimental.pallas import tpu as pltpu
from jax.sharding import PartitionSpec as P

HEAD_DIM = 64
TOP = 2
SEQ = 197
EPSILON = 1e-06
LANES = 128
TILE = 256
STRIP = 64
SUB = 128
FAR = -1e30
BF = jnp.bfloat16
F32 = jnp.float32
VMEM_LIMIT = 60 * 1024 * 1024

ERFC = (
    0.2820843458175659,
    0.282412052154541,
    0.24283546209335327,
    0.2037508189678192,
    -0.029143672436475754,
    0.2817249596118927,
    -0.49039793014526367,
    0.2861193120479584,
    -0.05938538536429405,
)


def ceil_to(value, unit):
    return -(-value // unit) * unit


def dot_nn(a, b):
    return lax.dot_general(a, b, (((1,), (0,)), ((), ())), preferred_element_type=F32)


def dot_nt(a, b):
    return lax.dot_general(a, b, (((1,), (1,)), ((), ())), preferred_element_type=F32)


def dot_tn(a, b):
    return lax.dot_general(a, b, (((0,), (0,)), ((), ())), preferred_element_type=F32)


def gelu_both(hidden):
    bell = jnp.exp(hidden * hidden * -0.5)
    t = 1.0 / (1.0 + jnp.abs(hidden) * (0.5 * 0.5**0.5))
    series = jnp.full_like(t, ERFC[-1])
    for factor in ERFC[-2::-1]:
        series = series * t + factor
    tail = (0.5 * t) * series * bell
    share = jnp.where(hidden >= 0, 1.0 - tail, tail)
    return hidden * share, share + hidden * bell * 0.3989422804014327


def normalize(values):
    center = values - jnp.mean(values, -1, keepdims=True)
    spread = jnp.mean(center * center, -1, keepdims=True)
    inverse = lax.rsqrt(spread + EPSILON)
    return center * inverse, inverse


def window(image):
    start = image * SEQ // 16 * 16
    offset = image * SEQ - start
    return pl.multiple_of(start, 16), offset


WINDOW = ceil_to(SEQ + 15, 32)


def attend_kernel(
    experts, tokens, routes, packed, qkv, mixed, hidden, normed, probs, gates, first, small
):
    rows, width = tokens.shape
    images = rows // SEQ
    half = rows // 2
    small[...] = packed[:, 4 * width :].astype(F32).T
    gain_one, bias_one = small[experts : experts + 1, :], small[experts + 1 : experts + 2, :]
    gain_two, bias_two = small[experts + 2 : experts + 3, :], small[experts + 3 : experts + 4, :]

    def norm_one(j, carry):
        part = pl.ds(pl.multiple_of(j * STRIP, STRIP), STRIP)
        unit, _ = normalize(tokens[part, :].astype(F32))
        first[part, :] = (unit * gain_one + bias_one).astype(BF)
        mixed[part, :] = jnp.zeros((STRIP, width), BF)
        return carry

    lax.fori_loop(0, rows // STRIP, norm_one, 0)
    for third in range(3):
        columns = slice(third * width, (third + 1) * width)

        def project(j, carry):
            part = pl.ds(pl.multiple_of(j * half, 16), half)
            qkv[part, columns] = dot_nn(first[part, :], packed[:, columns]).astype(BF)
            return carry

        lax.fori_loop(0, 2, project, 0)

    lane = lax.broadcasted_iota(jnp.int32, (1, LANES), 1)
    low = lane < HEAD_DIM
    scale = 1.0 / HEAD_DIM**0.5

    def attend(image, carry):
        start, offset = window(image)
        part = pl.ds(start, WINDOW)
        place = lax.broadcasted_iota(jnp.int32, (WINDOW, 1), 0) - offset
        mine = (place >= 0) & (place < SEQ)
        across = lax.broadcasted_iota(jnp.int32, (1, WINDOW), 1) - offset
        keys_mine = (across >= 0) & (across < SEQ)
        for pair in range(width // LANES):
            at = pair * LANES
            query = qkv[part, at : at + LANES]
            key = qkv[part, width + at : width + at + LANES]
            value = qkv[part, 2 * width + at : 2 * width + at + LANES]
            both = []
            for side in (low, ~low):
                chosen = jnp.where(side, query, jnp.zeros_like(query))
                scores = jnp.where(keys_mine, dot_nt(chosen, key) * scale, FAR)
                top = jnp.max(scores, -1, keepdims=True)
                raised = jnp.exp(scores - top)
                weights = raised * (1.0 / jnp.sum(raised, -1, keepdims=True))
                both.append(dot_nn(weights.astype(BF), value))
            out = jnp.where(low, both[0], both[1]).astype(BF)
            mixed[part, at : at + LANES] = jnp.where(mine, out, mixed[part, at : at + LANES])
        return carry

    lax.fori_loop(0, images, attend, 0)

    def merge(j, carry):
        part = pl.ds(pl.multiple_of(j * half, 16), half)
        hidden[part, :] = dot_nn(mixed[part, :], packed[:, 3 * width : 4 * width])
        return carry

    lax.fori_loop(0, 2, merge, 0)

    def norm_two(j, carry):
        part = pl.ds(pl.multiple_of(j * STRIP, STRIP), STRIP)
        total = tokens[part, :].astype(F32) + hidden[part, :]
        hidden[part, :] = total
        unit, _ = normalize(total)
        normed[part, :] = (unit * gain_two + bias_two).astype(BF)
        return carry

    lax.fori_loop(0, rows // STRIP, norm_two, 0)
    router = small[0 : max(experts, 16), :].astype(BF)
    logits = dot_nt(router, normed[...])[:experts]
    raised = jnp.exp(logits - jnp.max(logits, 0, keepdims=True))
    share = raised / jnp.sum(raised, 0, keepdims=True)
    probs[...] = share
    ids = lax.broadcasted_iota(jnp.int32, (experts, rows), 0)
    picked = (routes[0:1, :] == ids) | (routes[1:2, :] == ids)
    gates[...] = jnp.where(picked, share, 0.0)


def attend(tokens, routes, packed, experts):
    rows, width = tokens.shape
    shape = jax.ShapeDtypeStruct
    return pl.pallas_call(
        partial(attend_kernel, experts),
        out_shape=(
            shape((rows, 3 * width), BF),
            shape((rows, width), BF),
            shape((rows, width), F32),
            shape((rows, width), BF),
            shape((experts, rows), F32),
            shape((experts, rows), F32),
        ),
        in_specs=[pl.BlockSpec(memory_space=pltpu.VMEM)] * 3,
        out_specs=[pl.BlockSpec(memory_space=pltpu.VMEM)] * 6,
        scratch_shapes=[pltpu.VMEM((rows, width), BF), pltpu.VMEM((LANES, width), F32)],
        compiler_params=pltpu.CompilerParams(vmem_limit_bytes=VMEM_LIMIT),
        name="attend",
    )(tokens, routes, packed)


def expert_kernel(
    tiles,
    parts,
    room,
    meta,
    info,
    up,
    down,
    rows,
    upstream,
    mixture,
    row_grad,
    gate_grad,
    up_grad,
    down_grad,
    packed_rows,
    packed_grads,
    out_sum,
    back_sum,
    out_low,
    back_low,
    up_sum,
    down_sum,
):
    width = rows.shape[1]
    step = pl.program_id(0)
    member = jnp.minimum(step // parts, 1)
    part = step - member * parts
    span = up_sum.shape[1]
    stride = meta.shape[0] // 2

    @pl.when(step == 0)
    def _():
        def clear(j, carry):
            at = pl.ds(pl.multiple_of(j * TILE, TILE), TILE)
            for which in range(2):
                out_low[which, at, :] = jnp.zeros((TILE, width), BF)
                back_low[which, at, :] = jnp.zeros((TILE, width), BF)
            return carry

        lax.fori_loop(0, room // TILE, clear, 0)

    @pl.when((step < 2 * parts) & (part == 0))
    def _():
        def clear(j, carry):
            at = pl.ds(pl.multiple_of(j * TILE, TILE), TILE)
            packed_rows[at, :] = jnp.zeros((TILE, width), BF)
            packed_grads[at, :] = jnp.zeros((TILE, width), BF)
            return carry

        lax.fori_loop(0, room // TILE, clear, 0)

        def gather(tile, carry):
            begin = meta[member * stride + tile]
            end = meta[member * stride + tile + 1]
            base = begin // 16 * 16
            count = jnp.where(end > begin, (end - base + SUB - 1) // SUB, 0)
            at = pl.ds(pl.multiple_of(tile * TILE, TILE), TILE)
            known = info[tile]
            order = jnp.where(member == 0, known[0:1, :], known[1:2, :])
            columns = known.T
            gate = jnp.where(member == 0, columns[:, 2:3], columns[:, 3:4])
            source = rows[at, :]
            gated = (upstream[at, :].astype(F32) * gate).astype(BF)

            def place(j, inner):
                origin = pl.multiple_of(base + j * SUB, 16)
                wanted = lax.broadcasted_iota(jnp.int32, (SUB, 1), 0) + origin
                chosen = jnp.where(order == wanted.astype(F32), 1.0, 0.0).astype(BF)
                to = pl.ds(origin, SUB)
                packed_rows[to, :] += dot_nn(chosen, source).astype(BF)
                packed_grads[to, :] += dot_nn(chosen, gated).astype(BF)
                return inner

            return lax.fori_loop(0, count, place, carry)

        lax.fori_loop(0, tiles, gather, 0)

    @pl.when(step < 2 * parts)
    def _():
        up_part = up[...].reshape(width, span)
        down_part = down[...].reshape(span, width)
        chunks = (meta[member * stride + tiles] + TILE - 1) // TILE
        up_sum[...] = jnp.zeros(up_sum.shape, F32)
        down_sum[...] = jnp.zeros(down_sum.shape, F32)

        def chunk(j, carry):
            at = pl.ds(pl.multiple_of(j * TILE, TILE), TILE)
            source = packed_rows[at, :]
            grads = packed_grads[at, :]
            active, slope = gelu_both(dot_nn(source, up_part))
            active = active.astype(BF)
            out = dot_nn(active, down_part)
            pre_grad = (dot_nt(grads, down_part) * slope).astype(BF)
            back = dot_nt(pre_grad, up_part)

            @pl.when(part == 0)
            def _():
                out_sum[at, :] = out
                back_sum[at, :] = back

            @pl.when((part > 0) & (part < parts - 1))
            def _():
                out_sum[at, :] += out
                back_sum[at, :] += back

            @pl.when(part == parts - 1)
            def _():
                out_low[member, at, :] = (out_sum[at, :] + out).astype(BF)
                back_low[member, at, :] = (back_sum[at, :] + back).astype(BF)

            down_sum[...] += dot_tn(active, grads)
            up_sum[...] += dot_tn(source, pre_grad)
            return carry

        lax.fori_loop(0, chunks, chunk, 0)
        up_grad[...] = up_sum[...].astype(BF).reshape(up_grad.shape)
        down_grad[...] = down_sum[...].astype(BF).reshape(down_grad.shape)

    @pl.when(step >= 2 * parts)
    def _():
        tile = step - 2 * parts
        at = pl.ds(pl.multiple_of(tile * TILE, TILE), TILE)
        columns = info[tile].T
        grads = upstream[at, :].astype(F32)
        mixture[...] = jnp.zeros(mixture.shape, mixture.dtype)
        lane = lax.broadcasted_iota(jnp.int32, (1, LANES), 1)
        zero = jnp.zeros((TILE, width), F32)
        mix, back, dots = zero, zero, jnp.zeros((TILE, LANES), F32)
        for which in range(2):
            begin = meta[which * stride + tile]
            end = meta[which * stride + tile + 1]
            base = begin // 16 * 16
            count = jnp.where(end > begin, (end - base + TILE - 1) // TILE, 0)
            order = columns[:, which : which + 1]

            def fetch(j, carry, which=which, base=base, order=order):
                out, back = carry
                origin = pl.multiple_of(base + j * TILE, 16)
                wanted = lax.broadcasted_iota(jnp.int32, (1, TILE), 1) + origin
                chosen = jnp.where(order == wanted.astype(F32), 1.0, 0.0).astype(BF)
                source = pl.ds(origin, TILE)
                out += dot_nn(chosen, out_low[which, source, :])
                back += dot_nn(chosen, back_low[which, source, :])
                return out, back

            out, back = lax.fori_loop(0, count, fetch, (zero, back))
            mix += out * columns[:, 2 + which : 3 + which]
            dots += jnp.where(lane == which, jnp.sum(out * grads, -1, keepdims=True), 0.0)
        mixture[...] = mix.astype(BF)
        row_grad[...] = back.astype(BF)
        gate_grad[...] = dots.T[:8]


def expert_block(meta, info, up, down, rows, upstream, most):
    shards, members, rows_up, hidden_units = up.shape
    rows_down = down.shape[2]
    count, width = rows.shape
    tiles = count // TILE
    parts = hidden_units // 512
    span = hidden_units // parts
    room = ceil_to(most, TILE) + TILE
    shape = jax.ShapeDtypeStruct
    last = 2 * parts - 1

    def member_of(i):
        return jnp.minimum(i, last) // parts

    def part_of(i):
        return jnp.minimum(i, last) % parts

    up_spec = pl.BlockSpec(
        (shards, 1, rows_up, span), lambda i, *_: (0, member_of(i), 0, part_of(i))
    )
    down_spec = pl.BlockSpec(
        (span // rows_down, 1, rows_down, width), lambda i, *_: (part_of(i), member_of(i), 0, 0)
    )
    tile_spec = pl.BlockSpec((TILE, width), lambda i, *_: (jnp.maximum(i - last - 1, 0), 0))
    whole = pl.BlockSpec(memory_space=pltpu.VMEM)
    return pl.pallas_call(
        partial(expert_kernel, tiles, parts, room),
        grid_spec=pltpu.PrefetchScalarGridSpec(
            num_scalar_prefetch=1,
            grid=(2 * parts + tiles,),
            in_specs=[whole, up_spec, down_spec, whole, whole],
            out_specs=[
                tile_spec,
                tile_spec,
                pl.BlockSpec((8, TILE), lambda i, *_: (0, jnp.maximum(i - last - 1, 0))),
                up_spec,
                down_spec,
            ],
            scratch_shapes=[
                pltpu.VMEM((room, width), BF),
                pltpu.VMEM((room, width), BF),
                pltpu.VMEM((room, width), F32),
                pltpu.VMEM((room, width), F32),
                pltpu.VMEM((2, room, width), BF),
                pltpu.VMEM((2, room, width), BF),
                pltpu.VMEM((width, span), F32),
                pltpu.VMEM((span, width), F32),
            ],
        ),
        out_shape=(
            shape((count, width), BF),
            shape((count, width), BF),
            shape((8, count), F32),
            shape(up.shape, BF),
            shape(down.shape, BF),
        ),
        compiler_params=pltpu.CompilerParams(
            vmem_limit_bytes=VMEM_LIMIT, dimension_semantics=("arbitrary",)
        ),
        name="experts",
    )(meta, info, up, down, rows, upstream)


def retreat_kernel(
    experts,
    tokens,
    cotangent,
    hidden,
    normed,
    qkv,
    mixed,
    probs,
    gate_grad,
    returned,
    packed,
    token_grad,
    grads,
    first,
    hidden_grad,
    branch_grad,
    joined_grad,
    small,
    sums,
    totals,
):
    rows, width = tokens.shape
    real = token_grad.shape[0]
    images = rows // SEQ
    half = rows // 2
    small[...] = packed[:, 4 * width :].astype(F32).T
    gain_one, bias_one = small[experts : experts + 1, :], small[experts + 1 : experts + 2, :]
    gain_two = small[experts + 2 : experts + 3, :]
    sums[...] = jnp.zeros(sums.shape, F32)
    totals[...] = jnp.zeros(totals.shape, F32)

    share = probs[...]
    change = gate_grad[...]
    tilt = share * (change - jnp.sum(share * change, 0, keepdims=True))
    if experts < 16:
        tilt = jnp.concatenate([tilt, jnp.zeros((16 - experts, rows), F32)], 0)
    tilt = tilt.astype(BF)
    router = small[0 : tilt.shape[0], :].astype(BF)
    keep = lax.broadcasted_iota(jnp.int32, (tilt.shape[0], 1), 0) < experts
    router = jnp.where(keep, router, jnp.zeros_like(router))
    sums[0 : tilt.shape[0], :] = dot_nn(tilt, normed[...])
    hidden_grad[...] = dot_tn(tilt, router)

    def norm_two(j, carry):
        part = pl.ds(pl.multiple_of(j * STRIP, STRIP), STRIP)
        change = hidden_grad[part, :]
        for owner in range(returned.shape[0]):
            change += returned[owner, part, :].astype(F32)
        unit, inverse = normalize(hidden[part, :])
        tail = change * unit
        totals[0] += jnp.sum(tail.reshape(STRIP // 8, 8, width), 0)
        totals[1] += jnp.sum(change.reshape(STRIP // 8, 8, width), 0)
        change = change * gain_two
        mean = jnp.mean(change, -1, keepdims=True)
        lean = jnp.mean(change * unit, -1, keepdims=True)
        total = cotangent[part, :].astype(F32) + inverse * (change - mean - unit * lean)
        hidden_grad[part, :] = total
        branch_grad[part, :] = total.astype(BF)
        unit, _ = normalize(tokens[part, :].astype(F32))
        first[part, :] = (unit * gain_one + bias_one).astype(BF)
        joined_grad[part, :] = jnp.zeros((STRIP, 3 * width), BF)
        return carry

    lax.fori_loop(0, rows // STRIP, norm_two, 0)
    merge = slice(3 * width, 4 * width)
    grads[:, merge] = dot_tn(mixed[...], branch_grad[...]).astype(BF)

    def project(j, carry):
        part = pl.ds(pl.multiple_of(j * half, 16), half)
        branch_grad[part, :] = dot_nt(branch_grad[part, :], packed[:, merge]).astype(BF)
        return carry

    lax.fori_loop(0, 2, project, 0)

    lane = lax.broadcasted_iota(jnp.int32, (1, LANES), 1)
    low = lane < HEAD_DIM
    scale = 1.0 / HEAD_DIM**0.5

    def attend(image, carry):
        start, offset = window(image)
        part = pl.ds(start, WINDOW)
        place = lax.broadcasted_iota(jnp.int32, (WINDOW, 1), 0) - offset
        mine = (place >= 0) & (place < SEQ)
        for pair in range(width // LANES):
            at = pair * LANES
            query = qkv[part, at : at + LANES]
            key = qkv[part, width + at : width + at + LANES]
            value = qkv[part, 2 * width + at : 2 * width + at + LANES]
            change = branch_grad[part, at : at + LANES]
            change = jnp.where(mine, change, jnp.zeros_like(change))
            sides = []
            for side in (low, ~low):
                chosen = jnp.where(side, query, jnp.zeros_like(query))
                scores = jnp.where(mine, dot_nt(key, chosen) * scale, FAR)
                raised = jnp.exp(scores - jnp.max(scores, 0, keepdims=True))
                weights = raised * (1.0 / jnp.sum(raised, 0, keepdims=True))
                slope = dot_nt(value, jnp.where(side, change, jnp.zeros_like(change)))
                lean = jnp.sum(weights * slope, 0, keepdims=True)
                slope = (weights * (slope - lean)).astype(BF)
                sides.append(
                    (
                        dot_tn(slope, key) * scale,
                        dot_nn(slope, query) * scale,
                        dot_nn(weights.astype(BF), change),
                    )
                )
            for third in range(3):
                to = third * width + at
                joined_grad[part, to : to + LANES] += jnp.where(
                    low, sides[0][third], sides[1][third]
                ).astype(BF)
        return carry

    lax.fori_loop(0, images, attend, 0)
    for third in range(3):
        columns = slice(third * width, (third + 1) * width)
        grads[:, columns] = dot_tn(first[...], joined_grad[:, columns]).astype(BF)

    def finish(start, size):
        part = pl.ds(start, size)
        change = dot_nt(joined_grad[part, :], packed[:, : 3 * width])
        unit, inverse = normalize(tokens[part, :].astype(F32))
        tail = change * unit
        totals[2] += jnp.sum(tail.reshape(size // 8, 8, width), 0)
        totals[3] += jnp.sum(change.reshape(size // 8, 8, width), 0)
        change = change * gain_one
        mean = jnp.mean(change, -1, keepdims=True)
        lean = jnp.mean(change * unit, -1, keepdims=True)
        return hidden_grad[part, :] + inverse * (change - mean - unit * lean)

    block = 2 * STRIP

    def finish_loop(j, carry):
        start = pl.multiple_of(j * block, block)
        token_grad[pl.ds(start, block), :] = finish(start, block)
        return carry

    lax.fori_loop(0, real // block, finish_loop, 0)
    done = real // block * block
    if done < real:
        token_grad[done:real, :] = finish(done, ceil_to(real - done, 16))[: real - done]
    for which, row in ((2, experts), (3, experts + 1), (0, experts + 2), (1, experts + 3)):
        sums[row : row + 1, :] = jnp.sum(totals[which], 0, keepdims=True)
    grads[:, 4 * width :] = sums[...].T.astype(BF)


def retreat(
    tokens, cotangent, hidden, normed, qkv, mixed, probs, gate_grad, returned, packed, real
):
    rows, width = tokens.shape
    experts = probs.shape[0]
    shape = jax.ShapeDtypeStruct
    return pl.pallas_call(
        partial(retreat_kernel, experts),
        out_shape=(shape((real, width), F32), shape(packed.shape, BF)),
        in_specs=[pl.BlockSpec(memory_space=pltpu.VMEM)] * 10,
        out_specs=[pl.BlockSpec(memory_space=pltpu.VMEM)] * 2,
        scratch_shapes=[
            pltpu.VMEM((rows, width), BF),
            pltpu.VMEM((rows, width), F32),
            pltpu.VMEM((rows, width), BF),
            pltpu.VMEM((rows, 3 * width), BF),
            pltpu.VMEM((LANES, width), F32),
            pltpu.VMEM((LANES, width), F32),
            pltpu.VMEM((4, 8, width), F32),
        ],
        compiler_params=pltpu.CompilerParams(vmem_limit_bytes=VMEM_LIMIT),
        name="retreat",
    )(tokens, cotangent, hidden, normed, qkv, mixed, probs, gate_grad, returned, packed)


def plan_rows(routes, first_expert):
    owners, _, padded = routes.shape
    tiles = owners * padded // TILE
    mine = first_expert + jnp.arange(2, dtype=jnp.int32)[:, None, None]
    chosen = (routes[None, :, 0] == mine) | (routes[None, :, 1] == mine)
    chosen = chosen.reshape(2, tiles, TILE)
    flags = chosen.astype(BF)
    upper = jnp.triu(jnp.ones((TILE, TILE), BF))
    within = jnp.dot(flags.reshape(2 * tiles, TILE), upper, preferred_element_type=F32)
    within = within.reshape(2, tiles, TILE)
    counts = within[:, :, -1]
    below = jnp.tril(jnp.ones((tiles + 1, tiles), F32), -1)
    begins = jnp.sum(below[None] * counts[:, None, :], 2)
    order = jnp.where(chosen, begins[:, :tiles, None] + within - 1.0, -1.0)
    return order, begins.astype(jnp.int32).reshape(-1)


def local(
    tokens,
    routes,
    cotangent,
    attend_gain,
    attend_bias,
    triple_weight,
    merge_weight,
    mixture_gain,
    mixture_bias,
    router_weight,
    expert_up,
    expert_down,
):
    real, width = tokens.shape
    experts = router_weight.shape[1]
    owners = lax.axis_size("expert")
    capacity = 2 * TOP * real // experts
    padded = ceil_to(real, STRIP)
    spare = LANES - experts - 4
    here = lax.axis_index("expert")

    small = jnp.concatenate(
        [
            router_weight,
            attend_gain[:, None],
            attend_bias[:, None],
            mixture_gain[:, None],
            mixture_bias[:, None],
            jnp.zeros((router_weight.shape[0], spare), F32),
        ],
        1,
    )
    packed = jnp.concatenate([triple_weight, merge_weight, small], 1).astype(BF)
    packed = lax.all_gather(packed, "fsdp", axis=0, tiled=True)
    up_full = lax.all_gather(expert_up.astype(BF), "fsdp", axis=0)
    down_full = lax.all_gather(expert_down.astype(BF), "fsdp", axis=0)

    token_rows = jnp.pad(tokens, ((0, padded - real), (0, 0)))
    upstream = jnp.pad(cotangent, ((0, padded - real), (0, 0)))
    route_rows = jnp.pad(routes.T, ((0, 0), (0, padded - real)), constant_values=-1)
    all_routes = lax.all_gather(route_rows, "expert", axis=0)
    order, meta = plan_rows(all_routes, here * 2)
    tiles = owners * padded // TILE
    all_upstream = lax.all_gather(upstream, "expert", axis=0, tiled=True)

    qkv, mixed, hidden, normed, probs, gates = attend(token_rows, route_rows, packed, experts)
    all_rows = lax.all_gather(normed, "expert", axis=0, tiled=True)
    all_gates = lax.all_gather(gates, "expert", axis=0)
    own_gates = lax.dynamic_slice_in_dim(all_gates, here * 2, 2, 1)
    own_gates = own_gates.transpose(1, 0, 2).reshape(2, tiles, TILE)
    info = jnp.concatenate([order, own_gates, jnp.zeros((4, tiles, TILE), F32)], 0)
    info = info.transpose(1, 0, 2)

    mixture, row_grad, gate_grad, up_grad, down_grad = expert_block(
        meta, info, up_full, down_full, all_rows, all_upstream, owners * capacity
    )
    gate_grad = gate_grad[:2].reshape(2, owners, padded).transpose(1, 0, 2)
    gate_grad = lax.all_to_all(gate_grad, "expert", 0, 0).reshape(experts, padded)
    row_grad = lax.psum_scatter(
        row_grad.reshape(owners, padded, width), "expert", scatter_dimension=0, tiled=True
    )
    mixture = lax.psum_scatter(
        mixture.reshape(owners, padded, width), "expert", scatter_dimension=0, tiled=True
    )
    block_out = (hidden[:real] + mixture[0, :real].astype(F32)).astype(BF)
    up_grad = lax.psum_scatter(up_grad, "fsdp", scatter_dimension=0, tiled=True)
    down_grad = lax.psum_scatter(down_grad, "fsdp", scatter_dimension=0, tiled=True)

    token_grad, grads = retreat(
        token_rows,
        upstream,
        hidden,
        normed,
        qkv,
        mixed,
        probs,
        gate_grad,
        row_grad,
        packed,
        real,
    )
    grads = lax.psum_scatter(grads, "fsdp", scatter_dimension=0, tiled=True)
    grads = lax.psum(grads, "expert").astype(F32)
    rest = grads[:, 4 * width :]
    return (
        block_out,
        token_grad,
        rest[:, experts],
        rest[:, experts + 1],
        grads[:, : 3 * width],
        grads[:, 3 * width : 4 * width],
        rest[:, experts + 2],
        rest[:, experts + 3],
        rest[:, :experts],
        up_grad[0].astype(F32),
        down_grad[0].astype(F32),
    )


def solution(mesh):
    return jax.shard_map(
        local,
        mesh=mesh,
        in_specs=(
            P(("expert", "fsdp"), None),
            P(("expert", "fsdp"), None),
            P(("expert", "fsdp"), None),
            P("fsdp"),
            P("fsdp"),
            P("fsdp", None),
            P("fsdp", None),
            P("fsdp"),
            P("fsdp"),
            P("fsdp", None),
            P("expert", "fsdp", None),
            P("expert", "fsdp", None),
        ),
        out_specs=(
            P(("expert", "fsdp"), None),
            P(("expert", "fsdp"), None),
            P("fsdp"),
            P("fsdp"),
            P("fsdp", None),
            P("fsdp", None),
            P("fsdp"),
            P("fsdp"),
            P("fsdp", None),
            P("expert", "fsdp", None),
            P("expert", "fsdp", None),
        ),
        check_vma=False,
    )
```

```python
from functools import partial

import jax
import jax.numpy as jnp
from jax import lax
from jax.experimental import pallas as pl
from jax.experimental.pallas import tpu as pltpu
from jax.sharding import PartitionSpec as P

HEAD_DIM = 64
TOP = 2
SEQ = 197
EPSILON = 1e-06
LANES = 128
TILE = 256
STRIP = 64
SUB = 128
FAR = -1e30
BF = jnp.bfloat16
F32 = jnp.float32
VMEM_LIMIT = 60 * 1024 * 1024

ERFC = (
    0.2820843458175659,
    0.282412052154541,
    0.24283546209335327,
    0.2037508189678192,
    -0.029143672436475754,
    0.2817249596118927,
    -0.49039793014526367,
    0.2861193120479584,
    -0.05938538536429405,
)


def ceil_to(value, unit):
    return -(-value // unit) * unit


def dot_nn(a, b):
    return lax.dot_general(a, b, (((1,), (0,)), ((), ())), preferred_element_type=F32)


def dot_nt(a, b):
    return lax.dot_general(a, b, (((1,), (1,)), ((), ())), preferred_element_type=F32)


def dot_tn(a, b):
    return lax.dot_general(a, b, (((0,), (0,)), ((), ())), preferred_element_type=F32)


def gelu_both(hidden):
    bell = jnp.exp(hidden * hidden * -0.5)
    t = 1.0 / (1.0 + jnp.abs(hidden) * (0.5 * 0.5**0.5))
    series = jnp.full_like(t, ERFC[-1])
    for factor in ERFC[-2::-1]:
        series = series * t + factor
    tail = (0.5 * t) * series * bell
    share = jnp.where(hidden >= 0, 1.0 - tail, tail)
    return hidden * share, share + hidden * bell * 0.3989422804014327


def normalize(values):
    center = values - jnp.mean(values, -1, keepdims=True)
    spread = jnp.mean(center * center, -1, keepdims=True)
    inverse = lax.rsqrt(spread + EPSILON)
    return center * inverse, inverse


def window(image):
    start = image * SEQ // 16 * 16
    offset = image * SEQ - start
    return pl.multiple_of(start, 16), offset


WINDOW = ceil_to(SEQ + 15, 32)


def attend_kernel(
    experts, tokens, routes, packed, qkv, mixed, hidden, normed, probs, gates, first, small
):
    rows, width = tokens.shape
    images = rows // SEQ
    half = rows // 2
    small[...] = packed[:, 4 * width :].astype(F32).T
    gain_one, bias_one = small[experts : experts + 1, :], small[experts + 1 : experts + 2, :]
    gain_two, bias_two = small[experts + 2 : experts + 3, :], small[experts + 3 : experts + 4, :]

    def norm_one(j, carry):
        part = pl.ds(pl.multiple_of(j * STRIP, STRIP), STRIP)
        unit, _ = normalize(tokens[part, :].astype(F32))
        first[part, :] = (unit * gain_one + bias_one).astype(BF)
        mixed[part, :] = jnp.zeros((STRIP, width), BF)
        return carry

    lax.fori_loop(0, rows // STRIP, norm_one, 0)
    for third in range(3):
        columns = slice(third * width, (third + 1) * width)

        def project(j, carry):
            part = pl.ds(pl.multiple_of(j * half, 16), half)
            qkv[part, columns] = dot_nn(first[part, :], packed[:, columns]).astype(BF)
            return carry

        lax.fori_loop(0, 2, project, 0)

    lane = lax.broadcasted_iota(jnp.int32, (1, LANES), 1)
    low = lane < HEAD_DIM
    scale = 1.0 / HEAD_DIM**0.5

    def attend(image, carry):
        start, offset = window(image)
        part = pl.ds(start, WINDOW)
        place = lax.broadcasted_iota(jnp.int32, (WINDOW, 1), 0) - offset
        mine = (place >= 0) & (place < SEQ)
        across = lax.broadcasted_iota(jnp.int32, (1, WINDOW), 1) - offset
        keys_mine = (across >= 0) & (across < SEQ)
        for pair in range(width // LANES):
            at = pair * LANES
            query = qkv[part, at : at + LANES]
            key = qkv[part, width + at : width + at + LANES]
            value = qkv[part, 2 * width + at : 2 * width + at + LANES]
            both = []
            for side in (low, ~low):
                chosen = jnp.where(side, query, jnp.zeros_like(query))
                scores = jnp.where(keys_mine, dot_nt(chosen, key) * scale, FAR)
                top = jnp.max(scores, -1, keepdims=True)
                raised = jnp.exp(scores - top)
                weights = raised * (1.0 / jnp.sum(raised, -1, keepdims=True))
                both.append(dot_nn(weights.astype(BF), value))
            out = jnp.where(low, both[0], both[1]).astype(BF)
            mixed[part, at : at + LANES] = jnp.where(mine, out, mixed[part, at : at + LANES])
        return carry

    lax.fori_loop(0, images, attend, 0)

    def merge(j, carry):
        part = pl.ds(pl.multiple_of(j * half, 16), half)
        hidden[part, :] = dot_nn(mixed[part, :], packed[:, 3 * width : 4 * width])
        return carry

    lax.fori_loop(0, 2, merge, 0)

    def norm_two(j, carry):
        part = pl.ds(pl.multiple_of(j * STRIP, STRIP), STRIP)
        total = tokens[part, :].astype(F32) + hidden[part, :]
        hidden[part, :] = total
        unit, _ = normalize(total)
        normed[part, :] = (unit * gain_two + bias_two).astype(BF)
        return carry

    lax.fori_loop(0, rows // STRIP, norm_two, 0)
    router = small[0 : max(experts, 16), :].astype(BF)
    logits = dot_nt(router, normed[...])[:experts]
    raised = jnp.exp(logits - jnp.max(logits, 0, keepdims=True))
    share = raised / jnp.sum(raised, 0, keepdims=True)
    probs[...] = share
    ids = lax.broadcasted_iota(jnp.int32, (experts, rows), 0)
    picked = (routes[0:1, :] == ids) | (routes[1:2, :] == ids)
    gates[...] = jnp.where(picked, share, 0.0)


def attend(tokens, routes, packed, experts):
    rows, width = tokens.shape
    shape = jax.ShapeDtypeStruct
    return pl.pallas_call(
        partial(attend_kernel, experts),
        out_shape=(
            shape((rows, 3 * width), BF),
            shape((rows, width), BF),
            shape((rows, width), F32),
            shape((rows, width), BF),
            shape((experts, rows), F32),
            shape((experts, rows), F32),
        ),
        in_specs=[pl.BlockSpec(memory_space=pltpu.VMEM)] * 3,
        out_specs=[pl.BlockSpec(memory_space=pltpu.VMEM)] * 6,
        scratch_shapes=[pltpu.VMEM((rows, width), BF), pltpu.VMEM((LANES, width), F32)],
        compiler_params=pltpu.CompilerParams(vmem_limit_bytes=VMEM_LIMIT),
        name="attend",
    )(tokens, routes, packed)


def expert_kernel(
    tiles,
    parts,
    room,
    meta,
    info,
    up,
    down,
    rows,
    upstream,
    mixture,
    row_grad,
    gate_grad,
    up_grad,
    down_grad,
    packed_rows,
    packed_grads,
    out_sum,
    back_sum,
    out_low,
    back_low,
    up_sum,
    down_sum,
):
    width = rows.shape[1]
    step = pl.program_id(0)
    owned = out_low.shape[0]
    member = jnp.minimum(step // parts, owned - 1)
    part = step - member * parts
    span = up_sum.shape[1]
    stride = meta.shape[0] // owned

    @pl.when(step == 0)
    def _():
        def clear(j, carry):
            at = pl.ds(pl.multiple_of(j * TILE, TILE), TILE)
            for which in range(owned):
                out_low[which, at, :] = jnp.zeros((TILE, width), BF)
                back_low[which, at, :] = jnp.zeros((TILE, width), BF)
            return carry

        lax.fori_loop(0, room // TILE, clear, 0)

    @pl.when((step < owned * parts) & (part == 0))
    def _():
        def clear(j, carry):
            at = pl.ds(pl.multiple_of(j * TILE, TILE), TILE)
            packed_rows[at, :] = jnp.zeros((TILE, width), BF)
            packed_grads[at, :] = jnp.zeros((TILE, width), BF)
            return carry

        lax.fori_loop(0, room // TILE, clear, 0)

        def gather(tile, carry):
            begin = meta[member * stride + tile]
            end = meta[member * stride + tile + 1]
            base = begin // 16 * 16
            count = jnp.where(end > begin, (end - base + SUB - 1) // SUB, 0)
            at = pl.ds(pl.multiple_of(tile * TILE, TILE), TILE)
            order = info[tile, pl.ds(member, 1), :]
            columns = info[tile].T
            which = lax.broadcasted_iota(jnp.int32, (1, columns.shape[1]), 1)
            gate = jnp.where(which == owned + member, columns, 0.0)
            gate = jnp.sum(gate, -1, keepdims=True)
            source = rows[at, :]
            gated = (upstream[at, :].astype(F32) * gate).astype(BF)

            def place(j, inner):
                origin = pl.multiple_of(base + j * SUB, 16)
                wanted = lax.broadcasted_iota(jnp.int32, (SUB, 1), 0) + origin
                chosen = jnp.where(order == wanted.astype(F32), 1.0, 0.0).astype(BF)
                to = pl.ds(origin, SUB)
                packed_rows[to, :] += dot_nn(chosen, source).astype(BF)
                packed_grads[to, :] += dot_nn(chosen, gated).astype(BF)
                return inner

            return lax.fori_loop(0, count, place, carry)

        lax.fori_loop(0, tiles, gather, 0)

    @pl.when(step < owned * parts)
    def _():
        up_part = up[...].reshape(width, span)
        down_part = down[...].reshape(span, width)
        chunks = (meta[member * stride + tiles] + TILE - 1) // TILE
        up_sum[...] = jnp.zeros(up_sum.shape, F32)
        down_sum[...] = jnp.zeros(down_sum.shape, F32)

        def chunk(j, carry):
            at = pl.ds(pl.multiple_of(j * TILE, TILE), TILE)
            source = packed_rows[at, :]
            grads = packed_grads[at, :]
            active, slope = gelu_both(dot_nn(source, up_part))
            active = active.astype(BF)
            out = dot_nn(active, down_part)
            pre_grad = (dot_nt(grads, down_part) * slope).astype(BF)
            back = dot_nt(pre_grad, up_part)

            @pl.when(part == 0)
            def _():
                out_sum[at, :] = out
                back_sum[at, :] = back

            @pl.when((part > 0) & (part < parts - 1))
            def _():
                out_sum[at, :] += out
                back_sum[at, :] += back

            @pl.when(part == parts - 1)
            def _():
                out_low[member, at, :] = (out_sum[at, :] + out).astype(BF)
                back_low[member, at, :] = (back_sum[at, :] + back).astype(BF)

            down_sum[...] += dot_tn(active, grads)
            up_sum[...] += dot_tn(source, pre_grad)
            return carry

        lax.fori_loop(0, chunks, chunk, 0)
        up_grad[...] = up_sum[...].astype(BF).reshape(up_grad.shape)
        down_grad[...] = down_sum[...].astype(BF).reshape(down_grad.shape)

    @pl.when(step >= owned * parts)
    def _():
        tile = step - owned * parts
        at = pl.ds(pl.multiple_of(tile * TILE, TILE), TILE)
        columns = info[tile].T
        grads = upstream[at, :].astype(F32)
        mixture[...] = jnp.zeros(mixture.shape, mixture.dtype)
        lane = lax.broadcasted_iota(jnp.int32, (1, LANES), 1)
        zero = jnp.zeros((TILE, width), F32)
        mix, back, dots = zero, zero, jnp.zeros((TILE, LANES), F32)
        for which in range(owned):
            begin = meta[which * stride + tile]
            end = meta[which * stride + tile + 1]
            base = begin // 16 * 16
            count = jnp.where(end > begin, (end - base + TILE - 1) // TILE, 0)
            order = columns[:, which : which + 1]

            def fetch(j, carry, which=which, base=base, order=order):
                out, back = carry
                origin = pl.multiple_of(base + j * TILE, 16)
                wanted = lax.broadcasted_iota(jnp.int32, (1, TILE), 1) + origin
                chosen = jnp.where(order == wanted.astype(F32), 1.0, 0.0).astype(BF)
                source = pl.ds(origin, TILE)
                out += dot_nn(chosen, out_low[which, source, :])
                back += dot_nn(chosen, back_low[which, source, :])
                return out, back

            out, back = lax.fori_loop(0, count, fetch, (zero, back))
            mix += out * columns[:, owned + which : owned + which + 1]
            dots += jnp.where(lane == which, jnp.sum(out * grads, -1, keepdims=True), 0.0)
        mixture[...] = mix.astype(BF)
        row_grad[...] = back.astype(BF)
        gate_grad[...] = dots.T[:8]


def expert_block(meta, info, up, down, rows, upstream, most):
    groups, shards, members, rows_up, hidden_units = up.shape
    rows_down = down.shape[3]
    owned = groups * members
    count, width = rows.shape
    tiles = count // TILE
    parts = hidden_units // 512
    span = hidden_units // parts
    room = ceil_to(most, TILE) + TILE
    shape = jax.ShapeDtypeStruct
    last = owned * parts - 1

    def member_of(i):
        return jnp.minimum(i, last) // parts

    def part_of(i):
        return jnp.minimum(i, last) % parts

    up_spec = pl.BlockSpec(
        (1, shards, 1, rows_up, span),
        lambda i, *_: (member_of(i) // members, 0, member_of(i) % members, 0, part_of(i)),
    )
    down_spec = pl.BlockSpec(
        (1, span // rows_down, 1, rows_down, width),
        lambda i, *_: (member_of(i) // members, part_of(i), member_of(i) % members, 0, 0),
    )
    tile_spec = pl.BlockSpec((TILE, width), lambda i, *_: (jnp.maximum(i - last - 1, 0), 0))
    whole = pl.BlockSpec(memory_space=pltpu.VMEM)
    return pl.pallas_call(
        partial(expert_kernel, tiles, parts, room),
        grid_spec=pltpu.PrefetchScalarGridSpec(
            num_scalar_prefetch=1,
            grid=(owned * parts + tiles,),
            in_specs=[whole, up_spec, down_spec, whole, whole],
            out_specs=[
                tile_spec,
                tile_spec,
                pl.BlockSpec((8, TILE), lambda i, *_: (0, jnp.maximum(i - last - 1, 0))),
                up_spec,
                down_spec,
            ],
            scratch_shapes=[
                pltpu.VMEM((room, width), BF),
                pltpu.VMEM((room, width), BF),
                pltpu.VMEM((room, width), F32),
                pltpu.VMEM((room, width), F32),
                pltpu.VMEM((owned, room, width), BF),
                pltpu.VMEM((owned, room, width), BF),
                pltpu.VMEM((width, span), F32),
                pltpu.VMEM((span, width), F32),
            ],
        ),
        out_shape=(
            shape((count, width), BF),
            shape((count, width), BF),
            shape((8, count), F32),
            shape(up.shape, BF),
            shape(down.shape, BF),
        ),
        compiler_params=pltpu.CompilerParams(
            vmem_limit_bytes=VMEM_LIMIT, dimension_semantics=("arbitrary",)
        ),
        name="experts",
    )(meta, info, up, down, rows, upstream)


def retreat_kernel(
    experts,
    tokens,
    cotangent,
    hidden,
    normed,
    qkv,
    mixed,
    probs,
    gate_grad,
    packed,
    *rest,
):
    returned, rest = rest[:-9], rest[-9:]
    token_grad, grads, first, hidden_grad, branch_grad, joined_grad, small, sums, totals = rest
    rows, width = tokens.shape
    real = token_grad.shape[0]
    images = rows // SEQ
    half = rows // 2
    small[...] = packed[:, 4 * width :].astype(F32).T
    gain_one, bias_one = small[experts : experts + 1, :], small[experts + 1 : experts + 2, :]
    gain_two = small[experts + 2 : experts + 3, :]
    sums[...] = jnp.zeros(sums.shape, F32)
    totals[...] = jnp.zeros(totals.shape, F32)

    share = probs[...]
    change = gate_grad[...]
    tilt = share * (change - jnp.sum(share * change, 0, keepdims=True))
    if experts < 16:
        tilt = jnp.concatenate([tilt, jnp.zeros((16 - experts, rows), F32)], 0)
    tilt = tilt.astype(BF)
    router = small[0 : tilt.shape[0], :].astype(BF)
    keep = lax.broadcasted_iota(jnp.int32, (tilt.shape[0], 1), 0) < experts
    router = jnp.where(keep, router, jnp.zeros_like(router))
    sums[0 : tilt.shape[0], :] = dot_nn(tilt, normed[...])
    hidden_grad[...] = dot_tn(tilt, router)

    def norm_two(j, carry):
        part = pl.ds(pl.multiple_of(j * STRIP, STRIP), STRIP)
        change = hidden_grad[part, :]
        for arrived in returned:
            change += arrived[part, :].astype(F32)
        unit, inverse = normalize(hidden[part, :])
        tail = change * unit
        totals[0] += jnp.sum(tail.reshape(STRIP // 8, 8, width), 0)
        totals[1] += jnp.sum(change.reshape(STRIP // 8, 8, width), 0)
        change = change * gain_two
        mean = jnp.mean(change, -1, keepdims=True)
        lean = jnp.mean(change * unit, -1, keepdims=True)
        total = cotangent[part, :].astype(F32) + inverse * (change - mean - unit * lean)
        hidden_grad[part, :] = total
        branch_grad[part, :] = total.astype(BF)
        unit, _ = normalize(tokens[part, :].astype(F32))
        first[part, :] = (unit * gain_one + bias_one).astype(BF)
        joined_grad[part, :] = jnp.zeros((STRIP, 3 * width), BF)
        return carry

    lax.fori_loop(0, rows // STRIP, norm_two, 0)
    merge = slice(3 * width, 4 * width)
    grads[:, merge] = dot_tn(mixed[...], branch_grad[...]).astype(BF)

    def project(j, carry):
        part = pl.ds(pl.multiple_of(j * half, 16), half)
        branch_grad[part, :] = dot_nt(branch_grad[part, :], packed[:, merge]).astype(BF)
        return carry

    lax.fori_loop(0, 2, project, 0)

    lane = lax.broadcasted_iota(jnp.int32, (1, LANES), 1)
    low = lane < HEAD_DIM
    scale = 1.0 / HEAD_DIM**0.5

    def attend(image, carry):
        start, offset = window(image)
        part = pl.ds(start, WINDOW)
        place = lax.broadcasted_iota(jnp.int32, (WINDOW, 1), 0) - offset
        mine = (place >= 0) & (place < SEQ)
        for pair in range(width // LANES):
            at = pair * LANES
            query = qkv[part, at : at + LANES]
            key = qkv[part, width + at : width + at + LANES]
            value = qkv[part, 2 * width + at : 2 * width + at + LANES]
            change = branch_grad[part, at : at + LANES]
            change = jnp.where(mine, change, jnp.zeros_like(change))
            sides = []
            for side in (low, ~low):
                chosen = jnp.where(side, query, jnp.zeros_like(query))
                scores = jnp.where(mine, dot_nt(key, chosen) * scale, FAR)
                raised = jnp.exp(scores - jnp.max(scores, 0, keepdims=True))
                weights = raised * (1.0 / jnp.sum(raised, 0, keepdims=True))
                slope = dot_nt(value, jnp.where(side, change, jnp.zeros_like(change)))
                lean = jnp.sum(weights * slope, 0, keepdims=True)
                slope = (weights * (slope - lean)).astype(BF)
                sides.append(
                    (
                        dot_tn(slope, key) * scale,
                        dot_nn(slope, query) * scale,
                        dot_nn(weights.astype(BF), change),
                    )
                )
            for third in range(3):
                to = third * width + at
                joined_grad[part, to : to + LANES] += jnp.where(
                    low, sides[0][third], sides[1][third]
                ).astype(BF)
        return carry

    lax.fori_loop(0, images, attend, 0)
    for third in range(3):
        columns = slice(third * width, (third + 1) * width)
        grads[:, columns] = dot_tn(first[...], joined_grad[:, columns]).astype(BF)

    def finish(start, size):
        part = pl.ds(start, size)
        change = dot_nt(joined_grad[part, :], packed[:, : 3 * width])
        unit, inverse = normalize(tokens[part, :].astype(F32))
        tail = change * unit
        totals[2] += jnp.sum(tail.reshape(size // 8, 8, width), 0)
        totals[3] += jnp.sum(change.reshape(size // 8, 8, width), 0)
        change = change * gain_one
        mean = jnp.mean(change, -1, keepdims=True)
        lean = jnp.mean(change * unit, -1, keepdims=True)
        return hidden_grad[part, :] + inverse * (change - mean - unit * lean)

    block = 2 * STRIP

    def finish_loop(j, carry):
        start = pl.multiple_of(j * block, block)
        token_grad[pl.ds(start, block), :] = finish(start, block)
        return carry

    lax.fori_loop(0, real // block, finish_loop, 0)
    done = real // block * block
    if done < real:
        token_grad[done:real, :] = finish(done, ceil_to(real - done, 16))[: real - done]
    for which, row in ((2, experts), (3, experts + 1), (0, experts + 2), (1, experts + 3)):
        sums[row : row + 1, :] = jnp.sum(totals[which], 0, keepdims=True)
    grads[:, 4 * width :] = sums[...].T.astype(BF)


def retreat(
    tokens, cotangent, hidden, normed, qkv, mixed, probs, gate_grad, returned, packed, real
):
    rows, width = tokens.shape
    experts = probs.shape[0]
    shape = jax.ShapeDtypeStruct
    return pl.pallas_call(
        partial(retreat_kernel, experts),
        out_shape=(shape((real, width), F32), shape(packed.shape, BF)),
        in_specs=[pl.BlockSpec(memory_space=pltpu.VMEM)] * (9 + len(returned)),
        out_specs=[pl.BlockSpec(memory_space=pltpu.VMEM)] * 2,
        scratch_shapes=[
            pltpu.VMEM((rows, width), BF),
            pltpu.VMEM((rows, width), F32),
            pltpu.VMEM((rows, width), BF),
            pltpu.VMEM((rows, 3 * width), BF),
            pltpu.VMEM((LANES, width), F32),
            pltpu.VMEM((LANES, width), F32),
            pltpu.VMEM((4, 8, width), F32),
        ],
        compiler_params=pltpu.CompilerParams(vmem_limit_bytes=VMEM_LIMIT),
        name="retreat",
    )(tokens, cotangent, hidden, normed, qkv, mixed, probs, gate_grad, packed, *returned)


def plan_rows(routes, mine):
    owned = mine.shape[0]
    tiles = routes.shape[0] * routes.shape[2] // TILE
    mine = mine[:, None, None]
    chosen = (routes[None, :, 0] == mine) | (routes[None, :, 1] == mine)
    chosen = chosen.reshape(owned, tiles, TILE)
    flags = chosen.astype(BF)
    upper = jnp.triu(jnp.ones((TILE, TILE), BF))
    within = jnp.dot(flags.reshape(owned * tiles, TILE), upper, preferred_element_type=F32)
    within = within.reshape(owned, tiles, TILE)
    counts = within[:, :, -1]
    below = jnp.tril(jnp.ones((tiles + 1, tiles), F32), -1)
    begins = jnp.sum(below[None] * counts[:, None, :], 2)
    order = jnp.where(chosen, begins[:, :tiles, None] + within - 1.0, -1.0)
    return order, begins.astype(jnp.int32).reshape(-1)


def table_of(order, gates):
    owned, tiles, _ = order.shape
    parts = [order, gates]
    if 2 * owned < 8:
        parts.append(jnp.zeros((8 - 2 * owned, tiles, TILE), F32))
    return jnp.concatenate(parts, 0).transpose(1, 0, 2)


MESH = pl.DeviceIdType.MESH
ANY = pl.BlockSpec(memory_space=pl.ANY)
VMEM = pl.BlockSpec(memory_space=pltpu.VMEM)
PATHS = 10


class Place:
    def __init__(self):
        z, me = lax.axis_index("expert"), lax.axis_index("fsdp")
        self.me = me
        self.x = me + 2 - 4 * ((me // 2) % 2)
        turn = 4 - 8 * (me // 4)
        self.y = me + turn
        self.corner = self.x + turn
        self.swap = 1 - 2 * (me % 2)
        self.to_x, self.to_y = {"fsdp": self.x}, {"fsdp": self.y}
        self.to_core = {"fsdp": me + self.swap}
        self.to_twin = {"expert": z + 1 - 2 * (z % 2)}
        self.to_far = {"expert": (z + 2) % 4}

    def meet(self, partners):
        barrier = pltpu.get_barrier_semaphore()
        for partner in partners:
            pl.semaphore_signal(barrier, inc=1, device_id=partner, device_id_type=MESH)
        pl.semaphore_wait(barrier, len(partners))


def send_to(source, target, sent, arrived, partner):
    return pltpu.make_async_remote_copy(
        src_ref=source,
        dst_ref=target,
        send_sem=sent,
        recv_sem=arrived,
        device_id=partner,
        device_id_type=MESH,
    )


class Spread:
    def __init__(self, place, source, target, sent, arrived):
        def copy(path, piece, spot, partner):
            return send_to(piece, spot, sent.at[path], arrived.at[path], partner)

        def relay(path, spot, partner):
            return copy(path, spot, spot, partner)

        own = target.at[place.me]
        self.own_x = copy(0, source, own, place.to_x)
        self.own_y = copy(1, source, own, place.to_y)
        self.own_core = copy(2, source, own, place.to_core)
        self.x_on = relay(3, target.at[place.x, 0], place.to_y)
        self.x_core = relay(4, target.at[place.x], place.to_core)
        self.y_on = relay(5, target.at[place.y, 1], place.to_x)
        self.y_core = relay(6, target.at[place.y], place.to_core)
        self.low_core = relay(7, target.at[place.corner, 0], place.to_core)
        self.high_core = relay(8, target.at[place.corner, 1], place.to_core)
        self.last = (self.own_core, self.x_core, self.y_core, self.low_core, self.high_core)

    def start(self):
        for copy in (self.own_x, self.own_y, self.own_core):
            copy.start()

    def pass_on(self):
        self.own_x.wait_recv()
        self.x_on.start()
        self.x_core.start()
        self.own_y.wait_recv()
        self.y_on.start()
        self.y_core.start()

    def share(self):
        self.x_on.wait_recv()
        self.low_core.start()
        self.y_on.wait_recv()
        self.high_core.start()

    def finish(self):
        for copy in self.last:
            copy.wait_recv()
        for copy in self.last + (self.own_x, self.own_y, self.x_on, self.y_on):
            copy.wait_send()


def add_up(target, *terms):
    rows, columns = target.shape
    strip = max(16, 16384 // columns // 16 * 16)
    strip = min(strip, rows)

    def body(j, carry):
        part = pl.ds(pl.multiple_of(j * strip, strip), strip)
        total = terms[0][part, :].astype(F32)
        for term in terms[1:]:
            total += term[part, :].astype(F32)
        target[part, :] = total.astype(target.dtype)
        return carry

    lax.fori_loop(0, rows // strip, body, 0)


class Fold:
    def __init__(self, place, source, mine, got, bend, from_x, from_y, sent, arrived, loaded):
        def copy(path, piece, spot, partner):
            return send_to(piece, spot, sent.at[path], arrived.at[path], partner)

        slots = (place.me, place.x, place.y, place.corner)
        self.loads = [
            pltpu.make_async_copy(source.at[slot], mine.at[i], loaded.at[i])
            for i, slot in enumerate(slots)
        ]
        self.swaps = [
            copy(i, source.at[slot + place.swap], got.at[i], place.to_core)
            for i, slot in enumerate(slots)
        ]
        self.bend_y = copy(4, mine.at[3, 0], bend.at[0], place.to_y)
        self.bend_x = copy(5, mine.at[3, 1], bend.at[1], place.to_x)
        self.early_x = copy(6, mine.at[1, 1], from_x.at[1], place.to_x)
        self.early_y = copy(7, mine.at[2, 0], from_y.at[0], place.to_y)
        self.late_x = copy(8, mine.at[1, 0], from_x.at[0], place.to_x)
        self.late_y = copy(9, mine.at[2, 1], from_y.at[1], place.to_y)
        self.mine, self.got, self.bend = mine, got, bend
        self.from_x, self.from_y = from_x, from_y

    def start(self):
        for i in (3, 1, 2, 0):
            self.swaps[i].start()
            self.loads[i].start()

    def join(self, i):
        self.loads[i].wait()
        self.swaps[i].wait_recv()
        for half in range(2):
            mine = self.mine.at[i, half]
            add_up(mine, mine, self.got.at[i, half])

    def outward(self):
        self.join(3)
        self.bend_y.start()
        self.bend_x.start()
        self.join(1)
        self.early_x.start()
        self.join(2)
        self.early_y.start()

    def inward(self):
        self.bend_y.wait_recv()
        mine = self.mine.at[1, 0]
        add_up(mine, mine, self.bend.at[0])
        self.late_x.start()
        self.bend_x.wait_recv()
        mine = self.mine.at[2, 1]
        add_up(mine, mine, self.bend.at[1])
        self.late_y.start()

    def total(self, target, *more):
        self.loads[0].wait()
        self.swaps[0].wait_recv()
        for copy in (self.early_x, self.early_y, self.late_x, self.late_y):
            copy.wait_recv()
        for half in range(2):
            terms = [self.mine.at[0, half], self.got.at[0, half]]
            terms += [self.from_x.at[half], self.from_y.at[half]]
            add_up(target.at[half], *terms, *[term.at[half] for term in more])

    def finish(self):
        for copy in self.swaps:
            copy.wait_send()
        for copy in (self.bend_y, self.bend_x, self.early_x, self.early_y):
            copy.wait_send()
        self.late_x.wait_send()
        self.late_y.wait_send()


def fold_scratch(half):
    return [
        pltpu.VMEM((4, 2, *half), BF),
        pltpu.VMEM((4, 2, *half), BF),
        pltpu.VMEM((2, *half), BF),
        pltpu.VMEM((2, *half), BF),
        pltpu.VMEM((2, *half), BF),
        pltpu.SemaphoreType.DMA((PATHS,)),
        pltpu.SemaphoreType.DMA((PATHS,)),
        pltpu.SemaphoreType.DMA((4,)),
    ]


def comm_params(number):
    return pltpu.CompilerParams(
        collective_id=number, has_side_effects=True, vmem_limit_bytes=VMEM_LIMIT
    )


def gather_small_kernel(shard, full, sent, arrived, kept):
    place = Place()
    place.meet([place.to_x, place.to_y, place.to_core])
    keep = pltpu.make_async_copy(shard, full.at[place.me], kept)
    keep.start()
    spread = Spread(place, shard, full, sent, arrived)
    spread.start()
    spread.pass_on()
    spread.share()
    spread.finish()
    keep.wait()


def gather_small(shard):
    return pl.pallas_call(
        gather_small_kernel,
        out_shape=jax.ShapeDtypeStruct((8, *shard.shape), BF),
        in_specs=[VMEM],
        out_specs=VMEM,
        scratch_shapes=[
            pltpu.SemaphoreType.DMA((PATHS,)),
            pltpu.SemaphoreType.DMA((PATHS,)),
            pltpu.SemaphoreType.DMA(()),
        ],
        compiler_params=comm_params(1),
        name="gather_small",
    )(shard)


def gather_large_kernel(
    up, down, rows, upstream, gates, up_full, down_full, rows_full, upstream_full, gates_full, *sems
):
    sent, arrived, z_sent, z_arrived, kept = sems
    place = Place()
    place.meet([place.to_x, place.to_y, place.to_core, place.to_twin, place.to_far])
    twins, near, far, keeps = [], [], [], []
    for i, (source, full) in enumerate(((up, up_full), (down, down_full))):
        spot = full.at[1, place.me]
        twins.append(send_to(source, spot, z_sent.at[i], z_arrived.at[i], place.to_twin))
        near.append(Spread(place, source, full.at[0], sent.at[i], arrived.at[i]))
        far.append(Spread(place, spot, full.at[1], sent.at[2 + i], arrived.at[2 + i]))
        keeps.append(pltpu.make_async_copy(source, full.at[0, place.me], kept.at[i]))
    for copy in twins:
        copy.start()
    for spread in near:
        spread.start()
    pairs = ((rows, rows_full), (upstream, upstream_full), (gates, gates_full))
    across = []
    for i, (source, full) in enumerate(pairs):
        at = 2 + i
        across.append(
            send_to(source, full.at[1], z_sent.at[at], z_arrived.at[at], place.to_far)
        )
        keeps.append(pltpu.make_async_copy(source, full.at[0], kept.at[at]))
    for copy in across + keeps:
        copy.start()
    for i in range(2):
        near[i].pass_on()
        twins[i].wait_recv()
        far[i].start()
    for i in range(2):
        near[i].share()
        far[i].pass_on()
    for i in range(2):
        far[i].share()
    for spread in near + far:
        spread.finish()
    for copy in twins:
        copy.wait_send()
    for copy in across + keeps:
        copy.wait()


def gather_large(up, down, rows, upstream, gates):
    shape = jax.ShapeDtypeStruct
    return pl.pallas_call(
        gather_large_kernel,
        out_shape=(
            shape((2, 8, *up.shape), BF),
            shape((2, 8, *down.shape), BF),
            shape((2, *rows.shape), BF),
            shape((2, *upstream.shape), BF),
            shape((2, *gates.shape), F32),
        ),
        in_specs=[VMEM] * 5,
        out_specs=[ANY] * 5,
        scratch_shapes=[
            pltpu.SemaphoreType.DMA((4, PATHS)),
            pltpu.SemaphoreType.DMA((4, PATHS)),
            pltpu.SemaphoreType.DMA((5,)),
            pltpu.SemaphoreType.DMA((5,)),
            pltpu.SemaphoreType.DMA((5,)),
        ],
        compiler_params=comm_params(2),
        name="gather_large",
    )(up, down, rows, upstream, gates)


def reduce_large_kernel(
    up, down, rows, mixture, gates, up_total, down_total, rows_far, mixture_far, gates_far, *rest
):
    z_sent, z_arrived, up_low, down_low, up_far, down_far = rest[:6]
    buffers = rest[6:]
    place = Place()
    place.meet([place.to_x, place.to_y, place.to_core, place.to_twin, place.to_far])
    count = rows_far.shape[0]
    pairs = (
        (rows.at[pl.ds(count, count)], rows_far),
        (gates.at[:, pl.ds(count, count)], gates_far),
        (mixture.at[pl.ds(count, count)], mixture_far),
    )
    across = [
        send_to(source, target, z_sent.at[i], z_arrived.at[i], place.to_far)
        for i, (source, target) in enumerate(pairs)
    ]
    for copy in across:
        copy.start()
    sources = (up.at[1], down.at[1], up.at[0], down.at[0])
    folds = [
        Fold(place, source, *buffers[8 * i : 8 * i + 8]) for i, source in enumerate(sources)
    ]
    twins = [
        send_to(low, far, z_sent.at[3 + i], z_arrived.at[3 + i], place.to_twin)
        for i, (low, far) in enumerate(((up_low, up_far), (down_low, down_far)))
    ]
    for fold in folds:
        fold.start()
    folds[0].outward()
    folds[1].outward()
    folds[0].inward()
    folds[2].outward()
    folds[1].inward()
    folds[3].outward()
    folds[0].total(up_low)
    twins[0].start()
    folds[2].inward()
    folds[1].total(down_low)
    twins[1].start()
    folds[3].inward()
    twins[0].wait_recv()
    folds[2].total(up_total, up_far)
    twins[1].wait_recv()
    folds[3].total(down_total, down_far)
    for fold in folds:
        fold.finish()
    for copy in twins:
        copy.wait_send()
    for copy in across:
        copy.wait()


def reduce_large(up, down, rows, mixture, gates):
    shape = jax.ShapeDtypeStruct
    count = rows.shape[0] // 2
    half_up, half_down = up.shape[3:], down.shape[3:]
    return pl.pallas_call(
        reduce_large_kernel,
        out_shape=(
            shape(up.shape[2:], F32),
            shape(down.shape[2:], F32),
            shape((count, rows.shape[1]), BF),
            shape((count, mixture.shape[1]), BF),
            shape((gates.shape[0], count), F32),
        ),
        in_specs=[ANY] * 5,
        out_specs=[VMEM, VMEM, ANY, ANY, ANY],
        scratch_shapes=[
            pltpu.SemaphoreType.DMA((5,)),
            pltpu.SemaphoreType.DMA((5,)),
            pltpu.VMEM((2, *half_up), BF),
            pltpu.VMEM((2, *half_down), BF),
            pltpu.VMEM((2, *half_up), BF),
            pltpu.VMEM((2, *half_down), BF),
            *(fold_scratch(half_up) + fold_scratch(half_down)) * 2,
        ],
        compiler_params=comm_params(3),
        name="reduce_large",
    )(up, down, rows, mixture, gates)


def reduce_small_kernel(grads, total, z_sent, z_arrived, low, twin, middle, far, *buffers):
    place = Place()
    place.meet([place.to_x, place.to_y, place.to_core, place.to_twin, place.to_far])
    fold = Fold(place, grads, *buffers)
    fold.start()
    fold.outward()
    fold.inward()
    fold.total(low)
    first = send_to(low, twin, z_sent.at[0], z_arrived.at[0], place.to_twin)
    first.start()
    first.wait_recv()
    for half in range(2):
        add_up(middle.at[half], low.at[half], twin.at[half])
    second = send_to(middle, far, z_sent.at[1], z_arrived.at[1], place.to_far)
    second.start()
    second.wait_recv()
    for half in range(2):
        add_up(total.at[half], middle.at[half], far.at[half])
    fold.finish()
    first.wait_send()
    second.wait_send()


def reduce_small(grads):
    half = grads.shape[2:]
    return pl.pallas_call(
        reduce_small_kernel,
        out_shape=jax.ShapeDtypeStruct(grads.shape[1:], F32),
        in_specs=[ANY],
        out_specs=VMEM,
        scratch_shapes=[
            pltpu.SemaphoreType.DMA((2,)),
            pltpu.SemaphoreType.DMA((2,)),
            *[pltpu.VMEM((2, *half), BF)] * 4,
            *fold_scratch(half),
        ],
        compiler_params=comm_params(4),
        name="reduce_small",
    )(grads)


def pack(triple, merge, router, gain_one, bias_one, gain_two, bias_two):
    spare = LANES - router.shape[1] - 4
    columns = [vector[:, None] for vector in (gain_one, bias_one, gain_two, bias_two)]
    blank = jnp.zeros((router.shape[0], spare), F32)
    return jnp.concatenate([triple, merge, router, *columns, blank], 1).astype(BF)


def unpack(grads, width, experts):
    rest = grads[:, 4 * width :]
    return (
        rest[:, experts],
        rest[:, experts + 1],
        grads[:, : 3 * width],
        grads[:, 3 * width : 4 * width],
        rest[:, experts + 2],
        rest[:, experts + 3],
        rest[:, :experts],
    )


def local_any(
    tokens,
    routes,
    cotangent,
    attend_gain,
    attend_bias,
    triple_weight,
    merge_weight,
    mixture_gain,
    mixture_bias,
    router_weight,
    expert_up,
    expert_down,
):
    real, width = tokens.shape
    experts = router_weight.shape[1]
    owners = lax.axis_size("expert")
    capacity = 2 * TOP * real // experts
    padded = ceil_to(real, STRIP)
    here = lax.axis_index("expert")

    packed = pack(
        triple_weight,
        merge_weight,
        router_weight,
        attend_gain,
        attend_bias,
        mixture_gain,
        mixture_bias,
    )
    packed = lax.all_gather(packed, "fsdp", axis=0, tiled=True)
    up_full = lax.all_gather(expert_up.astype(BF), "fsdp", axis=0)
    down_full = lax.all_gather(expert_down.astype(BF), "fsdp", axis=0)

    token_rows = jnp.pad(tokens, ((0, padded - real), (0, 0)))
    upstream = jnp.pad(cotangent, ((0, padded - real), (0, 0)))
    route_rows = jnp.pad(routes.T, ((0, 0), (0, padded - real)), constant_values=-1)
    all_routes = lax.all_gather(route_rows, "expert", axis=0)
    order, meta = plan_rows(all_routes, here * 2 + jnp.arange(2, dtype=jnp.int32))
    tiles = owners * padded // TILE
    all_upstream = lax.all_gather(upstream, "expert", axis=0, tiled=True)

    qkv, mixed, hidden, normed, probs, gates = attend(token_rows, route_rows, packed, experts)
    all_rows = lax.all_gather(normed, "expert", axis=0, tiled=True)
    all_gates = lax.all_gather(gates, "expert", axis=0)
    own_gates = lax.dynamic_slice_in_dim(all_gates, here * 2, 2, 1)
    own_gates = own_gates.transpose(1, 0, 2).reshape(2, tiles, TILE)
    info = table_of(order, own_gates)

    mixture, row_grad, gate_grad, up_grad, down_grad = expert_block(
        meta, info, up_full[None], down_full[None], all_rows, all_upstream, owners * capacity
    )
    gate_grad = gate_grad[:2].reshape(2, owners, padded).transpose(1, 0, 2)
    gate_grad = lax.all_to_all(gate_grad, "expert", 0, 0).reshape(experts, padded)
    row_grad = lax.psum_scatter(
        row_grad.reshape(owners, padded, width), "expert", scatter_dimension=0, tiled=True
    )
    mixture = lax.psum_scatter(
        mixture.reshape(owners, padded, width), "expert", scatter_dimension=0, tiled=True
    )
    block_out = (hidden[:real] + mixture[0, :real].astype(F32)).astype(BF)
    up_grad = lax.psum_scatter(up_grad[0], "fsdp", scatter_dimension=0, tiled=True)
    down_grad = lax.psum_scatter(down_grad[0], "fsdp", scatter_dimension=0, tiled=True)

    token_grad, grads = retreat(
        token_rows,
        upstream,
        hidden,
        normed,
        qkv,
        mixed,
        probs,
        gate_grad,
        tuple(row_grad),
        packed,
        real,
    )
    grads = lax.psum_scatter(grads, "fsdp", scatter_dimension=0, tiled=True)
    grads = lax.psum(grads, "expert").astype(F32)
    return (block_out, token_grad) + unpack(grads, width, experts) + (
        up_grad[0].astype(F32),
        down_grad[0].astype(F32),
    )


def swapped(pair, flag, axis):
    return jnp.where(flag, jnp.flip(pair, axis), pair)


def local_square(
    tokens,
    routes,
    cotangent,
    attend_gain,
    attend_bias,
    triple_weight,
    merge_weight,
    mixture_gain,
    mixture_bias,
    router_weight,
    expert_up,
    expert_down,
):
    real, width = tokens.shape
    experts = router_weight.shape[1]
    capacity = 2 * TOP * real // experts
    padded = ceil_to(real, LANES)
    tiles = 2 * padded // TILE
    z = lax.axis_index("expert")
    odd, upper = z % 2 == 1, z >= 2

    shard = pack(
        triple_weight,
        merge_weight,
        router_weight,
        attend_gain,
        attend_bias,
        mixture_gain,
        mixture_bias,
    )
    packed = gather_small(shard.reshape(2, shard.shape[0] // 2, shard.shape[1]))
    packed = packed.reshape(8 * shard.shape[0], shard.shape[1])

    token_rows = jnp.pad(tokens, ((0, padded - real), (0, 0)))
    upstream = jnp.pad(cotangent, ((0, padded - real), (0, 0)))
    route_rows = jnp.pad(routes.T, ((0, 0), (0, padded - real)), constant_values=-1)
    far_routes = lax.ppermute(route_rows, "expert", [(i, (i + 2) % 4) for i in range(4)])
    mine = jnp.arange(2, dtype=jnp.int32)
    mine = jnp.concatenate([2 * z + mine, 2 * (z + 1 - 2 * (z % 2)) + mine])
    order, meta = plan_rows(jnp.stack([route_rows, far_routes]), mine)

    qkv, mixed, hidden, normed, probs, gates = attend(token_rows, route_rows, packed, experts)
    up_full, down_full, all_rows, all_upstream, all_gates = gather_large(
        expert_up.astype(BF), expert_down.astype(BF), normed, upstream, gates
    )
    own_gates = all_gates.reshape(2, 2, 2, 2, padded)
    own_gates = jnp.where(upper, own_gates[:, 1], own_gates[:, 0])
    own_gates = swapped(own_gates, odd, 1).transpose(1, 2, 0, 3)
    info = table_of(order, own_gates.reshape(4, tiles, TILE))

    mixture, row_grad, gate_grad, up_grad, down_grad = expert_block(
        meta,
        info,
        up_full,
        down_full,
        all_rows.reshape(2 * padded, width),
        all_upstream.reshape(2 * padded, width),
        2 * capacity,
    )
    up_grad, down_grad, row_far, mixture_far, gate_far = reduce_large(
        up_grad, down_grad, row_grad, mixture, gate_grad
    )
    gate_grad = jnp.stack([gate_grad[:4, :padded], gate_far[:4]]).reshape(2, 2, 2, padded)
    gate_grad = swapped(swapped(gate_grad, odd, 1), upper, 0).reshape(experts, padded)
    total = hidden[:real] + mixture[:real].astype(F32) + mixture_far[:real].astype(F32)
    block_out = total.astype(BF)
    token_grad, grads = retreat(
        token_rows,
        upstream,
        hidden,
        normed,
        qkv,
        mixed,
        probs,
        gate_grad,
        (row_grad, row_far),
        packed,
        real,
    )
    grads = reduce_small(grads.reshape(8, 2, shard.shape[0] // 2, shard.shape[1]))
    grads = grads.reshape(shard.shape)
    return (block_out, token_grad) + unpack(grads, width, experts) + (up_grad, down_grad)


def solution(mesh):
    square = dict(mesh.shape) == {"expert": 4, "fsdp": 8}
    return jax.shard_map(
        local_square if square else local_any,
        mesh=mesh,
        in_specs=(
            P(("expert", "fsdp"), None),
            P(("expert", "fsdp"), None),
            P(("expert", "fsdp"), None),
            P("fsdp"),
            P("fsdp"),
            P("fsdp", None),
            P("fsdp", None),
            P("fsdp"),
            P("fsdp"),
            P("fsdp", None),
            P("expert", "fsdp", None),
            P("expert", "fsdp", None),
        ),
        out_specs=(
            P(("expert", "fsdp"), None),
            P(("expert", "fsdp"), None),
            P("fsdp"),
            P("fsdp"),
            P("fsdp", None),
            P("fsdp", None),
            P("fsdp"),
            P("fsdp"),
            P("fsdp", None),
            P("expert", "fsdp", None),
            P("expert", "fsdp", None),
        ),
        check_vma=False,
    )
```

```python
from functools import partial

import jax
import jax.numpy as jnp
from jax import lax
from jax.experimental import pallas as pl
from jax.experimental.pallas import tpu as pltpu
from jax.sharding import PartitionSpec as P

HEAD_DIM = 64
TOP = 2
SEQ = 197
EPSILON = 1e-06
LANES = 128
TILE = 256
STRIP = 64
SUB = 128
FAR = -1e30
BF = jnp.bfloat16
F32 = jnp.float32
VMEM_LIMIT = 60 * 1024 * 1024

ERFC = (
    0.2820843458175659,
    0.282412052154541,
    0.24283546209335327,
    0.2037508189678192,
    -0.029143672436475754,
    0.2817249596118927,
    -0.49039793014526367,
    0.2861193120479584,
    -0.05938538536429405,
)


def ceil_to(value, unit):
    return -(-value // unit) * unit


def dot_nn(a, b):
    return lax.dot_general(a, b, (((1,), (0,)), ((), ())), preferred_element_type=F32)


def dot_nt(a, b):
    return lax.dot_general(a, b, (((1,), (1,)), ((), ())), preferred_element_type=F32)


def dot_tn(a, b):
    return lax.dot_general(a, b, (((0,), (0,)), ((), ())), preferred_element_type=F32)


def gelu_both(hidden):
    bell = jnp.exp(hidden * hidden * -0.5)
    t = 1.0 / (1.0 + jnp.abs(hidden) * (0.5 * 0.5**0.5))
    series = jnp.full_like(t, ERFC[-1])
    for factor in ERFC[-2::-1]:
        series = series * t + factor
    tail = (0.5 * t) * series * bell
    share = jnp.where(hidden >= 0, 1.0 - tail, tail)
    return hidden * share, share + hidden * bell * 0.3989422804014327


def normalize(values):
    center = values - jnp.mean(values, -1, keepdims=True)
    spread = jnp.mean(center * center, -1, keepdims=True)
    inverse = lax.rsqrt(spread + EPSILON)
    return center * inverse, inverse


def weight(packed, columns):
    part = packed[:, :, :, columns]
    return part.reshape(-1, part.shape[-1])


def window(image):
    start = image * SEQ // 16 * 16
    offset = image * SEQ - start
    return pl.multiple_of(start, 16), offset


WINDOW = ceil_to(SEQ + 15, 32)


def attend_kernel(
    experts, tokens, routes, packed, qkv, mixed, hidden, normed, probs, gates, first, small
):
    rows, width = tokens.shape
    images = rows // SEQ
    half = rows // 2
    small[...] = weight(packed, slice(4 * width, None)).astype(F32).T
    gain_one, bias_one = small[experts : experts + 1, :], small[experts + 1 : experts + 2, :]
    gain_two, bias_two = small[experts + 2 : experts + 3, :], small[experts + 3 : experts + 4, :]

    def norm_one(j, carry):
        part = pl.ds(pl.multiple_of(j * STRIP, STRIP), STRIP)
        unit, _ = normalize(tokens[part, :].astype(F32))
        first[part, :] = (unit * gain_one + bias_one).astype(BF)
        mixed[part, :] = jnp.zeros((STRIP, width), BF)
        return carry

    lax.fori_loop(0, rows // STRIP, norm_one, 0)
    for third in range(3):
        columns = slice(third * width, (third + 1) * width)

        def project(j, carry):
            part = pl.ds(pl.multiple_of(j * half, 16), half)
            qkv[part, columns] = dot_nn(first[part, :], weight(packed, columns)).astype(BF)
            return carry

        lax.fori_loop(0, 2, project, 0)

    lane = lax.broadcasted_iota(jnp.int32, (1, LANES), 1)
    low = lane < HEAD_DIM
    scale = 1.0 / HEAD_DIM**0.5

    def attend(image, carry):
        start, offset = window(image)
        part = pl.ds(start, WINDOW)
        place = lax.broadcasted_iota(jnp.int32, (WINDOW, 1), 0) - offset
        mine = (place >= 0) & (place < SEQ)
        across = lax.broadcasted_iota(jnp.int32, (1, WINDOW), 1) - offset
        keys_mine = (across >= 0) & (across < SEQ)
        for pair in range(width // LANES):
            at = pair * LANES
            query = qkv[part, at : at + LANES]
            key = qkv[part, width + at : width + at + LANES]
            value = qkv[part, 2 * width + at : 2 * width + at + LANES]
            both = []
            for side in (low, ~low):
                chosen = jnp.where(side, query, jnp.zeros_like(query))
                scores = jnp.where(keys_mine, dot_nt(chosen, key) * scale, FAR)
                top = jnp.max(scores, -1, keepdims=True)
                raised = jnp.exp(scores - top)
                weights = raised * (1.0 / jnp.sum(raised, -1, keepdims=True))
                both.append(dot_nn(weights.astype(BF), value))
            out = jnp.where(low, both[0], both[1]).astype(BF)
            mixed[part, at : at + LANES] = jnp.where(mine, out, mixed[part, at : at + LANES])
        return carry

    lax.fori_loop(0, images, attend, 0)

    def merge(j, carry):
        part = pl.ds(pl.multiple_of(j * half, 16), half)
        hidden[part, :] = dot_nn(mixed[part, :], weight(packed, slice(3 * width, 4 * width)))
        return carry

    lax.fori_loop(0, 2, merge, 0)

    def norm_two(j, carry):
        part = pl.ds(pl.multiple_of(j * STRIP, STRIP), STRIP)
        total = tokens[part, :].astype(F32) + hidden[part, :]
        hidden[part, :] = total
        unit, _ = normalize(total)
        normed[part, :] = (unit * gain_two + bias_two).astype(BF)
        return carry

    lax.fori_loop(0, rows // STRIP, norm_two, 0)
    router = small[0 : max(experts, 16), :].astype(BF)
    logits = dot_nt(router, normed[...])[:experts]
    raised = jnp.exp(logits - jnp.max(logits, 0, keepdims=True))
    share = raised / jnp.sum(raised, 0, keepdims=True)
    probs[...] = share
    ids = lax.broadcasted_iota(jnp.int32, (experts, rows), 0)
    picked = (routes[0:1, :] == ids) | (routes[1:2, :] == ids)
    gates[...] = jnp.where(picked, share, 0.0)


def attend(tokens, routes, packed, experts):
    rows, width = tokens.shape
    shape = jax.ShapeDtypeStruct
    return pl.pallas_call(
        partial(attend_kernel, experts),
        out_shape=(
            shape((rows, 3 * width), BF),
            shape((rows, width), BF),
            shape((rows, width), F32),
            shape((rows, width), BF),
            shape((experts, rows), F32),
            shape((experts, rows), F32),
        ),
        in_specs=[pl.BlockSpec(memory_space=pltpu.VMEM)] * 3,
        out_specs=[pl.BlockSpec(memory_space=pltpu.VMEM)] * 6,
        scratch_shapes=[pltpu.VMEM((rows, width), BF), pltpu.VMEM((LANES, width), F32)],
        compiler_params=pltpu.CompilerParams(vmem_limit_bytes=VMEM_LIMIT),
        name="attend",
    )(tokens, routes, packed)


def expert_kernel(
    tiles,
    parts,
    room,
    meta,
    info,
    up,
    down,
    rows,
    upstream,
    mixture,
    row_grad,
    gate_grad,
    up_grad,
    down_grad,
    packed_rows,
    packed_grads,
    out_sum,
    back_sum,
    out_low,
    back_low,
    up_sum,
    down_sum,
):
    width = rows.shape[1]
    step = pl.program_id(0)
    owned = out_low.shape[0]
    member = jnp.minimum(step // parts, owned - 1)
    part = step - member * parts
    span = up_sum.shape[1]
    stride = meta.shape[0] // owned

    @pl.when(step == 0)
    def _():
        def clear(j, carry):
            at = pl.ds(pl.multiple_of(j * TILE, TILE), TILE)
            for which in range(owned):
                out_low[which, at, :] = jnp.zeros((TILE, width), BF)
                back_low[which, at, :] = jnp.zeros((TILE, width), BF)
            return carry

        lax.fori_loop(0, room // TILE, clear, 0)

    @pl.when((step < owned * parts) & (part == 0))
    def _():
        def clear(j, carry):
            at = pl.ds(pl.multiple_of(j * TILE, TILE), TILE)
            packed_rows[at, :] = jnp.zeros((TILE, width), BF)
            packed_grads[at, :] = jnp.zeros((TILE, width), BF)
            return carry

        lax.fori_loop(0, room // TILE, clear, 0)

        def gather(tile, carry):
            begin = meta[member * stride + tile]
            end = meta[member * stride + tile + 1]
            base = begin // 16 * 16
            count = jnp.where(end > begin, (end - base + SUB - 1) // SUB, 0)
            at = pl.ds(pl.multiple_of(tile * TILE, TILE), TILE)
            order = info[tile, pl.ds(member, 1), :]
            columns = info[tile].T
            which = lax.broadcasted_iota(jnp.int32, (1, columns.shape[1]), 1)
            gate = jnp.where(which == owned + member, columns, 0.0)
            gate = jnp.sum(gate, -1, keepdims=True)
            source = rows[at, :]
            gated = (upstream[at, :].astype(F32) * gate).astype(BF)

            def place(j, inner):
                origin = pl.multiple_of(base + j * SUB, 16)
                wanted = lax.broadcasted_iota(jnp.int32, (SUB, 1), 0) + origin
                chosen = jnp.where(order == wanted.astype(F32), 1.0, 0.0).astype(BF)
                to = pl.ds(origin, SUB)
                packed_rows[to, :] += dot_nn(chosen, source).astype(BF)
                packed_grads[to, :] += dot_nn(chosen, gated).astype(BF)
                return inner

            return lax.fori_loop(0, count, place, carry)

        lax.fori_loop(0, tiles, gather, 0)

    @pl.when(step < owned * parts)
    def _():
        up_part = up[...].reshape(width, span)
        down_part = down[...].reshape(span, width)
        chunks = (meta[member * stride + tiles] + TILE - 1) // TILE
        up_sum[...] = jnp.zeros(up_sum.shape, F32)
        down_sum[...] = jnp.zeros(down_sum.shape, F32)

        def chunk(j, carry):
            at = pl.ds(pl.multiple_of(j * TILE, TILE), TILE)
            source = packed_rows[at, :]
            grads = packed_grads[at, :]
            active, slope = gelu_both(dot_nn(source, up_part))
            active = active.astype(BF)
            out = dot_nn(active, down_part)
            pre_grad = (dot_nt(grads, down_part) * slope).astype(BF)
            back = dot_nt(pre_grad, up_part)

            @pl.when(part == 0)
            def _():
                out_sum[at, :] = out
                back_sum[at, :] = back

            @pl.when((part > 0) & (part < parts - 1))
            def _():
                out_sum[at, :] += out
                back_sum[at, :] += back

            @pl.when(part == parts - 1)
            def _():
                out_low[member, at, :] = (out_sum[at, :] + out).astype(BF)
                back_low[member, at, :] = (back_sum[at, :] + back).astype(BF)

            down_sum[...] += dot_tn(active, grads)
            up_sum[...] += dot_tn(source, pre_grad)
            return carry

        lax.fori_loop(0, chunks, chunk, 0)
        up_grad[...] = up_sum[...].astype(BF).reshape(up_grad.shape)
        down_grad[...] = down_sum[...].astype(BF).reshape(down_grad.shape)

    @pl.when(step >= owned * parts)
    def _():
        tile = step - owned * parts
        at = pl.ds(pl.multiple_of(tile * TILE, TILE), TILE)
        columns = info[tile].T
        grads = upstream[at, :].astype(F32)
        mixture[...] = jnp.zeros(mixture.shape, mixture.dtype)
        lane = lax.broadcasted_iota(jnp.int32, (1, LANES), 1)
        zero = jnp.zeros((TILE, width), F32)
        mix, back, dots = zero, zero, jnp.zeros((TILE, LANES), F32)
        for which in range(owned):
            begin = meta[which * stride + tile]
            end = meta[which * stride + tile + 1]
            base = begin // 16 * 16
            count = jnp.where(end > begin, (end - base + TILE - 1) // TILE, 0)
            order = columns[:, which : which + 1]

            def fetch(j, carry, which=which, base=base, order=order):
                out, back = carry
                origin = pl.multiple_of(base + j * TILE, 16)
                wanted = lax.broadcasted_iota(jnp.int32, (1, TILE), 1) + origin
                chosen = jnp.where(order == wanted.astype(F32), 1.0, 0.0).astype(BF)
                source = pl.ds(origin, TILE)
                out += dot_nn(chosen, out_low[which, source, :])
                back += dot_nn(chosen, back_low[which, source, :])
                return out, back

            out, back = lax.fori_loop(0, count, fetch, (zero, back))
            mix += out * columns[:, owned + which : owned + which + 1]
            dots += jnp.where(lane == which, jnp.sum(out * grads, -1, keepdims=True), 0.0)
        mixture[...] = mix.astype(BF)
        row_grad[...] = back.astype(BF)
        gate_grad[...] = dots.T[:8]


def expert_block(meta, info, up, down, rows, upstream, most):
    groups, shards, members, rows_up, hidden_units = up.shape
    rows_down = down.shape[3]
    owned = groups * members
    count, width = rows.shape
    tiles = count // TILE
    parts = hidden_units // 512
    span = hidden_units // parts
    room = ceil_to(most, TILE) + TILE
    shape = jax.ShapeDtypeStruct
    last = owned * parts - 1

    def member_of(i):
        return jnp.minimum(i, last) // parts

    def part_of(i):
        return jnp.minimum(i, last) % parts

    up_spec = pl.BlockSpec(
        (1, shards, 1, rows_up, span),
        lambda i, *_: (member_of(i) // members, 0, member_of(i) % members, 0, part_of(i)),
    )
    down_spec = pl.BlockSpec(
        (1, span // rows_down, 1, rows_down, width),
        lambda i, *_: (member_of(i) // members, part_of(i), member_of(i) % members, 0, 0),
    )
    tile_spec = pl.BlockSpec((TILE, width), lambda i, *_: (jnp.maximum(i - last - 1, 0), 0))
    whole = pl.BlockSpec(memory_space=pltpu.VMEM)
    return pl.pallas_call(
        partial(expert_kernel, tiles, parts, room),
        grid_spec=pltpu.PrefetchScalarGridSpec(
            num_scalar_prefetch=1,
            grid=(owned * parts + tiles,),
            in_specs=[whole, up_spec, down_spec, whole, whole],
            out_specs=[
                tile_spec,
                tile_spec,
                pl.BlockSpec((8, TILE), lambda i, *_: (0, jnp.maximum(i - last - 1, 0))),
                up_spec,
                down_spec,
            ],
            scratch_shapes=[
                pltpu.VMEM((room, width), BF),
                pltpu.VMEM((room, width), BF),
                pltpu.VMEM((room, width), F32),
                pltpu.VMEM((room, width), F32),
                pltpu.VMEM((owned, room, width), BF),
                pltpu.VMEM((owned, room, width), BF),
                pltpu.VMEM((width, span), F32),
                pltpu.VMEM((span, width), F32),
            ],
        ),
        out_shape=(
            shape((count, width), BF),
            shape((count, width), BF),
            shape((8, count), F32),
            shape(up.shape, BF),
            shape(down.shape, BF),
        ),
        compiler_params=pltpu.CompilerParams(
            vmem_limit_bytes=VMEM_LIMIT, dimension_semantics=("arbitrary",)
        ),
        name="experts",
    )(meta, info, up, down, rows, upstream)


def retreat_kernel(
    experts,
    tokens,
    cotangent,
    hidden,
    normed,
    qkv,
    mixed,
    probs,
    gate_grad,
    packed,
    *rest,
):
    returned, rest = rest[:-9], rest[-9:]
    token_grad, grads, first, hidden_grad, branch_grad, joined_grad, small, sums, totals = rest
    rows, width = tokens.shape
    real = token_grad.shape[0]
    images = rows // SEQ
    half = rows // 2
    small[...] = weight(packed, slice(4 * width, None)).astype(F32).T
    gain_one, bias_one = small[experts : experts + 1, :], small[experts + 1 : experts + 2, :]
    gain_two = small[experts + 2 : experts + 3, :]
    sums[...] = jnp.zeros(sums.shape, F32)
    totals[...] = jnp.zeros(totals.shape, F32)

    share = probs[...]
    change = gate_grad[...]
    tilt = share * (change - jnp.sum(share * change, 0, keepdims=True))
    if experts < 16:
        tilt = jnp.concatenate([tilt, jnp.zeros((16 - experts, rows), F32)], 0)
    tilt = tilt.astype(BF)
    router = small[0 : tilt.shape[0], :].astype(BF)
    keep = lax.broadcasted_iota(jnp.int32, (tilt.shape[0], 1), 0) < experts
    router = jnp.where(keep, router, jnp.zeros_like(router))
    sums[0 : tilt.shape[0], :] = dot_nn(tilt, normed[...])
    hidden_grad[...] = dot_tn(tilt, router)

    def norm_two(j, carry):
        part = pl.ds(pl.multiple_of(j * STRIP, STRIP), STRIP)
        change = hidden_grad[part, :]
        for arrived in returned:
            change += arrived[part, :].astype(F32)
        unit, inverse = normalize(hidden[part, :])
        tail = change * unit
        totals[0] += jnp.sum(tail.reshape(STRIP // 8, 8, width), 0)
        totals[1] += jnp.sum(change.reshape(STRIP // 8, 8, width), 0)
        change = change * gain_two
        mean = jnp.mean(change, -1, keepdims=True)
        lean = jnp.mean(change * unit, -1, keepdims=True)
        total = cotangent[part, :].astype(F32) + inverse * (change - mean - unit * lean)
        hidden_grad[part, :] = total
        branch_grad[part, :] = total.astype(BF)
        unit, _ = normalize(tokens[part, :].astype(F32))
        first[part, :] = (unit * gain_one + bias_one).astype(BF)
        joined_grad[part, :] = jnp.zeros((STRIP, 3 * width), BF)
        return carry

    lax.fori_loop(0, rows // STRIP, norm_two, 0)
    merge = slice(3 * width, 4 * width)
    grads[:, merge] = dot_tn(mixed[...], branch_grad[...]).astype(BF)

    def project(j, carry):
        part = pl.ds(pl.multiple_of(j * half, 16), half)
        branch_grad[part, :] = dot_nt(branch_grad[part, :], weight(packed, merge)).astype(BF)
        return carry

    lax.fori_loop(0, 2, project, 0)

    lane = lax.broadcasted_iota(jnp.int32, (1, LANES), 1)
    low = lane < HEAD_DIM
    scale = 1.0 / HEAD_DIM**0.5

    def attend(image, carry):
        start, offset = window(image)
        part = pl.ds(start, WINDOW)
        place = lax.broadcasted_iota(jnp.int32, (WINDOW, 1), 0) - offset
        mine = (place >= 0) & (place < SEQ)
        for pair in range(width // LANES):
            at = pair * LANES
            query = qkv[part, at : at + LANES]
            key = qkv[part, width + at : width + at + LANES]
            value = qkv[part, 2 * width + at : 2 * width + at + LANES]
            change = branch_grad[part, at : at + LANES]
            change = jnp.where(mine, change, jnp.zeros_like(change))
            sides = []
            for side in (low, ~low):
                chosen = jnp.where(side, query, jnp.zeros_like(query))
                scores = jnp.where(mine, dot_nt(key, chosen) * scale, FAR)
                raised = jnp.exp(scores - jnp.max(scores, 0, keepdims=True))
                weights = raised * (1.0 / jnp.sum(raised, 0, keepdims=True))
                slope = dot_nt(value, jnp.where(side, change, jnp.zeros_like(change)))
                lean = jnp.sum(weights * slope, 0, keepdims=True)
                slope = (weights * (slope - lean)).astype(BF)
                sides.append(
                    (
                        dot_tn(slope, key) * scale,
                        dot_nn(slope, query) * scale,
                        dot_nn(weights.astype(BF), change),
                    )
                )
            for third in range(3):
                to = third * width + at
                joined_grad[part, to : to + LANES] += jnp.where(
                    low, sides[0][third], sides[1][third]
                ).astype(BF)
        return carry

    lax.fori_loop(0, images, attend, 0)
    for third in range(3):
        columns = slice(third * width, (third + 1) * width)
        grads[:, columns] = dot_tn(first[...], joined_grad[:, columns]).astype(BF)

    def finish(start, size):
        part = pl.ds(start, size)
        change = dot_nt(joined_grad[part, :], weight(packed, slice(0, 3 * width)))
        unit, inverse = normalize(tokens[part, :].astype(F32))
        tail = change * unit
        totals[2] += jnp.sum(tail.reshape(size // 8, 8, width), 0)
        totals[3] += jnp.sum(change.reshape(size // 8, 8, width), 0)
        change = change * gain_one
        mean = jnp.mean(change, -1, keepdims=True)
        lean = jnp.mean(change * unit, -1, keepdims=True)
        return hidden_grad[part, :] + inverse * (change - mean - unit * lean)

    block = 2 * STRIP

    def finish_loop(j, carry):
        start = pl.multiple_of(j * block, block)
        token_grad[pl.ds(start, block), :] = finish(start, block)
        return carry

    lax.fori_loop(0, real // block, finish_loop, 0)
    done = real // block * block
    if done < real:
        token_grad[done:real, :] = finish(done, ceil_to(real - done, 16))[: real - done]
    for which, row in ((2, experts), (3, experts + 1), (0, experts + 2), (1, experts + 3)):
        sums[row : row + 1, :] = jnp.sum(totals[which], 0, keepdims=True)
    grads[:, 4 * width :] = sums[...].T.astype(BF)


def retreat(
    tokens, cotangent, hidden, normed, qkv, mixed, probs, gate_grad, returned, packed, real
):
    rows, width = tokens.shape
    experts = probs.shape[0]
    shape = jax.ShapeDtypeStruct
    return pl.pallas_call(
        partial(retreat_kernel, experts),
        out_shape=(shape((real, width), F32), shape((width, packed.shape[-1]), BF)),
        in_specs=[pl.BlockSpec(memory_space=pltpu.VMEM)] * (9 + len(returned)),
        out_specs=[pl.BlockSpec(memory_space=pltpu.VMEM)] * 2,
        scratch_shapes=[
            pltpu.VMEM((rows, width), BF),
            pltpu.VMEM((rows, width), F32),
            pltpu.VMEM((rows, width), BF),
            pltpu.VMEM((rows, 3 * width), BF),
            pltpu.VMEM((LANES, width), F32),
            pltpu.VMEM((LANES, width), F32),
            pltpu.VMEM((4, 8, width), F32),
        ],
        compiler_params=pltpu.CompilerParams(vmem_limit_bytes=VMEM_LIMIT),
        name="retreat",
    )(tokens, cotangent, hidden, normed, qkv, mixed, probs, gate_grad, packed, *returned)


def plan_rows(routes, mine):
    owned = mine.shape[0]
    tiles = routes.shape[0] * routes.shape[2] // TILE
    mine = mine[:, None, None]
    chosen = (routes[None, :, 0] == mine) | (routes[None, :, 1] == mine)
    chosen = chosen.reshape(owned, tiles, TILE)
    flags = chosen.astype(BF)
    upper = jnp.triu(jnp.ones((TILE, TILE), BF))
    within = jnp.dot(flags.reshape(owned * tiles, TILE), upper, preferred_element_type=F32)
    within = within.reshape(owned, tiles, TILE)
    counts = within[:, :, -1]
    below = jnp.tril(jnp.ones((tiles + 1, tiles), F32), -1)
    begins = jnp.sum(below[None] * counts[:, None, :], 2)
    order = jnp.where(chosen, begins[:, :tiles, None] + within - 1.0, -1.0)
    return order, begins.astype(jnp.int32).reshape(-1)


def table_of(order, gates):
    owned, tiles, _ = order.shape
    parts = [order, gates]
    if 2 * owned < 8:
        parts.append(jnp.zeros((8 - 2 * owned, tiles, TILE), F32))
    return jnp.concatenate(parts, 0).transpose(1, 0, 2)


MESH = pl.DeviceIdType.MESH
ANY = pl.BlockSpec(memory_space=pl.ANY)
VMEM = pl.BlockSpec(memory_space=pltpu.VMEM)
PATHS = 10


class Place:
    def __init__(self):
        z, me = lax.axis_index("expert"), lax.axis_index("fsdp")
        self.me = me
        self.x = me + 2 - 4 * ((me // 2) % 2)
        turn = 4 - 8 * (me // 4)
        self.y = me + turn
        self.corner = self.x + turn
        self.swap = 1 - 2 * (me % 2)
        self.to_x, self.to_y = {"fsdp": self.x}, {"fsdp": self.y}
        self.to_core = {"fsdp": me + self.swap}
        self.to_twin = {"expert": z + 1 - 2 * (z % 2)}
        self.to_far = {"expert": (z + 2) % 4}

    def meet(self, partners):
        barrier = pltpu.get_barrier_semaphore()
        for partner in partners:
            pl.semaphore_signal(barrier, inc=1, device_id=partner, device_id_type=MESH)
        pl.semaphore_wait(barrier, len(partners))


def send_to(source, target, sent, arrived, partner):
    return pltpu.make_async_remote_copy(
        src_ref=source,
        dst_ref=target,
        send_sem=sent,
        recv_sem=arrived,
        device_id=partner,
        device_id_type=MESH,
    )


class Spread:
    def __init__(self, place, source, target, sent, arrived):
        def copy(path, piece, spot, partner):
            return send_to(piece, spot, sent.at[path], arrived.at[path], partner)

        def relay(path, spot, partner):
            return copy(path, spot, spot, partner)

        own = target.at[place.me]
        self.own_x = copy(0, source, own, place.to_x)
        self.own_y = copy(1, source, own, place.to_y)
        self.own_core = copy(2, source, own, place.to_core)
        self.x_on = relay(3, target.at[place.x, 0], place.to_y)
        self.x_core = relay(4, target.at[place.x], place.to_core)
        self.y_on = relay(5, target.at[place.y, 1], place.to_x)
        self.y_core = relay(6, target.at[place.y], place.to_core)
        self.low_core = relay(7, target.at[place.corner, 0], place.to_core)
        self.high_core = relay(8, target.at[place.corner, 1], place.to_core)
        self.last = (self.own_core, self.x_core, self.y_core, self.low_core, self.high_core)

    def start(self):
        for copy in (self.own_x, self.own_y, self.own_core):
            copy.start()

    def pass_on(self):
        self.own_x.wait_recv()
        self.x_on.start()
        self.x_core.start()
        self.own_y.wait_recv()
        self.y_on.start()
        self.y_core.start()

    def share(self):
        self.x_on.wait_recv()
        self.low_core.start()
        self.y_on.wait_recv()
        self.high_core.start()

    def finish(self):
        for copy in self.last:
            copy.wait_recv()
        for copy in self.last + (self.own_x, self.own_y, self.x_on, self.y_on):
            copy.wait_send()


def add_up(target, *terms):
    rows, columns = target.shape
    strip = max(16, 16384 // columns // 16 * 16)
    strip = min(strip, rows)

    def body(j, carry):
        part = pl.ds(pl.multiple_of(j * strip, strip), strip)
        total = terms[0][part, :].astype(F32)
        for term in terms[1:]:
            total += term[part, :].astype(F32)
        target[part, :] = total.astype(target.dtype)
        return carry

    lax.fori_loop(0, rows // strip, body, 0)


class Fold:
    def __init__(self, place, source, mine, got, bend, from_x, from_y, sent, arrived, loaded):
        def copy(path, piece, spot, partner):
            return send_to(piece, spot, sent.at[path], arrived.at[path], partner)

        slots = (place.me, place.x, place.y, place.corner)
        self.loads = [
            pltpu.make_async_copy(source.at[slot], mine.at[i], loaded.at[i])
            for i, slot in enumerate(slots)
        ]
        self.swaps = [
            copy(i, source.at[slot + place.swap], got.at[i], place.to_core)
            for i, slot in enumerate(slots)
        ]
        self.bend_y = copy(4, mine.at[3, 0], bend.at[0], place.to_y)
        self.bend_x = copy(5, mine.at[3, 1], bend.at[1], place.to_x)
        self.early_x = copy(6, mine.at[1, 1], from_x.at[1], place.to_x)
        self.early_y = copy(7, mine.at[2, 0], from_y.at[0], place.to_y)
        self.late_x = copy(8, mine.at[1, 0], from_x.at[0], place.to_x)
        self.late_y = copy(9, mine.at[2, 1], from_y.at[1], place.to_y)
        self.mine, self.got, self.bend = mine, got, bend
        self.from_x, self.from_y = from_x, from_y

    def start(self):
        for i in (3, 1, 2, 0):
            self.swaps[i].start()
            self.loads[i].start()

    def join(self, i):
        self.loads[i].wait()
        self.swaps[i].wait_recv()
        for half in range(2):
            mine = self.mine.at[i, half]
            add_up(mine, mine, self.got.at[i, half])

    def outward(self):
        self.join(3)
        self.bend_y.start()
        self.bend_x.start()
        self.join(1)
        self.early_x.start()
        self.join(2)
        self.early_y.start()

    def inward(self):
        self.bend_y.wait_recv()
        mine = self.mine.at[1, 0]
        add_up(mine, mine, self.bend.at[0])
        self.late_x.start()
        self.bend_x.wait_recv()
        mine = self.mine.at[2, 1]
        add_up(mine, mine, self.bend.at[1])
        self.late_y.start()

    def total(self, target, *more):
        self.loads[0].wait()
        self.swaps[0].wait_recv()
        for copy in (self.early_x, self.early_y, self.late_x, self.late_y):
            copy.wait_recv()
        for half in range(2):
            terms = [self.mine.at[0, half], self.got.at[0, half]]
            terms += [self.from_x.at[half], self.from_y.at[half]]
            add_up(target.at[half], *terms, *[term.at[half] for term in more])

    def finish(self):
        for copy in self.swaps:
            copy.wait_send()
        for copy in (self.bend_y, self.bend_x, self.early_x, self.early_y):
            copy.wait_send()
        self.late_x.wait_send()
        self.late_y.wait_send()


def fold_scratch(half):
    return [
        pltpu.VMEM((4, 2, *half), BF),
        pltpu.VMEM((4, 2, *half), BF),
        pltpu.VMEM((2, *half), BF),
        pltpu.VMEM((2, *half), BF),
        pltpu.VMEM((2, *half), BF),
        pltpu.SemaphoreType.DMA((PATHS,)),
        pltpu.SemaphoreType.DMA((PATHS,)),
        pltpu.SemaphoreType.DMA((4,)),
    ]


def comm_params(number):
    return pltpu.CompilerParams(
        collective_id=number, has_side_effects=True, vmem_limit_bytes=VMEM_LIMIT
    )


def front_kernel(
    experts,
    tokens,
    cotangent,
    routes,
    triple,
    merge,
    rest,
    up_shard,
    down_shard,
    token_rows,
    upstream,
    packed,
    qkv,
    mixed,
    hidden,
    normed,
    probs,
    up_full,
    down_full,
    rows_full,
    upstream_full,
    gates_full,
    shard,
    up,
    down,
    gates,
    first,
    small,
    sent,
    arrived,
    z_sent,
    z_arrived,
    kept,
):
    real, width = tokens.shape
    count = token_rows.shape[0]
    crossing = ceil_to(real, 16)
    place = Place()
    place.meet([place.to_x, place.to_y, place.to_core, place.to_twin, place.to_far])
    for half in range(2):
        part = slice(half * triple.shape[0] // 2, (half + 1) * triple.shape[0] // 2)
        shard[half, :, : 3 * width] = triple[part, :].astype(BF)
        shard[half, :, 3 * width : 4 * width] = merge[part, :].astype(BF)
        shard[half, :, 4 * width :] = rest[part, :].astype(BF)
    spread = Spread(place, shard, packed, sent.at[0], arrived.at[0])
    spread.start()
    keeps = [pltpu.make_async_copy(shard, packed.at[place.me], kept.at[0])]
    keeps[0].start()

    for half in range(2):
        add_up(up.at[half], up_shard.at[half])
        add_up(down.at[half], down_shard.at[half])
    twins, near, far = [], [], []
    for i, (source, full) in enumerate(((up, up_full), (down, down_full))):
        spot = full.at[1, place.me]
        twins.append(send_to(source, spot, z_sent.at[i], z_arrived.at[i], place.to_twin))
        near.append(Spread(place, source, full.at[0], sent.at[1 + i], arrived.at[1 + i]))
        far.append(Spread(place, spot, full.at[1], sent.at[3 + i], arrived.at[3 + i]))
        keeps.append(pltpu.make_async_copy(source, full.at[0, place.me], kept.at[1 + i]))
    for copy in twins:
        copy.start()
    pad_rows(cotangent, upstream)
    across = []

    def cross(source, full, whole):
        at = 2 + len(across)
        count = source.shape[0] if whole else crossing
        part = source.at[pl.ds(0, count)]
        target = full.at[1, pl.ds(0, count)]
        across.append(send_to(part, target, z_sent.at[at], z_arrived.at[at], place.to_far))
        across[-1].start()
        keeps.append(pltpu.make_async_copy(source, full.at[0], kept.at[len(keeps)]))
        keeps[-1].start()
        if not whole:
            left = pl.ds(crossing, source.shape[0] - crossing)
            copy = pltpu.make_async_copy(source.at[left], full.at[1, left], kept.at[len(keeps)])
            copy.start()
            keeps.append(copy)

    cross_first = len(keeps)
    for copy in keeps[1:cross_first]:
        copy.start()
    cross(upstream, upstream_full, False)
    pad_rows(tokens, token_rows)
    spread.pass_on()
    for other in near:
        other.start()
    spread.share()
    keeps[0].wait()
    spread.finish()

    attend_kernel(
        experts, token_rows, routes, packed, qkv, mixed, hidden, normed, probs, gates, first, small
    )
    cross(normed, rows_full, False)
    cross(gates, gates_full, True)
    for i in range(2):
        near[i].pass_on()
        twins[i].wait_recv()
        far[i].start()
    for i in range(2):
        near[i].share()
        far[i].pass_on()
    for i in range(2):
        far[i].share()
    for other in near + far:
        other.finish()
    for copy in twins:
        copy.wait_send()
    for copy in across + keeps[1:]:
        copy.wait()


def pad_rows(source, target):
    real, width = source.shape
    whole = real // STRIP * STRIP

    def body(j, carry):
        part = pl.ds(pl.multiple_of(j * STRIP, STRIP), STRIP)
        target[part, :] = source[part, :]
        return carry

    lax.fori_loop(0, whole // STRIP, body, 0)
    if whole < target.shape[0]:
        target[whole:, :] = jnp.zeros((target.shape[0] - whole, width), target.dtype)
    if whole < real:
        target[whole:real, :] = source[whole:real, :]


def front(tokens, cotangent, routes, triple, merge, rest, up, down, experts):
    real, width = tokens.shape
    rows = routes.shape[1]
    shape = jax.ShapeDtypeStruct
    columns = 4 * width + LANES
    half = triple.shape[0] // 2
    return pl.pallas_call(
        partial(front_kernel, experts),
        out_shape=(
            shape((rows, width), BF),
            shape((rows, width), BF),
            shape((8, 2, half, columns), BF),
            shape((rows, 3 * width), BF),
            shape((rows, width), BF),
            shape((rows, width), F32),
            shape((rows, width), BF),
            shape((experts, rows), F32),
            shape((2, 8, *up.shape), BF),
            shape((2, 8, *down.shape), BF),
            shape((2, rows, width), BF),
            shape((2, rows, width), BF),
            shape((2, experts, rows), F32),
        ),
        in_specs=[VMEM] * 8,
        out_specs=[VMEM] * 8 + [ANY] * 5,
        scratch_shapes=[
            pltpu.VMEM((2, half, columns), BF),
            pltpu.VMEM(up.shape, BF),
            pltpu.VMEM(down.shape, BF),
            pltpu.VMEM((experts, rows), F32),
            pltpu.VMEM((rows, width), BF),
            pltpu.VMEM((LANES, width), F32),
            pltpu.SemaphoreType.DMA((5, PATHS)),
            pltpu.SemaphoreType.DMA((5, PATHS)),
            pltpu.SemaphoreType.DMA((5,)),
            pltpu.SemaphoreType.DMA((5,)),
            pltpu.SemaphoreType.DMA((8,)),
        ],
        compiler_params=comm_params(1),
        name="front",
    )(tokens, cotangent, routes, triple, merge, rest, up, down)


def reduce_large_kernel(
    up, down, rows, mixture, gates, up_total, down_total, rows_far, mixture_far, gates_far, *rest
):
    z_sent, z_arrived, up_low, down_low, up_far, down_far = rest[:6]
    buffers = rest[6:]
    place = Place()
    place.meet([place.to_x, place.to_y, place.to_core, place.to_twin, place.to_far])
    count = rows_far.shape[0]
    pairs = (
        (rows.at[pl.ds(count, count)], rows_far),
        (gates.at[:, pl.ds(count, count)], gates_far),
        (mixture.at[pl.ds(count, count)], mixture_far),
    )
    across = [
        send_to(source, target, z_sent.at[i], z_arrived.at[i], place.to_far)
        for i, (source, target) in enumerate(pairs)
    ]
    for copy in across:
        copy.start()
    sources = (up.at[1], down.at[1], up.at[0], down.at[0])
    folds = [
        Fold(place, source, *buffers[8 * i : 8 * i + 8]) for i, source in enumerate(sources)
    ]
    twins = [
        send_to(low, far, z_sent.at[3 + i], z_arrived.at[3 + i], place.to_twin)
        for i, (low, far) in enumerate(((up_low, up_far), (down_low, down_far)))
    ]
    for fold in folds:
        fold.start()
    folds[0].outward()
    folds[1].outward()
    folds[0].inward()
    folds[2].outward()
    folds[1].inward()
    folds[3].outward()
    folds[0].total(up_low)
    twins[0].start()
    folds[2].inward()
    folds[1].total(down_low)
    twins[1].start()
    folds[3].inward()
    twins[0].wait_recv()
    folds[2].total(up_total, up_far)
    twins[1].wait_recv()
    folds[3].total(down_total, down_far)
    for fold in folds:
        fold.finish()
    for copy in twins:
        copy.wait_send()
    for copy in across:
        copy.wait()


def reduce_large(up, down, rows, mixture, gates):
    shape = jax.ShapeDtypeStruct
    count = rows.shape[0] // 2
    half_up, half_down = up.shape[3:], down.shape[3:]
    return pl.pallas_call(
        reduce_large_kernel,
        out_shape=(
            shape(up.shape[2:], F32),
            shape(down.shape[2:], F32),
            shape((count, rows.shape[1]), BF),
            shape((count, mixture.shape[1]), BF),
            shape((gates.shape[0], count), F32),
        ),
        in_specs=[ANY] * 5,
        out_specs=[VMEM, VMEM, ANY, ANY, ANY],
        scratch_shapes=[
            pltpu.SemaphoreType.DMA((5,)),
            pltpu.SemaphoreType.DMA((5,)),
            pltpu.VMEM((2, *half_up), BF),
            pltpu.VMEM((2, *half_down), BF),
            pltpu.VMEM((2, *half_up), BF),
            pltpu.VMEM((2, *half_down), BF),
            *(fold_scratch(half_up) + fold_scratch(half_down)) * 2,
        ],
        compiler_params=comm_params(3),
        name="reduce_large",
    )(up, down, rows, mixture, gates)


def reduce_small_kernel(grads, total, z_sent, z_arrived, low, twin, middle, far, *buffers):
    place = Place()
    place.meet([place.to_x, place.to_y, place.to_core, place.to_twin, place.to_far])
    fold = Fold(place, grads, *buffers)
    fold.start()
    fold.outward()
    fold.inward()
    fold.total(low)
    first = send_to(low, twin, z_sent.at[0], z_arrived.at[0], place.to_twin)
    first.start()
    first.wait_recv()
    for half in range(2):
        add_up(middle.at[half], low.at[half], twin.at[half])
    second = send_to(middle, far, z_sent.at[1], z_arrived.at[1], place.to_far)
    second.start()
    second.wait_recv()
    for half in range(2):
        add_up(total.at[half], middle.at[half], far.at[half])
    fold.finish()
    first.wait_send()
    second.wait_send()


def reduce_small(grads):
    half = grads.shape[2:]
    return pl.pallas_call(
        reduce_small_kernel,
        out_shape=jax.ShapeDtypeStruct(grads.shape[1:], F32),
        in_specs=[ANY],
        out_specs=VMEM,
        scratch_shapes=[
            pltpu.SemaphoreType.DMA((2,)),
            pltpu.SemaphoreType.DMA((2,)),
            *[pltpu.VMEM((2, *half), BF)] * 4,
            *fold_scratch(half),
        ],
        compiler_params=comm_params(4),
        name="reduce_small",
    )(grads)


def pack(triple, merge, router, gain_one, bias_one, gain_two, bias_two):
    rest = pack_small(router, gain_one, bias_one, gain_two, bias_two)
    return jnp.concatenate([triple, merge, rest], 1).astype(BF)


def pack_small(router, *vectors):
    total = jnp.pad(router, ((0, 0), (0, LANES - router.shape[1])))
    for i, vector in enumerate(vectors):
        at = router.shape[1] + i
        total += jnp.pad(vector[:, None], ((0, 0), (at, LANES - at - 1)))
    return total


def unpack(grads, width, experts):
    rest = grads[:, 4 * width :]
    return (
        rest[:, experts],
        rest[:, experts + 1],
        grads[:, : 3 * width],
        grads[:, 3 * width : 4 * width],
        rest[:, experts + 2],
        rest[:, experts + 3],
        rest[:, :experts],
    )


def local_any(
    tokens,
    routes,
    cotangent,
    attend_gain,
    attend_bias,
    triple_weight,
    merge_weight,
    mixture_gain,
    mixture_bias,
    router_weight,
    expert_up,
    expert_down,
):
    real, width = tokens.shape
    experts = router_weight.shape[1]
    owners = lax.axis_size("expert")
    capacity = 2 * TOP * real // experts
    padded = ceil_to(real, STRIP)
    here = lax.axis_index("expert")

    packed = pack(
        triple_weight,
        merge_weight,
        router_weight,
        attend_gain,
        attend_bias,
        mixture_gain,
        mixture_bias,
    )
    packed = lax.all_gather(packed, "fsdp", axis=0, tiled=True)
    packed = packed.reshape(-1, 2, STRIP // 2, packed.shape[1])
    up_full = lax.all_gather(expert_up.astype(BF), "fsdp", axis=0)
    down_full = lax.all_gather(expert_down.astype(BF), "fsdp", axis=0)

    token_rows = jnp.pad(tokens, ((0, padded - real), (0, 0)))
    upstream = jnp.pad(cotangent, ((0, padded - real), (0, 0)))
    route_rows = jnp.pad(routes.T, ((0, 0), (0, padded - real)), constant_values=-1)
    all_routes = lax.all_gather(route_rows, "expert", axis=0)
    order, meta = plan_rows(all_routes, here * 2 + jnp.arange(2, dtype=jnp.int32))
    tiles = owners * padded // TILE
    all_upstream = lax.all_gather(upstream, "expert", axis=0, tiled=True)

    qkv, mixed, hidden, normed, probs, gates = attend(token_rows, route_rows, packed, experts)
    all_rows = lax.all_gather(normed, "expert", axis=0, tiled=True)
    all_gates = lax.all_gather(gates, "expert", axis=0)
    own_gates = lax.dynamic_slice_in_dim(all_gates, here * 2, 2, 1)
    own_gates = own_gates.transpose(1, 0, 2).reshape(2, tiles, TILE)
    info = table_of(order, own_gates)

    mixture, row_grad, gate_grad, up_grad, down_grad = expert_block(
        meta, info, up_full[None], down_full[None], all_rows, all_upstream, owners * capacity
    )
    gate_grad = gate_grad[:2].reshape(2, owners, padded).transpose(1, 0, 2)
    gate_grad = lax.all_to_all(gate_grad, "expert", 0, 0).reshape(experts, padded)
    row_grad = lax.psum_scatter(
        row_grad.reshape(owners, padded, width), "expert", scatter_dimension=0, tiled=True
    )
    mixture = lax.psum_scatter(
        mixture.reshape(owners, padded, width), "expert", scatter_dimension=0, tiled=True
    )
    block_out = (hidden[:real] + mixture[0, :real].astype(F32)).astype(BF)
    up_grad = lax.psum_scatter(up_grad[0], "fsdp", scatter_dimension=0, tiled=True)
    down_grad = lax.psum_scatter(down_grad[0], "fsdp", scatter_dimension=0, tiled=True)

    token_grad, grads = retreat(
        token_rows,
        upstream,
        hidden,
        normed,
        qkv,
        mixed,
        probs,
        gate_grad,
        tuple(row_grad),
        packed,
        real,
    )
    grads = lax.psum_scatter(grads, "fsdp", scatter_dimension=0, tiled=True)
    grads = lax.psum(grads, "expert").astype(F32)
    return (block_out, token_grad) + unpack(grads, width, experts) + (
        up_grad[0].astype(F32),
        down_grad[0].astype(F32),
    )


def swapped(pair, flag, axis):
    return jnp.where(flag, jnp.flip(pair, axis), pair)


def local_square(
    tokens,
    routes,
    cotangent,
    attend_gain,
    attend_bias,
    triple_weight,
    merge_weight,
    mixture_gain,
    mixture_bias,
    router_weight,
    expert_up,
    expert_down,
):
    real, width = tokens.shape
    experts = router_weight.shape[1]
    capacity = 2 * TOP * real // experts
    padded = ceil_to(real, LANES)
    tiles = 2 * padded // TILE
    z = lax.axis_index("expert")
    odd, upper = z % 2 == 1, z >= 2

    route_rows = jnp.pad(routes.T, ((0, 0), (0, padded - real)), constant_values=-1)
    far_routes = lax.ppermute(route_rows, "expert", [(i, (i + 2) % 4) for i in range(4)])
    mine = jnp.arange(2, dtype=jnp.int32)
    mine = jnp.concatenate([2 * z + mine, 2 * (z + 1 - 2 * (z % 2)) + mine])
    order, meta = plan_rows(jnp.stack([route_rows, far_routes]), mine)
    rest = pack_small(router_weight, attend_gain, attend_bias, mixture_gain, mixture_bias)
    (
        token_rows,
        upstream,
        packed,
        qkv,
        mixed,
        hidden,
        normed,
        probs,
        up_full,
        down_full,
        all_rows,
        all_upstream,
        all_gates,
    ) = front(
        tokens,
        cotangent,
        route_rows,
        triple_weight,
        merge_weight,
        rest,
        expert_up,
        expert_down,
        experts,
    )
    own_gates = all_gates.reshape(2, 2, 2, 2, padded)
    own_gates = jnp.where(upper, own_gates[:, 1], own_gates[:, 0])
    own_gates = swapped(own_gates, odd, 1).transpose(1, 2, 0, 3)
    info = table_of(order, own_gates.reshape(4, tiles, TILE))

    mixture, row_grad, gate_grad, up_grad, down_grad = expert_block(
        meta,
        info,
        up_full,
        down_full,
        all_rows.reshape(2 * padded, width),
        all_upstream.reshape(2 * padded, width),
        2 * capacity,
    )
    up_grad, down_grad, row_far, mixture_far, gate_far = reduce_large(
        up_grad, down_grad, row_grad, mixture, gate_grad
    )
    gate_grad = jnp.stack([gate_grad[:4, :padded], gate_far[:4]]).reshape(2, 2, 2, padded)
    gate_grad = swapped(swapped(gate_grad, odd, 1), upper, 0).reshape(experts, padded)
    total = hidden[:real] + mixture[:real].astype(F32) + mixture_far[:real].astype(F32)
    block_out = total.astype(BF)
    token_grad, grads = retreat(
        token_rows,
        upstream,
        hidden,
        normed,
        qkv,
        mixed,
        probs,
        gate_grad,
        (row_grad, row_far),
        packed,
        real,
    )
    grads = reduce_small(grads.reshape(packed.shape)).reshape(-1, packed.shape[-1])
    return (block_out, token_grad) + unpack(grads, width, experts) + (up_grad, down_grad)


def solution(mesh):
    square = dict(mesh.shape) == {"expert": 4, "fsdp": 8}
    return jax.shard_map(
        local_square if square else local_any,
        mesh=mesh,
        in_specs=(
            P(("expert", "fsdp"), None),
            P(("expert", "fsdp"), None),
            P(("expert", "fsdp"), None),
            P("fsdp"),
            P("fsdp"),
            P("fsdp", None),
            P("fsdp", None),
            P("fsdp"),
            P("fsdp"),
            P("fsdp", None),
            P("expert", "fsdp", None),
            P("expert", "fsdp", None),
        ),
        out_specs=(
            P(("expert", "fsdp"), None),
            P(("expert", "fsdp"), None),
            P("fsdp"),
            P("fsdp"),
            P("fsdp", None),
            P("fsdp", None),
            P("fsdp"),
            P("fsdp"),
            P("fsdp", None),
            P("expert", "fsdp", None),
            P("expert", "fsdp", None),
        ),
        check_vma=False,
    )
```

```python
from functools import partial

import jax
import jax.numpy as jnp
from jax import lax
from jax.experimental import pallas as pl
from jax.experimental.pallas import tpu as pltpu
from jax.sharding import PartitionSpec as P

HEAD_DIM = 64
TOP = 2
SEQ = 197
EPSILON = 1e-06
LANES = 128
TILE = 256
STRIP = 64
SUB = 128
FAR = -1e30
BF = jnp.bfloat16
F32 = jnp.float32
VMEM_LIMIT = 63 * 1024 * 1024

ERFC = (
    0.2820843458175659,
    0.282412052154541,
    0.24283546209335327,
    0.2037508189678192,
    -0.029143672436475754,
    0.2817249596118927,
    -0.49039793014526367,
    0.2861193120479584,
    -0.05938538536429405,
)


def ceil_to(value, unit):
    return -(-value // unit) * unit


def dot_nn(a, b):
    return lax.dot_general(a, b, (((1,), (0,)), ((), ())), preferred_element_type=F32)


def dot_nt(a, b):
    return lax.dot_general(a, b, (((1,), (1,)), ((), ())), preferred_element_type=F32)


def dot_tn(a, b):
    return lax.dot_general(a, b, (((0,), (0,)), ((), ())), preferred_element_type=F32)


def gelu_both(hidden):
    bell = jnp.exp(hidden * hidden * -0.5)
    t = 1.0 / (1.0 + jnp.abs(hidden) * (0.5 * 0.5**0.5))
    series = jnp.full_like(t, ERFC[-1])
    for factor in ERFC[-2::-1]:
        series = series * t + factor
    tail = (0.5 * t) * series * bell
    share = jnp.where(hidden >= 0, 1.0 - tail, tail)
    return hidden * share, share + hidden * bell * 0.3989422804014327


def normalize(values):
    center = values - jnp.mean(values, -1, keepdims=True)
    spread = jnp.mean(center * center, -1, keepdims=True)
    inverse = lax.rsqrt(spread + EPSILON)
    return center * inverse, inverse


def weight(packed, columns):
    part = packed[:, :, :, columns]
    return part.reshape(-1, part.shape[-1])


def set_weight(grads, columns, value):
    spot = grads.shape[:3]
    grads[:, :, :, columns] = value.astype(BF).reshape(*spot, value.shape[1])


def window(image):
    start = image * SEQ // 16 * 16
    offset = image * SEQ - start
    return pl.multiple_of(start, 16), offset


WINDOW = ceil_to(SEQ + 15, 32)


def attend_kernel(
    experts, tokens, routes, packed, qkv, mixed, hidden, normed, probs, gates, first, small
):
    rows, width = tokens.shape
    images = rows // SEQ
    half = rows // 2
    small[...] = weight(packed, slice(4 * width, None)).astype(F32).T
    gain_one, bias_one = small[experts : experts + 1, :], small[experts + 1 : experts + 2, :]
    gain_two, bias_two = small[experts + 2 : experts + 3, :], small[experts + 3 : experts + 4, :]

    def norm_one(j, carry):
        part = pl.ds(pl.multiple_of(j * STRIP, STRIP), STRIP)
        unit, _ = normalize(tokens[part, :].astype(F32))
        first[part, :] = (unit * gain_one + bias_one).astype(BF)
        mixed[part, :] = jnp.zeros((STRIP, width), BF)
        return carry

    lax.fori_loop(0, rows // STRIP, norm_one, 0)
    for third in range(3):
        columns = slice(third * width, (third + 1) * width)

        def project(j, carry):
            part = pl.ds(pl.multiple_of(j * half, 16), half)
            qkv[part, columns] = dot_nn(first[part, :], weight(packed, columns)).astype(BF)
            return carry

        lax.fori_loop(0, 2, project, 0)

    lane = lax.broadcasted_iota(jnp.int32, (1, LANES), 1)
    low = lane < HEAD_DIM
    scale = 1.0 / HEAD_DIM**0.5

    def attend(image, carry):
        start, offset = window(image)
        part = pl.ds(start, WINDOW)
        place = lax.broadcasted_iota(jnp.int32, (WINDOW, 1), 0) - offset
        mine = (place >= 0) & (place < SEQ)
        across = lax.broadcasted_iota(jnp.int32, (1, WINDOW), 1) - offset
        keys_mine = (across >= 0) & (across < SEQ)
        for pair in range(width // LANES):
            at = pair * LANES
            query = qkv[part, at : at + LANES]
            key = qkv[part, width + at : width + at + LANES]
            value = qkv[part, 2 * width + at : 2 * width + at + LANES]
            both = []
            for side in (low, ~low):
                chosen = jnp.where(side, query, jnp.zeros_like(query))
                scores = jnp.where(keys_mine, dot_nt(chosen, key) * scale, FAR)
                top = jnp.max(scores, -1, keepdims=True)
                raised = jnp.exp(scores - top)
                weights = raised * (1.0 / jnp.sum(raised, -1, keepdims=True))
                both.append(dot_nn(weights.astype(BF), value))
            out = jnp.where(low, both[0], both[1]).astype(BF)
            mixed[part, at : at + LANES] = jnp.where(mine, out, mixed[part, at : at + LANES])
        return carry

    lax.fori_loop(0, images, attend, 0)

    def merge(j, carry):
        part = pl.ds(pl.multiple_of(j * half, 16), half)
        hidden[part, :] = dot_nn(mixed[part, :], weight(packed, slice(3 * width, 4 * width)))
        return carry

    lax.fori_loop(0, 2, merge, 0)

    def norm_two(j, carry):
        part = pl.ds(pl.multiple_of(j * STRIP, STRIP), STRIP)
        total = tokens[part, :].astype(F32) + hidden[part, :]
        hidden[part, :] = total
        unit, _ = normalize(total)
        normed[part, :] = (unit * gain_two + bias_two).astype(BF)
        return carry

    lax.fori_loop(0, rows // STRIP, norm_two, 0)
    router = small[0 : max(experts, 16), :].astype(BF)
    logits = dot_nt(router, normed[...])[:experts]
    raised = jnp.exp(logits - jnp.max(logits, 0, keepdims=True))
    share = raised / jnp.sum(raised, 0, keepdims=True)
    probs[...] = share
    ids = lax.broadcasted_iota(jnp.int32, (experts, rows), 0)
    picked = (routes[0:1, :] == ids) | (routes[1:2, :] == ids)
    gates[...] = jnp.where(picked, share, 0.0)


def attend(tokens, routes, packed, experts):
    rows, width = tokens.shape
    shape = jax.ShapeDtypeStruct
    return pl.pallas_call(
        partial(attend_kernel, experts),
        out_shape=(
            shape((rows, 3 * width), BF),
            shape((rows, width), BF),
            shape((rows, width), F32),
            shape((rows, width), BF),
            shape((experts, rows), F32),
            shape((experts, rows), F32),
        ),
        in_specs=[pl.BlockSpec(memory_space=pltpu.VMEM)] * 3,
        out_specs=[pl.BlockSpec(memory_space=pltpu.VMEM)] * 6,
        scratch_shapes=[pltpu.VMEM((rows, width), BF), pltpu.VMEM((LANES, width), F32)],
        compiler_params=pltpu.CompilerParams(vmem_limit_bytes=VMEM_LIMIT),
        name="attend",
    )(tokens, routes, packed)


def expert_kernel(
    tiles,
    parts,
    room,
    meta,
    info,
    up,
    down,
    rows,
    upstream,
    mixture,
    row_grad,
    gate_grad,
    up_grad,
    down_grad,
    packed_rows,
    packed_grads,
    out_sum,
    back_sum,
    out_low,
    back_low,
    up_sum,
    down_sum,
):
    width = rows.shape[1]
    step = pl.program_id(0)
    owned = out_low.shape[0]
    member = jnp.minimum(step // parts, owned - 1)
    part = step - member * parts
    span = up_sum.shape[1]
    stride = meta.shape[0] // owned

    @pl.when(step == 0)
    def _():
        def clear(j, carry):
            at = pl.ds(pl.multiple_of(j * TILE, TILE), TILE)
            for which in range(owned):
                out_low[which, at, :] = jnp.zeros((TILE, width), BF)
                back_low[which, at, :] = jnp.zeros((TILE, width), BF)
            return carry

        lax.fori_loop(0, room // TILE, clear, 0)

    @pl.when((step < owned * parts) & (part == 0))
    def _():
        def clear(j, carry):
            at = pl.ds(pl.multiple_of(j * TILE, TILE), TILE)
            packed_rows[at, :] = jnp.zeros((TILE, width), BF)
            packed_grads[at, :] = jnp.zeros((TILE, width), BF)
            return carry

        lax.fori_loop(0, room // TILE, clear, 0)

        def gather(tile, carry):
            begin = meta[member * stride + tile]
            end = meta[member * stride + tile + 1]
            base = begin // 16 * 16
            count = jnp.where(end > begin, (end - base + SUB - 1) // SUB, 0)
            at = pl.ds(pl.multiple_of(tile * TILE, TILE), TILE)
            order = info[tile, pl.ds(member, 1), :]
            columns = info[tile].T
            which = lax.broadcasted_iota(jnp.int32, (1, columns.shape[1]), 1)
            gate = jnp.where(which == owned + member, columns, 0.0)
            gate = jnp.sum(gate, -1, keepdims=True)
            source = rows[at, :]
            gated = (upstream[at, :].astype(F32) * gate).astype(BF)

            def place(j, inner):
                origin = pl.multiple_of(base + j * SUB, 16)
                wanted = lax.broadcasted_iota(jnp.int32, (SUB, 1), 0) + origin
                chosen = jnp.where(order == wanted.astype(F32), 1.0, 0.0).astype(BF)
                to = pl.ds(origin, SUB)
                packed_rows[to, :] += dot_nn(chosen, source).astype(BF)
                packed_grads[to, :] += dot_nn(chosen, gated).astype(BF)
                return inner

            return lax.fori_loop(0, count, place, carry)

        lax.fori_loop(0, tiles, gather, 0)

    @pl.when(step < owned * parts)
    def _():
        up_part = up[...].reshape(width, span)
        down_part = down[...].reshape(span, width)
        chunks = (meta[member * stride + tiles] + TILE - 1) // TILE
        up_sum[...] = jnp.zeros(up_sum.shape, F32)
        down_sum[...] = jnp.zeros(down_sum.shape, F32)

        def chunk(j, carry):
            at = pl.ds(pl.multiple_of(j * TILE, TILE), TILE)
            source = packed_rows[at, :]
            grads = packed_grads[at, :]
            active, slope = gelu_both(dot_nn(source, up_part))
            active = active.astype(BF)
            out = dot_nn(active, down_part)
            pre_grad = (dot_nt(grads, down_part) * slope).astype(BF)
            back = dot_nt(pre_grad, up_part)

            @pl.when(part == 0)
            def _():
                out_sum[at, :] = out
                back_sum[at, :] = back

            @pl.when((part > 0) & (part < parts - 1))
            def _():
                out_sum[at, :] += out
                back_sum[at, :] += back

            @pl.when(part == parts - 1)
            def _():
                out_low[member, at, :] = (out_sum[at, :] + out).astype(BF)
                back_low[member, at, :] = (back_sum[at, :] + back).astype(BF)

            down_sum[...] += dot_tn(active, grads)
            up_sum[...] += dot_tn(source, pre_grad)
            return carry

        lax.fori_loop(0, chunks, chunk, 0)
        up_grad[...] = up_sum[...].astype(BF).reshape(up_grad.shape)
        down_grad[...] = down_sum[...].astype(BF).reshape(down_grad.shape)

    @pl.when(step >= owned * parts)
    def _():
        tile = step - owned * parts
        at = pl.ds(pl.multiple_of(tile * TILE, TILE), TILE)
        columns = info[tile].T
        grads = upstream[at, :].astype(F32)
        mixture[...] = jnp.zeros(mixture.shape, mixture.dtype)
        lane = lax.broadcasted_iota(jnp.int32, (1, LANES), 1)
        zero = jnp.zeros((TILE, width), F32)
        mix, back, dots = zero, zero, jnp.zeros((TILE, LANES), F32)
        for which in range(owned):
            begin = meta[which * stride + tile]
            end = meta[which * stride + tile + 1]
            base = begin // 16 * 16
            count = jnp.where(end > begin, (end - base + TILE - 1) // TILE, 0)
            order = columns[:, which : which + 1]

            def fetch(j, carry, which=which, base=base, order=order):
                out, back = carry
                origin = pl.multiple_of(base + j * TILE, 16)
                wanted = lax.broadcasted_iota(jnp.int32, (1, TILE), 1) + origin
                chosen = jnp.where(order == wanted.astype(F32), 1.0, 0.0).astype(BF)
                source = pl.ds(origin, TILE)
                out += dot_nn(chosen, out_low[which, source, :])
                back += dot_nn(chosen, back_low[which, source, :])
                return out, back

            out, back = lax.fori_loop(0, count, fetch, (zero, back))
            mix += out * columns[:, owned + which : owned + which + 1]
            dots += jnp.where(lane == which, jnp.sum(out * grads, -1, keepdims=True), 0.0)
        mixture[...] = mix.astype(BF)
        row_grad[...] = back.astype(BF)
        gate_grad[...] = dots.T[:8]


def expert_block(meta, info, up, down, rows, upstream, most):
    groups, shards, members, rows_up, hidden_units = up.shape
    rows_down = down.shape[3]
    owned = groups * members
    count, width = rows.shape
    tiles = count // TILE
    parts = hidden_units // 512
    span = hidden_units // parts
    room = ceil_to(most, TILE) + TILE
    shape = jax.ShapeDtypeStruct
    last = owned * parts - 1

    def member_of(i):
        return jnp.minimum(i, last) // parts

    def part_of(i):
        return jnp.minimum(i, last) % parts

    up_spec = pl.BlockSpec(
        (1, shards, 1, rows_up, span),
        lambda i, *_: (member_of(i) // members, 0, member_of(i) % members, 0, part_of(i)),
    )
    down_spec = pl.BlockSpec(
        (1, span // rows_down, 1, rows_down, width),
        lambda i, *_: (member_of(i) // members, part_of(i), member_of(i) % members, 0, 0),
    )
    tile_spec = pl.BlockSpec((TILE, width), lambda i, *_: (jnp.maximum(i - last - 1, 0), 0))
    whole = pl.BlockSpec(memory_space=pltpu.VMEM)
    return pl.pallas_call(
        partial(expert_kernel, tiles, parts, room),
        grid_spec=pltpu.PrefetchScalarGridSpec(
            num_scalar_prefetch=1,
            grid=(owned * parts + tiles,),
            in_specs=[whole, up_spec, down_spec, whole, whole],
            out_specs=[
                tile_spec,
                tile_spec,
                pl.BlockSpec((8, TILE), lambda i, *_: (0, jnp.maximum(i - last - 1, 0))),
                up_spec,
                down_spec,
            ],
            scratch_shapes=[
                pltpu.VMEM((room, width), BF),
                pltpu.VMEM((room, width), BF),
                pltpu.VMEM((room, width), F32),
                pltpu.VMEM((room, width), F32),
                pltpu.VMEM((owned, room, width), BF),
                pltpu.VMEM((owned, room, width), BF),
                pltpu.VMEM((width, span), F32),
                pltpu.VMEM((span, width), F32),
            ],
        ),
        out_shape=(
            shape((count, width), BF),
            shape((count, width), BF),
            shape((8, count), F32),
            shape(up.shape, BF),
            shape(down.shape, BF),
        ),
        compiler_params=pltpu.CompilerParams(
            vmem_limit_bytes=VMEM_LIMIT, dimension_semantics=("arbitrary",)
        ),
        name="experts",
    )(meta, info, up, down, rows, upstream)


def retreat_kernel(
    experts,
    steps,
    tokens,
    cotangent,
    hidden,
    normed,
    qkv,
    mixed,
    probs,
    gate_grad,
    packed,
    *rest,
):
    returned, rest = rest[:-9], rest[-9:]
    token_grad, grads, first, hidden_grad, branch_grad, joined_grad, small, sums, totals = rest
    rows, width = tokens.shape
    real = token_grad.shape[0]
    images = rows // SEQ
    half = rows // 2
    small[...] = weight(packed, slice(4 * width, None)).astype(F32).T
    gain_one, bias_one = small[experts : experts + 1, :], small[experts + 1 : experts + 2, :]
    gain_two = small[experts + 2 : experts + 3, :]
    sums[...] = jnp.zeros(sums.shape, F32)
    totals[...] = jnp.zeros(totals.shape, F32)

    share = probs[...]
    change = gate_grad[...]
    tilt = share * (change - jnp.sum(share * change, 0, keepdims=True))
    if experts < 16:
        tilt = jnp.concatenate([tilt, jnp.zeros((16 - experts, rows), F32)], 0)
    tilt = tilt.astype(BF)
    router = small[0 : tilt.shape[0], :].astype(BF)
    keep = lax.broadcasted_iota(jnp.int32, (tilt.shape[0], 1), 0) < experts
    router = jnp.where(keep, router, jnp.zeros_like(router))
    sums[0 : tilt.shape[0], :] = dot_nn(tilt, normed[...])
    hidden_grad[...] = dot_tn(tilt, router)

    def norm_two(j, carry):
        part = pl.ds(pl.multiple_of(j * STRIP, STRIP), STRIP)
        change = hidden_grad[part, :]
        for arrived in returned:
            change += arrived[part, :].astype(F32)
        unit, inverse = normalize(hidden[part, :])
        tail = change * unit
        totals[0] += jnp.sum(tail.reshape(STRIP // 8, 8, width), 0)
        totals[1] += jnp.sum(change.reshape(STRIP // 8, 8, width), 0)
        change = change * gain_two
        mean = jnp.mean(change, -1, keepdims=True)
        lean = jnp.mean(change * unit, -1, keepdims=True)
        total = cotangent[part, :].astype(F32) + inverse * (change - mean - unit * lean)
        hidden_grad[part, :] = total
        branch_grad[part, :] = total.astype(BF)
        unit, _ = normalize(tokens[part, :].astype(F32))
        first[part, :] = (unit * gain_one + bias_one).astype(BF)
        joined_grad[part, :] = jnp.zeros((STRIP, 3 * width), BF)
        return carry

    lax.fori_loop(0, rows // STRIP, norm_two, 0)
    merge = slice(3 * width, 4 * width)
    set_weight(grads, merge, dot_tn(mixed[...], branch_grad[...]))

    def project(j, carry):
        part = pl.ds(pl.multiple_of(j * half, 16), half)
        branch_grad[part, :] = dot_nt(branch_grad[part, :], weight(packed, merge)).astype(BF)
        return carry

    lax.fori_loop(0, 2, project, 0)
    steps[0]()

    lane = lax.broadcasted_iota(jnp.int32, (1, LANES), 1)
    low = lane < HEAD_DIM
    scale = 1.0 / HEAD_DIM**0.5

    def attend(image, carry):
        start, offset = window(image)
        part = pl.ds(start, WINDOW)
        place = lax.broadcasted_iota(jnp.int32, (WINDOW, 1), 0) - offset
        mine = (place >= 0) & (place < SEQ)
        for pair in range(width // LANES):
            at = pair * LANES
            query = qkv[part, at : at + LANES]
            key = qkv[part, width + at : width + at + LANES]
            value = qkv[part, 2 * width + at : 2 * width + at + LANES]
            change = branch_grad[part, at : at + LANES]
            change = jnp.where(mine, change, jnp.zeros_like(change))
            sides = []
            for side in (low, ~low):
                chosen = jnp.where(side, query, jnp.zeros_like(query))
                scores = jnp.where(mine, dot_nt(key, chosen) * scale, FAR)
                raised = jnp.exp(scores - jnp.max(scores, 0, keepdims=True))
                weights = raised * (1.0 / jnp.sum(raised, 0, keepdims=True))
                slope = dot_nt(value, jnp.where(side, change, jnp.zeros_like(change)))
                lean = jnp.sum(weights * slope, 0, keepdims=True)
                slope = (weights * (slope - lean)).astype(BF)
                sides.append(
                    (
                        dot_tn(slope, key) * scale,
                        dot_nn(slope, query) * scale,
                        dot_nn(weights.astype(BF), change),
                    )
                )
            for third in range(3):
                to = third * width + at
                joined_grad[part, to : to + LANES] += jnp.where(
                    low, sides[0][third], sides[1][third]
                ).astype(BF)
        return carry

    lax.fori_loop(0, images, attend, 0)
    steps[1]()
    for third in range(3):
        columns = slice(third * width, (third + 1) * width)
        set_weight(grads, columns, dot_tn(first[...], joined_grad[:, columns]))
    steps[2]()

    def finish(start, size):
        part = pl.ds(start, size)
        change = dot_nt(joined_grad[part, :], weight(packed, slice(0, 3 * width)))
        unit, inverse = normalize(tokens[part, :].astype(F32))
        tail = change * unit
        totals[2] += jnp.sum(tail.reshape(size // 8, 8, width), 0)
        totals[3] += jnp.sum(change.reshape(size // 8, 8, width), 0)
        change = change * gain_one
        mean = jnp.mean(change, -1, keepdims=True)
        lean = jnp.mean(change * unit, -1, keepdims=True)
        return hidden_grad[part, :] + inverse * (change - mean - unit * lean)

    block = 2 * STRIP

    def finish_loop(j, carry):
        start = pl.multiple_of(j * block, block)
        token_grad[pl.ds(start, block), :] = finish(start, block)
        return carry

    lax.fori_loop(0, real // block, finish_loop, 0)
    done = real // block * block
    if done < real:
        token_grad[done:real, :] = finish(done, ceil_to(real - done, 16))[: real - done]
    for which, row in ((2, experts), (3, experts + 1), (0, experts + 2), (1, experts + 3)):
        sums[row : row + 1, :] = jnp.sum(totals[which], 0, keepdims=True)
    set_weight(grads, slice(4 * width, None), sums[...].T)


def retreat(
    tokens, cotangent, hidden, normed, qkv, mixed, probs, gate_grad, returned, packed, real
):
    rows, width = tokens.shape
    experts = probs.shape[0]
    shape = jax.ShapeDtypeStruct
    return pl.pallas_call(
        partial(retreat_kernel, experts, (lambda: None,) * 3),
        out_shape=(shape((real, width), F32), shape(packed.shape, BF)),
        in_specs=[pl.BlockSpec(memory_space=pltpu.VMEM)] * (9 + len(returned)),
        out_specs=[pl.BlockSpec(memory_space=pltpu.VMEM)] * 2,
        scratch_shapes=[
            pltpu.VMEM((rows, width), BF),
            pltpu.VMEM((rows, width), F32),
            pltpu.VMEM((rows, width), BF),
            pltpu.VMEM((rows, 3 * width), BF),
            pltpu.VMEM((LANES, width), F32),
            pltpu.VMEM((LANES, width), F32),
            pltpu.VMEM((4, 8, width), F32),
        ],
        compiler_params=pltpu.CompilerParams(vmem_limit_bytes=VMEM_LIMIT),
        name="retreat",
    )(tokens, cotangent, hidden, normed, qkv, mixed, probs, gate_grad, packed, *returned)


def plan_rows(routes, mine):
    owned = mine.shape[0]
    tiles = routes.shape[0] * routes.shape[2] // TILE
    mine = mine[:, None, None]
    chosen = (routes[None, :, 0] == mine) | (routes[None, :, 1] == mine)
    chosen = chosen.reshape(owned, tiles, TILE)
    flags = chosen.astype(BF)
    upper = jnp.triu(jnp.ones((TILE, TILE), BF))
    within = jnp.dot(flags.reshape(owned * tiles, TILE), upper, preferred_element_type=F32)
    within = within.reshape(owned, tiles, TILE)
    counts = within[:, :, -1]
    below = jnp.tril(jnp.ones((tiles + 1, tiles), F32), -1)
    begins = jnp.sum(below[None] * counts[:, None, :], 2)
    order = jnp.where(chosen, begins[:, :tiles, None] + within - 1.0, -1.0)
    return order, begins.astype(jnp.int32).reshape(-1)


def table_of(order, gates):
    owned, tiles, _ = order.shape
    parts = [order, gates]
    if 2 * owned < 8:
        parts.append(jnp.zeros((8 - 2 * owned, tiles, TILE), F32))
    return jnp.concatenate(parts, 0).transpose(1, 0, 2)


MESH = pl.DeviceIdType.MESH
ANY = pl.BlockSpec(memory_space=pl.ANY)
VMEM = pl.BlockSpec(memory_space=pltpu.VMEM)
PATHS = 10


class Place:
    def __init__(self):
        z, me = lax.axis_index("expert"), lax.axis_index("fsdp")
        self.me = me
        self.x = me + 2 - 4 * ((me // 2) % 2)
        turn = 4 - 8 * (me // 4)
        self.y = me + turn
        self.corner = self.x + turn
        self.swap = 1 - 2 * (me % 2)
        self.to_x, self.to_y = {"fsdp": self.x}, {"fsdp": self.y}
        self.to_core = {"fsdp": me + self.swap}
        self.to_twin = {"expert": z + 1 - 2 * (z % 2)}
        self.to_far = {"expert": (z + 2) % 4}

    def meet(self, partners):
        barrier = pltpu.get_barrier_semaphore()
        for partner in partners:
            pl.semaphore_signal(barrier, inc=1, device_id=partner, device_id_type=MESH)
        pl.semaphore_wait(barrier, len(partners))


def send_to(source, target, sent, arrived, partner):
    return pltpu.make_async_remote_copy(
        src_ref=source,
        dst_ref=target,
        send_sem=sent,
        recv_sem=arrived,
        device_id=partner,
        device_id_type=MESH,
    )


class Spread:
    def __init__(self, place, source, target, sent, arrived):
        def copy(path, piece, spot, partner):
            return send_to(piece, spot, sent.at[path], arrived.at[path], partner)

        def relay(path, spot, partner):
            return copy(path, spot, spot, partner)

        own = target.at[place.me]
        self.own_x = copy(0, source, own, place.to_x)
        self.own_y = copy(1, source, own, place.to_y)
        self.own_core = copy(2, source, own, place.to_core)
        self.x_on = relay(3, target.at[place.x, 0], place.to_y)
        self.x_core = relay(4, target.at[place.x], place.to_core)
        self.y_on = relay(5, target.at[place.y, 1], place.to_x)
        self.y_core = relay(6, target.at[place.y], place.to_core)
        self.low_core = relay(7, target.at[place.corner, 0], place.to_core)
        self.high_core = relay(8, target.at[place.corner, 1], place.to_core)
        self.last = (self.own_core, self.x_core, self.y_core, self.low_core, self.high_core)

    def start(self):
        for copy in (self.own_x, self.own_y, self.own_core):
            copy.start()

    def pass_on(self):
        self.own_x.wait_recv()
        self.x_on.start()
        self.x_core.start()
        self.own_y.wait_recv()
        self.y_on.start()
        self.y_core.start()

    def share(self):
        self.x_on.wait_recv()
        self.low_core.start()
        self.y_on.wait_recv()
        self.high_core.start()

    def finish(self):
        for copy in self.last:
            copy.wait_recv()
        for copy in self.last + (self.own_x, self.own_y, self.x_on, self.y_on):
            copy.wait_send()


def add_up(target, *terms):
    rows, columns = target.shape
    strip = max(16, 16384 // columns // 16 * 16)
    strip = min(strip, rows)

    def body(j, carry):
        part = pl.ds(pl.multiple_of(j * strip, strip), strip)
        total = terms[0][part, :].astype(F32)
        for term in terms[1:]:
            total += term[part, :].astype(F32)
        target[part, :] = total.astype(target.dtype)
        return carry

    lax.fori_loop(0, rows // strip, body, 0)


class Fold:
    def __init__(self, place, source, mine, got, bend, from_x, from_y, sent, arrived, loaded):
        def copy(path, piece, spot, partner):
            return send_to(piece, spot, sent.at[path], arrived.at[path], partner)

        slots = (place.me, place.x, place.y, place.corner)
        self.loads = [
            pltpu.make_async_copy(source.at[slot], mine.at[i], loaded.at[i])
            for i, slot in enumerate(slots)
        ]
        self.swaps = [
            copy(i, source.at[slot + place.swap], got.at[i], place.to_core)
            for i, slot in enumerate(slots)
        ]
        self.bend_y = copy(4, mine.at[3, 0], bend.at[0], place.to_y)
        self.bend_x = copy(5, mine.at[3, 1], bend.at[1], place.to_x)
        self.early_x = copy(6, mine.at[1, 1], from_x.at[1], place.to_x)
        self.early_y = copy(7, mine.at[2, 0], from_y.at[0], place.to_y)
        self.late_x = copy(8, mine.at[1, 0], from_x.at[0], place.to_x)
        self.late_y = copy(9, mine.at[2, 1], from_y.at[1], place.to_y)
        self.mine, self.got, self.bend = mine, got, bend
        self.from_x, self.from_y = from_x, from_y

    def start(self):
        for i in (3, 1, 2, 0):
            self.swaps[i].start()
            self.loads[i].start()

    def join(self, i):
        self.loads[i].wait()
        self.swaps[i].wait_recv()
        for half in range(2):
            mine = self.mine.at[i, half]
            add_up(mine, mine, self.got.at[i, half])

    def outward(self):
        self.join(3)
        self.bend_y.start()
        self.bend_x.start()
        self.join(1)
        self.early_x.start()
        self.join(2)
        self.early_y.start()

    def inward(self):
        self.bend_y.wait_recv()
        mine = self.mine.at[1, 0]
        add_up(mine, mine, self.bend.at[0])
        self.late_x.start()
        self.bend_x.wait_recv()
        mine = self.mine.at[2, 1]
        add_up(mine, mine, self.bend.at[1])
        self.late_y.start()

    def total(self, target, *more):
        self.loads[0].wait()
        self.swaps[0].wait_recv()
        for copy in (self.early_x, self.early_y, self.late_x, self.late_y):
            copy.wait_recv()
        for half in range(2):
            terms = [self.mine.at[0, half], self.got.at[0, half]]
            terms += [self.from_x.at[half], self.from_y.at[half]]
            add_up(target.at[half], *terms, *[term.at[half] for term in more])

    def finish(self):
        for copy in self.swaps:
            copy.wait_send()
        for copy in (self.bend_y, self.bend_x, self.early_x, self.early_y):
            copy.wait_send()
        self.late_x.wait_send()
        self.late_y.wait_send()


def fold_scratch(half):
    return [
        pltpu.VMEM((4, 2, *half), BF),
        pltpu.VMEM((4, 2, *half), BF),
        pltpu.VMEM((2, *half), BF),
        pltpu.VMEM((2, *half), BF),
        pltpu.VMEM((2, *half), BF),
        pltpu.SemaphoreType.DMA((PATHS,)),
        pltpu.SemaphoreType.DMA((PATHS,)),
        pltpu.SemaphoreType.DMA((4,)),
    ]


def comm_params(number):
    return pltpu.CompilerParams(
        collective_id=number, has_side_effects=True, vmem_limit_bytes=VMEM_LIMIT
    )


def front_kernel(
    experts,
    tokens,
    cotangent,
    routes,
    triple,
    merge,
    rest,
    up_shard,
    down_shard,
    token_rows,
    upstream,
    packed,
    qkv,
    mixed,
    hidden,
    normed,
    probs,
    up_full,
    down_full,
    rows_full,
    upstream_full,
    gates_full,
    shard,
    up,
    down,
    gates,
    first,
    small,
    sent,
    arrived,
    z_sent,
    z_arrived,
    kept,
):
    real, width = tokens.shape
    count = token_rows.shape[0]
    crossing = ceil_to(real, 16)
    place = Place()
    place.meet([place.to_x, place.to_y, place.to_core, place.to_twin, place.to_far])
    for half in range(2):
        part = slice(half * triple.shape[0] // 2, (half + 1) * triple.shape[0] // 2)
        shard[half, :, : 3 * width] = triple[part, :].astype(BF)
        shard[half, :, 3 * width : 4 * width] = merge[part, :].astype(BF)
        shard[half, :, 4 * width :] = rest[part, :].astype(BF)
    spread = Spread(place, shard, packed, sent.at[0], arrived.at[0])
    spread.start()
    keeps = [pltpu.make_async_copy(shard, packed.at[place.me], kept.at[0])]
    keeps[0].start()

    for half in range(2):
        add_up(up.at[half], up_shard.at[half])
        add_up(down.at[half], down_shard.at[half])
    twins, near, far = [], [], []
    for i, (source, full) in enumerate(((up, up_full), (down, down_full))):
        spot = full.at[1, place.me]
        twins.append(send_to(source, spot, z_sent.at[i], z_arrived.at[i], place.to_twin))
        near.append(Spread(place, source, full.at[0], sent.at[1 + i], arrived.at[1 + i]))
        far.append(Spread(place, spot, full.at[1], sent.at[3 + i], arrived.at[3 + i]))
        keeps.append(pltpu.make_async_copy(source, full.at[0, place.me], kept.at[1 + i]))
    for copy in twins:
        copy.start()
    pad_rows(cotangent, upstream)
    across = []

    def cross(source, full, whole):
        at = 2 + len(across)
        count = source.shape[0] if whole else crossing
        part = source.at[pl.ds(0, count)]
        target = full.at[1, pl.ds(0, count)]
        across.append(send_to(part, target, z_sent.at[at], z_arrived.at[at], place.to_far))
        across[-1].start()
        keeps.append(pltpu.make_async_copy(source, full.at[0], kept.at[len(keeps)]))
        keeps[-1].start()
        if not whole:
            left = pl.ds(crossing, source.shape[0] - crossing)
            copy = pltpu.make_async_copy(source.at[left], full.at[1, left], kept.at[len(keeps)])
            copy.start()
            keeps.append(copy)

    cross_first = len(keeps)
    for copy in keeps[1:cross_first]:
        copy.start()
    cross(upstream, upstream_full, False)
    pad_rows(tokens, token_rows)
    spread.pass_on()
    for other in near:
        other.start()
    spread.share()
    keeps[0].wait()
    spread.finish()

    attend_kernel(
        experts, token_rows, routes, packed, qkv, mixed, hidden, normed, probs, gates, first, small
    )
    cross(normed, rows_full, False)
    cross(gates, gates_full, True)
    for i in range(2):
        near[i].pass_on()
        twins[i].wait_recv()
        far[i].start()
    for i in range(2):
        near[i].share()
        far[i].pass_on()
    for i in range(2):
        far[i].share()
    for other in near + far:
        other.finish()
    for copy in twins:
        copy.wait_send()
    for copy in across + keeps[1:]:
        copy.wait()


def pad_rows(source, target):
    real, width = source.shape
    whole = real // STRIP * STRIP

    def body(j, carry):
        part = pl.ds(pl.multiple_of(j * STRIP, STRIP), STRIP)
        target[part, :] = source[part, :]
        return carry

    lax.fori_loop(0, whole // STRIP, body, 0)
    if whole < target.shape[0]:
        target[whole:, :] = jnp.zeros((target.shape[0] - whole, width), target.dtype)
    if whole < real:
        target[whole:real, :] = source[whole:real, :]


def front(tokens, cotangent, routes, triple, merge, rest, up, down, experts):
    real, width = tokens.shape
    rows = routes.shape[1]
    shape = jax.ShapeDtypeStruct
    columns = 4 * width + LANES
    half = triple.shape[0] // 2
    return pl.pallas_call(
        partial(front_kernel, experts),
        out_shape=(
            shape((rows, width), BF),
            shape((rows, width), BF),
            shape((8, 2, half, columns), BF),
            shape((rows, 3 * width), BF),
            shape((rows, width), BF),
            shape((rows, width), F32),
            shape((rows, width), BF),
            shape((experts, rows), F32),
            shape((2, 8, *up.shape), BF),
            shape((2, 8, *down.shape), BF),
            shape((2, rows, width), BF),
            shape((2, rows, width), BF),
            shape((2, experts, rows), F32),
        ),
        in_specs=[VMEM] * 8,
        out_specs=[VMEM] * 8 + [ANY] * 5,
        scratch_shapes=[
            pltpu.VMEM((2, half, columns), BF),
            pltpu.VMEM(up.shape, BF),
            pltpu.VMEM(down.shape, BF),
            pltpu.VMEM((experts, rows), F32),
            pltpu.VMEM((rows, width), BF),
            pltpu.VMEM((LANES, width), F32),
            pltpu.SemaphoreType.DMA((5, PATHS)),
            pltpu.SemaphoreType.DMA((5, PATHS)),
            pltpu.SemaphoreType.DMA((5,)),
            pltpu.SemaphoreType.DMA((5,)),
            pltpu.SemaphoreType.DMA((8,)),
        ],
        compiler_params=comm_params(1),
        name="front",
    )(tokens, cotangent, routes, triple, merge, rest, up, down)


def back_kernel(
    experts,
    tokens,
    cotangent,
    hidden,
    normed,
    qkv,
    mixed,
    probs,
    packed,
    gates,
    rows,
    mixture,
    up,
    down,
    block_out,
    token_grad,
    triple_total,
    merge_total,
    small_total,
    up_total,
    down_total,
    gates_far,
    rows_near,
    rows_far,
    mixture_near,
    mixture_far,
    change,
    first,
    hidden_grad,
    branch_grad,
    joined_grad,
    small,
    sums,
    totals,
    grads,
    grads_low,
    grads_twin,
    grads_middle,
    grads_far,
    up_low,
    down_low,
    up_far,
    down_far,
    z_sent,
    z_arrived,
    loaded,
    *buffers,
):
    real, width = token_grad.shape
    count = tokens.shape[0]
    crossing = ceil_to(real, 16)
    place = Place()
    place.meet([place.to_x, place.to_y, place.to_core, place.to_twin, place.to_far])
    near, far = pl.ds(0, crossing), pl.ds(count, crossing)
    pairs = (
        (rows.at[far], rows_far.at[near]),
        (gates.at[:, pl.ds(count, count)], gates_far),
        (mixture.at[far], mixture_far),
    )
    across = [
        send_to(source, target, z_sent.at[i], z_arrived.at[i], place.to_far)
        for i, (source, target) in enumerate(pairs)
    ]
    for copy in across:
        copy.start()
    sources = (up.at[1], down.at[1], up.at[0], down.at[0], grads)
    folds = [
        Fold(place, source, *buffers[8 * i : 8 * i + 8]) for i, source in enumerate(sources)
    ]
    twins = [
        send_to(low, other, z_sent.at[3 + i], z_arrived.at[3 + i], place.to_twin)
        for i, (low, other) in enumerate(
            ((up_low, up_far), (down_low, down_far), (grads_low, grads_twin))
        )
    ]
    last = send_to(grads_middle, grads_far, z_sent.at[6], z_arrived.at[6], place.to_far)
    for fold in folds[:4]:
        fold.start()
    loads = (
        pltpu.make_async_copy(rows.at[pl.ds(0, count)], rows_near, loaded.at[0]),
        pltpu.make_async_copy(mixture.at[near], mixture_near, loaded.at[1]),
    )
    for copy in loads:
        copy.start()
    rows_far[crossing:, :] = jnp.zeros((count - crossing, width), BF)
    folds[0].outward()
    folds[1].outward()
    folds[0].inward()
    folds[2].outward()
    folds[3].outward()

    across[1].wait_recv()
    z = lax.axis_index("expert")
    own = [gates[at : at + 2, :count] for at in (0, 2)]
    other = [gates_far[at : at + 2, :] for at in (0, 2)]
    odd = jnp.full((2, count), z % 2, jnp.int32) == 1
    upper = jnp.full((2, count), z // 2, jnp.int32) == 1
    for pair in (own, other):
        pair[:] = [jnp.where(odd, pair[1], pair[0]), jnp.where(odd, pair[0], pair[1])]
    for i in range(2):
        change[2 * i : 2 * i + 2, :] = jnp.where(upper, other[i], own[i])
        change[4 + 2 * i : 6 + 2 * i, :] = jnp.where(upper, own[i], other[i])
    loads[0].wait()
    across[0].wait_recv()

    def middle_step():
        folds[2].inward()
        folds[0].total(up_low)
        twins[0].start()

    def late_step():
        folds[3].inward()
        folds[1].total(down_low)
        twins[1].start()

    retreat_kernel(
        experts,
        (folds[1].inward, middle_step, late_step),
        tokens,
        cotangent,
        hidden,
        normed,
        qkv,
        mixed,
        probs,
        change,
        packed,
        rows_near,
        rows_far,
        token_grad,
        grads,
        first,
        hidden_grad,
        branch_grad,
        joined_grad,
        small,
        sums,
        totals,
    )
    tail = folds[4]
    tail.start()
    tail.outward()
    tail.inward()
    tail.total(grads_low)
    twins[2].start()

    loads[1].wait()
    across[2].wait_recv()

    def output(start, size):
        part = pl.ds(start, size)
        total = hidden[part, :] + mixture_near[part, :].astype(F32)
        return (total + mixture_far[part, :].astype(F32)).astype(BF)

    def output_loop(j, carry):
        start = pl.multiple_of(j * STRIP, STRIP)
        block_out[pl.ds(start, STRIP), :] = output(start, STRIP)
        return carry

    lax.fori_loop(0, real // STRIP, output_loop, 0)
    done = real // STRIP * STRIP
    if done < real:
        block_out[done:real, :] = output(done, crossing - done)[: real - done]

    twins[2].wait_recv()
    for half in range(2):
        add_up(grads_middle.at[half], grads_low.at[half], grads_twin.at[half])
    last.start()
    twins[0].wait_recv()
    folds[2].total(up_total, up_far)
    twins[1].wait_recv()
    folds[3].total(down_total, down_far)
    last.wait_recv()
    size = triple_total.shape[0] // 2
    for half in range(2):
        part = slice(half * size, half * size + size)
        total = grads_middle[half].astype(F32) + grads_far[half].astype(F32)
        triple_total[part, :] = total[:, : 3 * width]
        merge_total[part, :] = total[:, 3 * width : 4 * width]
        small_total[part, :] = total[:, 4 * width :]
    for fold in folds:
        fold.finish()
    for copy in across + twins + [last]:
        copy.wait_send()


def back(
    tokens, cotangent, hidden, normed, qkv, mixed, probs, packed, gates, rows, mixture, up, down, real
):
    count, width = tokens.shape
    experts = probs.shape[0]
    shape = jax.ShapeDtypeStruct
    halves = [up.shape[3:], down.shape[3:]] * 2 + [packed.shape[2:]]
    size = 2 * packed.shape[2]
    crossing = ceil_to(real, 16)
    scratch = [pltpu.VMEM((8, count), F32)]
    scratch += [pltpu.VMEM((count, width), BF)] * 2
    scratch += [pltpu.VMEM((crossing, width), BF)] * 2
    scratch += [
        pltpu.VMEM((experts, count), F32),
        pltpu.VMEM((count, width), BF),
        pltpu.VMEM((count, width), F32),
        pltpu.VMEM((count, width), BF),
        pltpu.VMEM((count, 3 * width), BF),
        pltpu.VMEM((LANES, width), F32),
        pltpu.VMEM((LANES, width), F32),
        pltpu.VMEM((4, 8, width), F32),
        pltpu.VMEM(packed.shape, BF),
    ]
    scratch += [pltpu.VMEM(packed.shape[1:], BF)] * 4
    scratch += [pltpu.VMEM((2, *half), BF) for half in halves[:4]]
    scratch += [pltpu.SemaphoreType.DMA((7,))] * 2 + [pltpu.SemaphoreType.DMA((2,))]
    for half in halves:
        scratch += fold_scratch(half)
    return pl.pallas_call(
        partial(back_kernel, experts),
        out_shape=(
            shape((real, width), BF),
            shape((real, width), F32),
            shape((size, 3 * width), F32),
            shape((size, width), F32),
            shape((size, LANES), F32),
            shape(up.shape[2:], F32),
            shape(down.shape[2:], F32),
        ),
        in_specs=[VMEM] * 9 + [ANY] * 4,
        out_specs=[VMEM] * 7,
        scratch_shapes=scratch,
        compiler_params=comm_params(3),
        name="back",
    )(tokens, cotangent, hidden, normed, qkv, mixed, probs, packed, gates, rows, mixture, up, down)


def pack(triple, merge, router, gain_one, bias_one, gain_two, bias_two):
    rest = pack_small(router, gain_one, bias_one, gain_two, bias_two)
    return jnp.concatenate([triple, merge, rest], 1).astype(BF)


def pack_small(router, *vectors):
    total = jnp.pad(router, ((0, 0), (0, LANES - router.shape[1])))
    for i, vector in enumerate(vectors):
        at = router.shape[1] + i
        total += jnp.pad(vector[:, None], ((0, 0), (at, LANES - at - 1)))
    return total


def unpack(grads, width, experts):
    rest = grads[:, 4 * width :]
    return (
        rest[:, experts],
        rest[:, experts + 1],
        grads[:, : 3 * width],
        grads[:, 3 * width : 4 * width],
        rest[:, experts + 2],
        rest[:, experts + 3],
        rest[:, :experts],
    )


def local_any(
    tokens,
    routes,
    cotangent,
    attend_gain,
    attend_bias,
    triple_weight,
    merge_weight,
    mixture_gain,
    mixture_bias,
    router_weight,
    expert_up,
    expert_down,
):
    real, width = tokens.shape
    experts = router_weight.shape[1]
    owners = lax.axis_size("expert")
    capacity = 2 * TOP * real // experts
    padded = ceil_to(real, STRIP)
    here = lax.axis_index("expert")

    packed = pack(
        triple_weight,
        merge_weight,
        router_weight,
        attend_gain,
        attend_bias,
        mixture_gain,
        mixture_bias,
    )
    packed = lax.all_gather(packed, "fsdp", axis=0, tiled=True)
    packed = packed.reshape(-1, 2, STRIP // 2, packed.shape[1])
    up_full = lax.all_gather(expert_up.astype(BF), "fsdp", axis=0)
    down_full = lax.all_gather(expert_down.astype(BF), "fsdp", axis=0)

    token_rows = jnp.pad(tokens, ((0, padded - real), (0, 0)))
    upstream = jnp.pad(cotangent, ((0, padded - real), (0, 0)))
    route_rows = jnp.pad(routes.T, ((0, 0), (0, padded - real)), constant_values=-1)
    all_routes = lax.all_gather(route_rows, "expert", axis=0)
    order, meta = plan_rows(all_routes, here * 2 + jnp.arange(2, dtype=jnp.int32))
    tiles = owners * padded // TILE
    all_upstream = lax.all_gather(upstream, "expert", axis=0, tiled=True)

    qkv, mixed, hidden, normed, probs, gates = attend(token_rows, route_rows, packed, experts)
    all_rows = lax.all_gather(normed, "expert", axis=0, tiled=True)
    all_gates = lax.all_gather(gates, "expert", axis=0)
    own_gates = lax.dynamic_slice_in_dim(all_gates, here * 2, 2, 1)
    own_gates = own_gates.transpose(1, 0, 2).reshape(2, tiles, TILE)
    info = table_of(order, own_gates)

    mixture, row_grad, gate_grad, up_grad, down_grad = expert_block(
        meta, info, up_full[None], down_full[None], all_rows, all_upstream, owners * capacity
    )
    gate_grad = gate_grad[:2].reshape(2, owners, padded).transpose(1, 0, 2)
    gate_grad = lax.all_to_all(gate_grad, "expert", 0, 0).reshape(experts, padded)
    row_grad = lax.psum_scatter(
        row_grad.reshape(owners, padded, width), "expert", scatter_dimension=0, tiled=True
    )
    mixture = lax.psum_scatter(
        mixture.reshape(owners, padded, width), "expert", scatter_dimension=0, tiled=True
    )
    block_out = (hidden[:real] + mixture[0, :real].astype(F32)).astype(BF)
    up_grad = lax.psum_scatter(up_grad[0], "fsdp", scatter_dimension=0, tiled=True)
    down_grad = lax.psum_scatter(down_grad[0], "fsdp", scatter_dimension=0, tiled=True)

    token_grad, grads = retreat(
        token_rows,
        upstream,
        hidden,
        normed,
        qkv,
        mixed,
        probs,
        gate_grad,
        tuple(row_grad),
        packed,
        real,
    )
    grads = grads.reshape(width, packed.shape[-1])
    grads = lax.psum_scatter(grads, "fsdp", scatter_dimension=0, tiled=True)
    grads = lax.psum(grads, "expert").astype(F32)
    return (block_out, token_grad) + unpack(grads, width, experts) + (
        up_grad[0].astype(F32),
        down_grad[0].astype(F32),
    )


def swapped(pair, flag, axis):
    return jnp.where(flag, jnp.flip(pair, axis), pair)


def local_square(
    tokens,
    routes,
    cotangent,
    attend_gain,
    attend_bias,
    triple_weight,
    merge_weight,
    mixture_gain,
    mixture_bias,
    router_weight,
    expert_up,
    expert_down,
):
    real, width = tokens.shape
    experts = router_weight.shape[1]
    capacity = 2 * TOP * real // experts
    padded = ceil_to(real, LANES)
    tiles = 2 * padded // TILE
    z = lax.axis_index("expert")
    odd, upper = z % 2 == 1, z >= 2

    route_rows = jnp.pad(routes.T, ((0, 0), (0, padded - real)), constant_values=-1)
    far_routes = lax.ppermute(route_rows, "expert", [(i, (i + 2) % 4) for i in range(4)])
    mine = jnp.arange(2, dtype=jnp.int32)
    mine = jnp.concatenate([2 * z + mine, 2 * (z + 1 - 2 * (z % 2)) + mine])
    order, meta = plan_rows(jnp.stack([route_rows, far_routes]), mine)
    rest = pack_small(router_weight, attend_gain, attend_bias, mixture_gain, mixture_bias)
    (
        token_rows,
        upstream,
        packed,
        qkv,
        mixed,
        hidden,
        normed,
        probs,
        up_full,
        down_full,
        all_rows,
        all_upstream,
        all_gates,
    ) = front(
        tokens,
        cotangent,
        route_rows,
        triple_weight,
        merge_weight,
        rest,
        expert_up,
        expert_down,
        experts,
    )
    own_gates = all_gates.reshape(2, 2, 2, 2, padded)
    own_gates = jnp.where(upper, own_gates[:, 1], own_gates[:, 0])
    own_gates = swapped(own_gates, odd, 1).transpose(1, 2, 0, 3)
    info = table_of(order, own_gates.reshape(4, tiles, TILE))

    mixture, row_grad, gate_grad, up_grad, down_grad = expert_block(
        meta,
        info,
        up_full,
        down_full,
        all_rows.reshape(2 * padded, width),
        all_upstream.reshape(2 * padded, width),
        2 * capacity,
    )
    block_out, token_grad, triple_grad, merge_grad, rest, up_grad, down_grad = back(
        token_rows,
        upstream,
        hidden,
        normed,
        qkv,
        mixed,
        probs,
        packed,
        gate_grad,
        row_grad,
        mixture,
        up_grad,
        down_grad,
        real,
    )
    return (
        block_out,
        token_grad,
        rest[:, experts],
        rest[:, experts + 1],
        triple_grad,
        merge_grad,
        rest[:, experts + 2],
        rest[:, experts + 3],
        rest[:, :experts],
        up_grad,
        down_grad,
    )


def solution(mesh):
    square = dict(mesh.shape) == {"expert": 4, "fsdp": 8}
    return jax.shard_map(
        local_square if square else local_any,
        mesh=mesh,
        in_specs=(
            P(("expert", "fsdp"), None),
            P(("expert", "fsdp"), None),
            P(("expert", "fsdp"), None),
            P("fsdp"),
            P("fsdp"),
            P("fsdp", None),
            P("fsdp", None),
            P("fsdp"),
            P("fsdp"),
            P("fsdp", None),
            P("expert", "fsdp", None),
            P("expert", "fsdp", None),
        ),
        out_specs=(
            P(("expert", "fsdp"), None),
            P(("expert", "fsdp"), None),
            P("fsdp"),
            P("fsdp"),
            P("fsdp", None),
            P("fsdp", None),
            P("fsdp"),
            P("fsdp"),
            P("fsdp", None),
            P("expert", "fsdp", None),
            P("expert", "fsdp", None),
        ),
        check_vma=False,
    )
```

```python
from functools import partial

import jax
import jax.numpy as jnp
from jax import lax
from jax.experimental import pallas as pl
from jax.experimental.pallas import tpu as pltpu
from jax.sharding import PartitionSpec as P

HEAD_DIM = 64
TOP = 2
SEQ = 197
EPSILON = 1e-06
LANES = 128
TILE = 256
STRIP = 64
SUB = 128
FAR = -1e30
BF = jnp.bfloat16
F32 = jnp.float32
VMEM_LIMIT = 63 * 1024 * 1024

ERFC = (
    0.2820843458175659,
    0.282412052154541,
    0.24283546209335327,
    0.2037508189678192,
    -0.029143672436475754,
    0.2817249596118927,
    -0.49039793014526367,
    0.2861193120479584,
    -0.05938538536429405,
)


def ceil_to(value, unit):
    return -(-value // unit) * unit


def dot_nn(a, b):
    return lax.dot_general(a, b, (((1,), (0,)), ((), ())), preferred_element_type=F32)


def dot_nt(a, b):
    return lax.dot_general(a, b, (((1,), (1,)), ((), ())), preferred_element_type=F32)


def dot_tn(a, b):
    return lax.dot_general(a, b, (((0,), (0,)), ((), ())), preferred_element_type=F32)


def gelu_both(hidden):
    bell = jnp.exp(hidden * hidden * -0.5)
    t = 1.0 / (1.0 + jnp.abs(hidden) * (0.5 * 0.5**0.5))
    series = jnp.full_like(t, ERFC[-1])
    for factor in ERFC[-2::-1]:
        series = series * t + factor
    tail = (0.5 * t) * series * bell
    share = jnp.where(hidden >= 0, 1.0 - tail, tail)
    return hidden * share, share + hidden * bell * 0.3989422804014327


def normalize(values):
    center = values - jnp.mean(values, -1, keepdims=True)
    spread = jnp.mean(center * center, -1, keepdims=True)
    inverse = lax.rsqrt(spread + EPSILON)
    return center * inverse, inverse


def weight(packed, columns):
    part = packed[:, :, :, columns]
    return part.reshape(-1, part.shape[-1])


def set_weight(grads, columns, value):
    spot = grads.shape[:3]
    grads[:, :, :, columns] = value.astype(BF).reshape(*spot, value.shape[1])


def window(image):
    start = image * SEQ // 16 * 16
    offset = image * SEQ - start
    return pl.multiple_of(start, 16), offset


WINDOW = ceil_to(SEQ + 15, 32)


def attend_kernel(
    experts, tokens, routes, packed, qkv, mixed, hidden, normed, probs, gates, first, small
):
    rows, width = tokens.shape
    images = rows // SEQ
    half = rows // 2
    small[...] = weight(packed, slice(4 * width, None)).astype(F32).T
    gain_one, bias_one = small[experts : experts + 1, :], small[experts + 1 : experts + 2, :]
    gain_two, bias_two = small[experts + 2 : experts + 3, :], small[experts + 3 : experts + 4, :]

    def norm_one(j, carry):
        part = pl.ds(pl.multiple_of(j * STRIP, STRIP), STRIP)
        unit, _ = normalize(tokens[part, :].astype(F32))
        first[part, :] = (unit * gain_one + bias_one).astype(BF)
        mixed[part, :] = jnp.zeros((STRIP, width), BF)
        return carry

    lax.fori_loop(0, rows // STRIP, norm_one, 0)
    for third in range(3):
        columns = slice(third * width, (third + 1) * width)

        def project(j, carry):
            part = pl.ds(pl.multiple_of(j * half, 16), half)
            qkv[part, columns] = dot_nn(first[part, :], weight(packed, columns)).astype(BF)
            return carry

        lax.fori_loop(0, 2, project, 0)

    lane = lax.broadcasted_iota(jnp.int32, (1, LANES), 1)
    low = lane < HEAD_DIM
    scale = 1.0 / HEAD_DIM**0.5

    def attend(image, carry):
        start, offset = window(image)
        part = pl.ds(start, WINDOW)
        place = lax.broadcasted_iota(jnp.int32, (WINDOW, 1), 0) - offset
        mine = (place >= 0) & (place < SEQ)
        across = lax.broadcasted_iota(jnp.int32, (1, WINDOW), 1) - offset
        keys_mine = (across >= 0) & (across < SEQ)
        for pair in range(width // LANES):
            at = pair * LANES
            query = qkv[part, at : at + LANES]
            key = qkv[part, width + at : width + at + LANES]
            value = qkv[part, 2 * width + at : 2 * width + at + LANES]
            both = []
            for side in (low, ~low):
                chosen = jnp.where(side, query, jnp.zeros_like(query))
                scores = jnp.where(keys_mine, dot_nt(chosen, key) * scale, FAR)
                top = jnp.max(scores, -1, keepdims=True)
                raised = jnp.exp(scores - top)
                weights = raised * (1.0 / jnp.sum(raised, -1, keepdims=True))
                both.append(dot_nn(weights.astype(BF), value))
            out = jnp.where(low, both[0], both[1]).astype(BF)
            mixed[part, at : at + LANES] = jnp.where(mine, out, mixed[part, at : at + LANES])
        return carry

    lax.fori_loop(0, images, attend, 0)

    def merge(j, carry):
        part = pl.ds(pl.multiple_of(j * half, 16), half)
        hidden[part, :] = dot_nn(mixed[part, :], weight(packed, slice(3 * width, 4 * width)))
        return carry

    lax.fori_loop(0, 2, merge, 0)

    def norm_two(j, carry):
        part = pl.ds(pl.multiple_of(j * STRIP, STRIP), STRIP)
        total = tokens[part, :].astype(F32) + hidden[part, :]
        hidden[part, :] = total
        unit, _ = normalize(total)
        normed[part, :] = (unit * gain_two + bias_two).astype(BF)
        return carry

    lax.fori_loop(0, rows // STRIP, norm_two, 0)
    router = small[0 : max(experts, 16), :].astype(BF)
    logits = dot_nt(router, normed[...])[:experts]
    raised = jnp.exp(logits - jnp.max(logits, 0, keepdims=True))
    share = raised / jnp.sum(raised, 0, keepdims=True)
    probs[...] = share
    ids = lax.broadcasted_iota(jnp.int32, (experts, rows), 0)
    picked = (routes[0:1, :] == ids) | (routes[1:2, :] == ids)
    gates[...] = jnp.where(picked, share, 0.0)


def attend(tokens, routes, packed, experts):
    rows, width = tokens.shape
    shape = jax.ShapeDtypeStruct
    return pl.pallas_call(
        partial(attend_kernel, experts),
        out_shape=(
            shape((rows, 3 * width), BF),
            shape((rows, width), BF),
            shape((rows, width), F32),
            shape((rows, width), BF),
            shape((experts, rows), F32),
            shape((experts, rows), F32),
        ),
        in_specs=[pl.BlockSpec(memory_space=pltpu.VMEM)] * 3,
        out_specs=[pl.BlockSpec(memory_space=pltpu.VMEM)] * 6,
        scratch_shapes=[pltpu.VMEM((rows, width), BF), pltpu.VMEM((LANES, width), F32)],
        compiler_params=pltpu.CompilerParams(vmem_limit_bytes=VMEM_LIMIT),
        name="attend",
    )(tokens, routes, packed)


def expert_kernel(
    tiles,
    parts,
    room,
    meta,
    info,
    up,
    down,
    rows,
    upstream,
    mixture,
    row_grad,
    gate_grad,
    up_grad,
    down_grad,
    slot_gate,
    out_sum,
    back_sum,
    packed,
    up_sum,
    down_sum,
):
    width = rows.shape[1]
    step = pl.program_id(0)
    owned = packed.shape[0]
    member = jnp.minimum(step // parts, owned - 1)
    part = step - member * parts
    span = up_sum.shape[1]
    stride = meta.shape[0] // owned

    def windows(tile):
        bases, count = [], 0
        for which in range(owned):
            begin = meta[which * stride + tile]
            end = meta[which * stride + tile + 1]
            bases.append(begin // 16 * 16)
            used = jnp.where(end > begin, (end - bases[-1] + SUB - 1) // SUB, 0)
            count = jnp.maximum(count, used)
        return bases, count

    @pl.when(step == 0)
    def _():
        def clear(j, carry):
            at = pl.ds(pl.multiple_of(j * TILE, TILE), TILE)
            for which in range(owned):
                packed[which, at, :] = jnp.zeros((TILE, packed.shape[2]), BF)
                slot_gate[which, at, :] = jnp.zeros((TILE, LANES), F32)
            return carry

        lax.fori_loop(0, room // TILE, clear, 0)

        def gather(tile, carry):
            bases, count = windows(tile)
            at = pl.ds(pl.multiple_of(tile * TILE, TILE), TILE)
            known = info[tile]

            def place(j, inner):
                spots, chosen = [], []
                for which in range(owned):
                    origin = pl.multiple_of(bases[which] + j * SUB, 16)
                    wanted = lax.broadcasted_iota(jnp.int32, (SUB, 1), 0) + origin
                    hit = known[which : which + 1, :] == wanted.astype(F32)
                    gate = jnp.where(hit, known[owned + which : owned + which + 1, :], 0.0)
                    to = pl.ds(origin, SUB)
                    slot_gate[which, to, :] += jnp.sum(gate, -1, keepdims=True)
                    spots.append(to)
                    chosen.append(jnp.where(hit, 1.0, 0.0).astype(BF))
                chosen = jnp.concatenate(chosen, 0)
                for at_column, source in ((0, rows), (width, upstream)):
                    picked = dot_nn(chosen, source[at, :]).astype(BF)
                    columns = slice(at_column, at_column + width)
                    for which, to in enumerate(spots):
                        packed[which, to, columns] += picked[which * SUB : (which + 1) * SUB]
                return inner

            return lax.fori_loop(0, count, place, carry)

        lax.fori_loop(0, tiles, gather, 0)

    @pl.when(step < owned * parts)
    def _():
        up_part = up[...].reshape(width, span)
        down_part = down[...].reshape(span, width)
        chunks = (meta[member * stride + tiles] + TILE - 1) // TILE
        up_sum[...] = jnp.zeros(up_sum.shape, F32)
        down_sum[...] = jnp.zeros(down_sum.shape, F32)

        def chunk(j, carry):
            at = pl.ds(pl.multiple_of(j * TILE, TILE), TILE)
            source = packed[member, at, :width]
            change = packed[member, at, width : 2 * width].astype(F32)
            gate = slot_gate[member, at, 0:1]
            grads = (change * gate).astype(BF)
            active, slope = gelu_both(dot_nn(source, up_part))
            active = active.astype(BF)
            out = dot_nn(active, down_part)
            pre_grad = (dot_nt(grads, down_part) * slope).astype(BF)
            back = dot_nt(pre_grad, up_part)

            @pl.when(part == 0)
            def _():
                out_sum[at, :] = out
                back_sum[at, :] = back

            @pl.when((part > 0) & (part < parts - 1))
            def _():
                out_sum[at, :] += out
                back_sum[at, :] += back

            @pl.when(part == parts - 1)
            def _():
                total = (out_sum[at, :] + out).astype(BF).astype(F32)
                change = packed[member, at, width : 2 * width].astype(F32)
                dots = jnp.sum(total * change, -1, keepdims=True)
                packed[member, at, :width] = (total * gate).astype(BF)
                packed[member, at, width : 2 * width] = (back_sum[at, :] + back).astype(BF)
                high = dots.astype(BF).astype(F32)
                lane = lax.broadcasted_iota(jnp.int32, (1, LANES), 1)
                both = jnp.where(lane == member, high, 0.0)
                both += jnp.where(lane == member + owned, dots - high, 0.0)
                packed[member, at, 2 * width :] = both.astype(BF)

            down_sum[...] += dot_tn(active, grads)
            up_sum[...] += dot_tn(source, pre_grad)
            return carry

        lax.fori_loop(0, chunks, chunk, 0)
        up_grad[...] = up_sum[...].astype(BF).reshape(up_grad.shape)
        down_grad[...] = down_sum[...].astype(BF).reshape(down_grad.shape)

    @pl.when(step >= owned * parts)
    def _():
        tile = step - owned * parts
        bases, count = windows(tile)
        columns = info[tile].T

        def fetch(j, total):
            chosen, source = [], []
            for which in range(owned):
                origin = pl.multiple_of(bases[which] + j * SUB, 16)
                wanted = lax.broadcasted_iota(jnp.int32, (1, SUB), 1) + origin
                hit = columns[:, which : which + 1] == wanted.astype(F32)
                chosen.append(jnp.where(hit, 1.0, 0.0).astype(BF))
                source.append(packed[which, pl.ds(origin, SUB), :])
            return total + dot_nn(jnp.concatenate(chosen, 1), jnp.concatenate(source, 0))

        total = lax.fori_loop(0, count, fetch, jnp.zeros((TILE, packed.shape[2]), F32))
        mixture[...] = total[:, :width].astype(BF)
        row_grad[...] = total[:, width : 2 * width].astype(BF)
        dots = total[:, 2 * width :].T
        dots = dots[:owned] + dots[owned : 2 * owned]
        gate_grad[...] = jnp.zeros(gate_grad.shape, F32)
        gate_grad[:owned, :] = dots


def expert_block(meta, info, up, down, rows, upstream, most):
    groups, shards, members, rows_up, hidden_units = up.shape
    rows_down = down.shape[3]
    owned = groups * members
    count, width = rows.shape
    tiles = count // TILE
    parts = hidden_units // 512
    span = hidden_units // parts
    held = ceil_to(most, TILE)
    room = ceil_to(most + 3 * SUB, TILE)
    shape = jax.ShapeDtypeStruct
    last = owned * parts - 1

    def member_of(i):
        return jnp.minimum(i, last) // parts

    def part_of(i):
        return jnp.minimum(i, last) % parts

    up_spec = pl.BlockSpec(
        (1, shards, 1, rows_up, span),
        lambda i, *_: (member_of(i) // members, 0, member_of(i) % members, 0, part_of(i)),
    )
    down_spec = pl.BlockSpec(
        (1, span // rows_down, 1, rows_down, width),
        lambda i, *_: (member_of(i) // members, part_of(i), member_of(i) % members, 0, 0),
    )
    tile_spec = pl.BlockSpec((TILE, width), lambda i, *_: (jnp.maximum(i - last - 1, 0), 0))
    whole = pl.BlockSpec(memory_space=pltpu.VMEM)
    return pl.pallas_call(
        partial(expert_kernel, tiles, parts, room),
        grid_spec=pltpu.PrefetchScalarGridSpec(
            num_scalar_prefetch=1,
            grid=(owned * parts + tiles,),
            in_specs=[whole, up_spec, down_spec, whole, whole],
            out_specs=[
                tile_spec,
                tile_spec,
                pl.BlockSpec((8, TILE), lambda i, *_: (0, jnp.maximum(i - last - 1, 0))),
                up_spec,
                down_spec,
            ],
            scratch_shapes=[
                pltpu.VMEM((owned, room, LANES), F32),
                pltpu.VMEM((held, width), F32),
                pltpu.VMEM((held, width), F32),
                pltpu.VMEM((owned, room, 2 * width + LANES), BF),
                pltpu.VMEM((width, span), F32),
                pltpu.VMEM((span, width), F32),
            ],
        ),
        out_shape=(
            shape((count, width), BF),
            shape((count, width), BF),
            shape((8, count), F32),
            shape(up.shape, BF),
            shape(down.shape, BF),
        ),
        compiler_params=pltpu.CompilerParams(
            vmem_limit_bytes=VMEM_LIMIT, dimension_semantics=("arbitrary",)
        ),
        name="experts",
    )(meta, info, up, down, rows, upstream)


def retreat_kernel(
    experts,
    steps,
    tokens,
    cotangent,
    hidden,
    normed,
    qkv,
    mixed,
    probs,
    gate_grad,
    packed,
    *rest,
):
    returned, rest = rest[:-9], rest[-9:]
    token_grad, grads, first, hidden_grad, branch_grad, joined_grad, small, sums, totals = rest
    rows, width = tokens.shape
    real = token_grad.shape[0]
    images = rows // SEQ
    half = rows // 2
    small[...] = weight(packed, slice(4 * width, None)).astype(F32).T
    gain_one, bias_one = small[experts : experts + 1, :], small[experts + 1 : experts + 2, :]
    gain_two = small[experts + 2 : experts + 3, :]
    sums[...] = jnp.zeros(sums.shape, F32)
    totals[...] = jnp.zeros(totals.shape, F32)

    share = probs[...]
    change = gate_grad[...]
    tilt = share * (change - jnp.sum(share * change, 0, keepdims=True))
    if experts < 16:
        tilt = jnp.concatenate([tilt, jnp.zeros((16 - experts, rows), F32)], 0)
    tilt = tilt.astype(BF)
    router = small[0 : tilt.shape[0], :].astype(BF)
    keep = lax.broadcasted_iota(jnp.int32, (tilt.shape[0], 1), 0) < experts
    router = jnp.where(keep, router, jnp.zeros_like(router))
    sums[0 : tilt.shape[0], :] = dot_nn(tilt, normed[...])
    hidden_grad[...] = dot_tn(tilt, router)

    def norm_two(j, carry):
        part = pl.ds(pl.multiple_of(j * STRIP, STRIP), STRIP)
        change = hidden_grad[part, :]
        for arrived in returned:
            change += arrived[part, :].astype(F32)
        unit, inverse = normalize(hidden[part, :])
        tail = change * unit
        totals[0] += jnp.sum(tail.reshape(STRIP // 8, 8, width), 0)
        totals[1] += jnp.sum(change.reshape(STRIP // 8, 8, width), 0)
        change = change * gain_two
        mean = jnp.mean(change, -1, keepdims=True)
        lean = jnp.mean(change * unit, -1, keepdims=True)
        total = cotangent[part, :].astype(F32) + inverse * (change - mean - unit * lean)
        hidden_grad[part, :] = total
        branch_grad[part, :] = total.astype(BF)
        unit, _ = normalize(tokens[part, :].astype(F32))
        first[part, :] = (unit * gain_one + bias_one).astype(BF)
        joined_grad[part, :] = jnp.zeros((STRIP, 3 * width), BF)
        return carry

    lax.fori_loop(0, rows // STRIP, norm_two, 0)
    merge = slice(3 * width, 4 * width)
    set_weight(grads, merge, dot_tn(mixed[...], branch_grad[...]))

    def project(j, carry):
        part = pl.ds(pl.multiple_of(j * half, 16), half)
        branch_grad[part, :] = dot_nt(branch_grad[part, :], weight(packed, merge)).astype(BF)
        return carry

    lax.fori_loop(0, 2, project, 0)
    steps[0]()

    lane = lax.broadcasted_iota(jnp.int32, (1, LANES), 1)
    low = lane < HEAD_DIM
    scale = 1.0 / HEAD_DIM**0.5

    def attend(image, carry):
        start, offset = window(image)
        part = pl.ds(start, WINDOW)
        place = lax.broadcasted_iota(jnp.int32, (WINDOW, 1), 0) - offset
        mine = (place >= 0) & (place < SEQ)
        for pair in range(width // LANES):
            at = pair * LANES
            query = qkv[part, at : at + LANES]
            key = qkv[part, width + at : width + at + LANES]
            value = qkv[part, 2 * width + at : 2 * width + at + LANES]
            change = branch_grad[part, at : at + LANES]
            change = jnp.where(mine, change, jnp.zeros_like(change))
            sides = []
            for side in (low, ~low):
                chosen = jnp.where(side, query, jnp.zeros_like(query))
                scores = jnp.where(mine, dot_nt(key, chosen) * scale, FAR)
                raised = jnp.exp(scores - jnp.max(scores, 0, keepdims=True))
                weights = raised * (1.0 / jnp.sum(raised, 0, keepdims=True))
                slope = dot_nt(value, jnp.where(side, change, jnp.zeros_like(change)))
                lean = jnp.sum(weights * slope, 0, keepdims=True)
                slope = (weights * (slope - lean)).astype(BF)
                sides.append(
                    (
                        dot_tn(slope, key) * scale,
                        dot_nn(slope, query) * scale,
                        dot_nn(weights.astype(BF), change),
                    )
                )
            for third in range(3):
                to = third * width + at
                joined_grad[part, to : to + LANES] += jnp.where(
                    low, sides[0][third], sides[1][third]
                ).astype(BF)
        return carry

    lax.fori_loop(0, images, attend, 0)
    steps[1]()
    for third in range(3):
        columns = slice(third * width, (third + 1) * width)
        set_weight(grads, columns, dot_tn(first[...], joined_grad[:, columns]))
    steps[2]()

    def finish(start, size):
        part = pl.ds(start, size)
        change = dot_nt(joined_grad[part, :], weight(packed, slice(0, 3 * width)))
        unit, inverse = normalize(tokens[part, :].astype(F32))
        tail = change * unit
        totals[2] += jnp.sum(tail.reshape(size // 8, 8, width), 0)
        totals[3] += jnp.sum(change.reshape(size // 8, 8, width), 0)
        change = change * gain_one
        mean = jnp.mean(change, -1, keepdims=True)
        lean = jnp.mean(change * unit, -1, keepdims=True)
        return hidden_grad[part, :] + inverse * (change - mean - unit * lean)

    block = 2 * STRIP

    def finish_loop(j, carry):
        start = pl.multiple_of(j * block, block)
        token_grad[pl.ds(start, block), :] = finish(start, block)
        return carry

    lax.fori_loop(0, real // block, finish_loop, 0)
    done = real // block * block
    if done < real:
        token_grad[done:real, :] = finish(done, ceil_to(real - done, 16))[: real - done]
    for which, row in ((2, experts), (3, experts + 1), (0, experts + 2), (1, experts + 3)):
        sums[row : row + 1, :] = jnp.sum(totals[which], 0, keepdims=True)
    set_weight(grads, slice(4 * width, None), sums[...].T)


def retreat(
    tokens, cotangent, hidden, normed, qkv, mixed, probs, gate_grad, returned, packed, real
):
    rows, width = tokens.shape
    experts = probs.shape[0]
    shape = jax.ShapeDtypeStruct
    return pl.pallas_call(
        partial(retreat_kernel, experts, (lambda: None,) * 3),
        out_shape=(shape((real, width), F32), shape(packed.shape, BF)),
        in_specs=[pl.BlockSpec(memory_space=pltpu.VMEM)] * (9 + len(returned)),
        out_specs=[pl.BlockSpec(memory_space=pltpu.VMEM)] * 2,
        scratch_shapes=[
            pltpu.VMEM((rows, width), BF),
            pltpu.VMEM((rows, width), F32),
            pltpu.VMEM((rows, width), BF),
            pltpu.VMEM((rows, 3 * width), BF),
            pltpu.VMEM((LANES, width), F32),
            pltpu.VMEM((LANES, width), F32),
            pltpu.VMEM((4, 8, width), F32),
        ],
        compiler_params=pltpu.CompilerParams(vmem_limit_bytes=VMEM_LIMIT),
        name="retreat",
    )(tokens, cotangent, hidden, normed, qkv, mixed, probs, gate_grad, packed, *returned)


def plan_rows(routes, mine):
    owned = mine.shape[0]
    tiles = routes.shape[0] * routes.shape[2] // TILE
    mine = mine[:, None, None]
    chosen = (routes[None, :, 0] == mine) | (routes[None, :, 1] == mine)
    chosen = chosen.reshape(owned, tiles, TILE)
    flags = chosen.astype(BF)
    upper = jnp.triu(jnp.ones((TILE, TILE), BF))
    within = jnp.dot(flags.reshape(owned * tiles, TILE), upper, preferred_element_type=F32)
    within = within.reshape(owned, tiles, TILE)
    counts = within[:, :, -1]
    below = jnp.tril(jnp.ones((tiles + 1, tiles), F32), -1)
    begins = jnp.sum(below[None] * counts[:, None, :], 2)
    order = jnp.where(chosen, begins[:, :tiles, None] + within - 1.0, -1.0)
    return order, begins.astype(jnp.int32).reshape(-1)


def table_of(order, gates):
    owned, tiles, _ = order.shape
    parts = [order, gates]
    if 2 * owned < 8:
        parts.append(jnp.zeros((8 - 2 * owned, tiles, TILE), F32))
    return jnp.concatenate(parts, 0).transpose(1, 0, 2)


MESH = pl.DeviceIdType.MESH
ANY = pl.BlockSpec(memory_space=pl.ANY)
VMEM = pl.BlockSpec(memory_space=pltpu.VMEM)
PATHS = 10


class Place:
    def __init__(self):
        z, me = lax.axis_index("expert"), lax.axis_index("fsdp")
        self.me = me
        self.x = me + 2 - 4 * ((me // 2) % 2)
        turn = 4 - 8 * (me // 4)
        self.y = me + turn
        self.corner = self.x + turn
        self.swap = 1 - 2 * (me % 2)
        self.to_x, self.to_y = {"fsdp": self.x}, {"fsdp": self.y}
        self.to_core = {"fsdp": me + self.swap}
        self.to_twin = {"expert": z + 1 - 2 * (z % 2)}
        self.to_far = {"expert": (z + 2) % 4}

    def meet(self, partners):
        barrier = pltpu.get_barrier_semaphore()
        for partner in partners:
            pl.semaphore_signal(barrier, inc=1, device_id=partner, device_id_type=MESH)
        pl.semaphore_wait(barrier, len(partners))


def send_to(source, target, sent, arrived, partner):
    return pltpu.make_async_remote_copy(
        src_ref=source,
        dst_ref=target,
        send_sem=sent,
        recv_sem=arrived,
        device_id=partner,
        device_id_type=MESH,
    )


class Spread:
    def __init__(self, place, source, target, sent, arrived):
        def copy(path, piece, spot, partner):
            return send_to(piece, spot, sent.at[path], arrived.at[path], partner)

        def relay(path, spot, partner):
            return copy(path, spot, spot, partner)

        own = target.at[place.me]
        self.own_x = copy(0, source, own, place.to_x)
        self.own_y = copy(1, source, own, place.to_y)
        self.own_core = copy(2, source, own, place.to_core)
        self.x_on = relay(3, target.at[place.x, 0], place.to_y)
        self.x_core = relay(4, target.at[place.x], place.to_core)
        self.y_on = relay(5, target.at[place.y, 1], place.to_x)
        self.y_core = relay(6, target.at[place.y], place.to_core)
        self.low_core = relay(7, target.at[place.corner, 0], place.to_core)
        self.high_core = relay(8, target.at[place.corner, 1], place.to_core)
        self.last = (self.own_core, self.x_core, self.y_core, self.low_core, self.high_core)

    def start(self):
        for copy in (self.own_x, self.own_y, self.own_core):
            copy.start()

    def pass_on(self):
        self.own_x.wait_recv()
        self.x_on.start()
        self.x_core.start()
        self.own_y.wait_recv()
        self.y_on.start()
        self.y_core.start()

    def share(self):
        self.x_on.wait_recv()
        self.low_core.start()
        self.y_on.wait_recv()
        self.high_core.start()

    def finish(self):
        for copy in self.last:
            copy.wait_recv()
        for copy in self.last + (self.own_x, self.own_y, self.x_on, self.y_on):
            copy.wait_send()


def add_up(target, *terms):
    rows, columns = target.shape
    strip = max(16, 16384 // columns // 16 * 16)
    strip = min(strip, rows)

    def body(j, carry):
        part = pl.ds(pl.multiple_of(j * strip, strip), strip)
        total = terms[0][part, :].astype(F32)
        for term in terms[1:]:
            total += term[part, :].astype(F32)
        target[part, :] = total.astype(target.dtype)
        return carry

    lax.fori_loop(0, rows // strip, body, 0)


class Fold:
    def __init__(self, place, source, mine, got, bend, from_x, from_y, sent, arrived, loaded):
        def copy(path, piece, spot, partner):
            return send_to(piece, spot, sent.at[path], arrived.at[path], partner)

        slots = (place.me, place.x, place.y, place.corner)
        self.loads = [
            pltpu.make_async_copy(source.at[slot], mine.at[i], loaded.at[i])
            for i, slot in enumerate(slots)
        ]
        self.swaps = [
            copy(i, source.at[slot + place.swap], got.at[i], place.to_core)
            for i, slot in enumerate(slots)
        ]
        self.bend_y = copy(4, mine.at[3, 0], bend.at[0], place.to_y)
        self.bend_x = copy(5, mine.at[3, 1], bend.at[1], place.to_x)
        self.early_x = copy(6, mine.at[1, 1], from_x.at[1], place.to_x)
        self.early_y = copy(7, mine.at[2, 0], from_y.at[0], place.to_y)
        self.late_x = copy(8, mine.at[1, 0], from_x.at[0], place.to_x)
        self.late_y = copy(9, mine.at[2, 1], from_y.at[1], place.to_y)
        self.mine, self.got, self.bend = mine, got, bend
        self.from_x, self.from_y = from_x, from_y

    def start(self):
        for i in (3, 1, 2, 0):
            self.swaps[i].start()
            self.loads[i].start()

    def join(self, i):
        self.loads[i].wait()
        self.swaps[i].wait_recv()
        for half in range(2):
            mine = self.mine.at[i, half]
            add_up(mine, mine, self.got.at[i, half])

    def outward(self):
        self.join(3)
        self.bend_y.start()
        self.bend_x.start()
        self.join(1)
        self.early_x.start()
        self.join(2)
        self.early_y.start()

    def inward(self):
        self.bend_y.wait_recv()
        mine = self.mine.at[1, 0]
        add_up(mine, mine, self.bend.at[0])
        self.late_x.start()
        self.bend_x.wait_recv()
        mine = self.mine.at[2, 1]
        add_up(mine, mine, self.bend.at[1])
        self.late_y.start()

    def total(self, target, *more):
        self.loads[0].wait()
        self.swaps[0].wait_recv()
        for copy in (self.early_x, self.early_y, self.late_x, self.late_y):
            copy.wait_recv()
        for half in range(2):
            terms = [self.mine.at[0, half], self.got.at[0, half]]
            terms += [self.from_x.at[half], self.from_y.at[half]]
            add_up(target.at[half], *terms, *[term.at[half] for term in more])

    def finish(self):
        for copy in self.swaps:
            copy.wait_send()
        for copy in (self.bend_y, self.bend_x, self.early_x, self.early_y):
            copy.wait_send()
        self.late_x.wait_send()
        self.late_y.wait_send()


def fold_scratch(half):
    return [
        pltpu.VMEM((4, 2, *half), BF),
        pltpu.VMEM((4, 2, *half), BF),
        pltpu.VMEM((2, *half), BF),
        pltpu.VMEM((2, *half), BF),
        pltpu.VMEM((2, *half), BF),
        pltpu.SemaphoreType.DMA((PATHS,)),
        pltpu.SemaphoreType.DMA((PATHS,)),
        pltpu.SemaphoreType.DMA((4,)),
    ]


def comm_params(number):
    return pltpu.CompilerParams(
        collective_id=number, has_side_effects=True, vmem_limit_bytes=VMEM_LIMIT
    )


def front_kernel(
    experts,
    tokens,
    cotangent,
    routes,
    triple,
    merge,
    rest,
    up_shard,
    down_shard,
    token_rows,
    upstream,
    packed,
    qkv,
    mixed,
    hidden,
    normed,
    probs,
    up_full,
    down_full,
    rows_full,
    upstream_full,
    gates_full,
    shard,
    up,
    down,
    gates,
    first,
    small,
    sent,
    arrived,
    z_sent,
    z_arrived,
    kept,
):
    real, width = tokens.shape
    count = token_rows.shape[0]
    crossing = ceil_to(real, 16)
    place = Place()
    place.meet([place.to_x, place.to_y, place.to_core, place.to_twin, place.to_far])
    for half in range(2):
        part = slice(half * triple.shape[0] // 2, (half + 1) * triple.shape[0] // 2)
        shard[half, :, : 3 * width] = triple[part, :].astype(BF)
        shard[half, :, 3 * width : 4 * width] = merge[part, :].astype(BF)
        shard[half, :, 4 * width :] = rest[part, :].astype(BF)
    spread = Spread(place, shard, packed, sent.at[0], arrived.at[0])
    spread.start()
    keeps = [pltpu.make_async_copy(shard, packed.at[place.me], kept.at[0])]
    keeps[0].start()

    for half in range(2):
        add_up(up.at[half], up_shard.at[half])
        add_up(down.at[half], down_shard.at[half])
    twins, near, far = [], [], []
    for i, (source, full) in enumerate(((up, up_full), (down, down_full))):
        spot = full.at[1, place.me]
        twins.append(send_to(source, spot, z_sent.at[i], z_arrived.at[i], place.to_twin))
        near.append(Spread(place, source, full.at[0], sent.at[1 + i], arrived.at[1 + i]))
        far.append(Spread(place, spot, full.at[1], sent.at[3 + i], arrived.at[3 + i]))
        keeps.append(pltpu.make_async_copy(source, full.at[0, place.me], kept.at[1 + i]))
    for copy in twins:
        copy.start()
    pad_rows(cotangent, upstream)
    across = []

    def cross(source, full, whole):
        at = 2 + len(across)
        count = source.shape[0] if whole else crossing
        part = source.at[pl.ds(0, count)]
        target = full.at[1, pl.ds(0, count)]
        across.append(send_to(part, target, z_sent.at[at], z_arrived.at[at], place.to_far))
        across[-1].start()
        keeps.append(pltpu.make_async_copy(source, full.at[0], kept.at[len(keeps)]))
        keeps[-1].start()
        if not whole:
            left = pl.ds(crossing, source.shape[0] - crossing)
            copy = pltpu.make_async_copy(source.at[left], full.at[1, left], kept.at[len(keeps)])
            copy.start()
            keeps.append(copy)

    cross_first = len(keeps)
    for copy in keeps[1:cross_first]:
        copy.start()
    cross(upstream, upstream_full, False)
    pad_rows(tokens, token_rows)
    spread.pass_on()
    for other in near:
        other.start()
    spread.share()
    keeps[0].wait()
    spread.finish()

    attend_kernel(
        experts, token_rows, routes, packed, qkv, mixed, hidden, normed, probs, gates, first, small
    )
    cross(normed, rows_full, False)
    cross(gates, gates_full, True)
    for i in range(2):
        near[i].pass_on()
        twins[i].wait_recv()
        far[i].start()
    for i in range(2):
        near[i].share()
        far[i].pass_on()
    for i in range(2):
        far[i].share()
    for other in near + far:
        other.finish()
    for copy in twins:
        copy.wait_send()
    for copy in across + keeps[1:]:
        copy.wait()


def pad_rows(source, target):
    real, width = source.shape
    whole = real // STRIP * STRIP

    def body(j, carry):
        part = pl.ds(pl.multiple_of(j * STRIP, STRIP), STRIP)
        target[part, :] = source[part, :]
        return carry

    lax.fori_loop(0, whole // STRIP, body, 0)
    if whole < target.shape[0]:
        target[whole:, :] = jnp.zeros((target.shape[0] - whole, width), target.dtype)
    if whole < real:
        target[whole:real, :] = source[whole:real, :]


def front(tokens, cotangent, routes, triple, merge, rest, up, down, experts):
    real, width = tokens.shape
    rows = routes.shape[1]
    shape = jax.ShapeDtypeStruct
    columns = 4 * width + LANES
    half = triple.shape[0] // 2
    return pl.pallas_call(
        partial(front_kernel, experts),
        out_shape=(
            shape((rows, width), BF),
            shape((rows, width), BF),
            shape((8, 2, half, columns), BF),
            shape((rows, 3 * width), BF),
            shape((rows, width), BF),
            shape((rows, width), F32),
            shape((rows, width), BF),
            shape((experts, rows), F32),
            shape((2, 8, *up.shape), BF),
            shape((2, 8, *down.shape), BF),
            shape((2, rows, width), BF),
            shape((2, rows, width), BF),
            shape((2, experts, rows), F32),
        ),
        in_specs=[VMEM] * 8,
        out_specs=[VMEM] * 8 + [ANY] * 5,
        scratch_shapes=[
            pltpu.VMEM((2, half, columns), BF),
            pltpu.VMEM(up.shape, BF),
            pltpu.VMEM(down.shape, BF),
            pltpu.VMEM((experts, rows), F32),
            pltpu.VMEM((rows, width), BF),
            pltpu.VMEM((LANES, width), F32),
            pltpu.SemaphoreType.DMA((5, PATHS)),
            pltpu.SemaphoreType.DMA((5, PATHS)),
            pltpu.SemaphoreType.DMA((5,)),
            pltpu.SemaphoreType.DMA((5,)),
            pltpu.SemaphoreType.DMA((8,)),
        ],
        compiler_params=comm_params(1),
        name="front",
    )(tokens, cotangent, routes, triple, merge, rest, up, down)


def back_kernel(
    experts,
    tokens,
    cotangent,
    hidden,
    normed,
    qkv,
    mixed,
    probs,
    packed,
    gates,
    rows,
    mixture,
    up,
    down,
    block_out,
    token_grad,
    triple_total,
    merge_total,
    small_total,
    up_total,
    down_total,
    gates_far,
    rows_near,
    rows_far,
    mixture_near,
    mixture_far,
    change,
    first,
    hidden_grad,
    branch_grad,
    joined_grad,
    small,
    sums,
    totals,
    grads,
    grads_low,
    grads_twin,
    grads_middle,
    grads_far,
    up_low,
    down_low,
    up_far,
    down_far,
    z_sent,
    z_arrived,
    loaded,
    *buffers,
):
    real, width = token_grad.shape
    count = tokens.shape[0]
    crossing = ceil_to(real, 16)
    place = Place()
    place.meet([place.to_x, place.to_y, place.to_core, place.to_twin, place.to_far])
    near, far = pl.ds(0, crossing), pl.ds(count, crossing)
    pairs = (
        (rows.at[far], rows_far.at[near]),
        (gates.at[:, pl.ds(count, count)], gates_far),
        (mixture.at[far], mixture_far),
    )
    across = [
        send_to(source, target, z_sent.at[i], z_arrived.at[i], place.to_far)
        for i, (source, target) in enumerate(pairs)
    ]
    for copy in across:
        copy.start()
    sources = (up.at[1], down.at[1], up.at[0], down.at[0], grads)
    folds = [
        Fold(place, source, *buffers[8 * i : 8 * i + 8]) for i, source in enumerate(sources)
    ]
    twins = [
        send_to(low, other, z_sent.at[3 + i], z_arrived.at[3 + i], place.to_twin)
        for i, (low, other) in enumerate(
            ((up_low, up_far), (down_low, down_far), (grads_low, grads_twin))
        )
    ]
    last = send_to(grads_middle, grads_far, z_sent.at[6], z_arrived.at[6], place.to_far)
    for fold in folds[:4]:
        fold.start()
    loads = (
        pltpu.make_async_copy(rows.at[pl.ds(0, count)], rows_near, loaded.at[0]),
        pltpu.make_async_copy(mixture.at[near], mixture_near, loaded.at[1]),
    )
    for copy in loads:
        copy.start()
    rows_far[crossing:, :] = jnp.zeros((count - crossing, width), BF)
    folds[0].outward()
    folds[1].outward()
    folds[0].inward()
    folds[2].outward()
    folds[3].outward()

    across[1].wait_recv()
    z = lax.axis_index("expert")
    own = [gates[at : at + 2, :count] for at in (0, 2)]
    other = [gates_far[at : at + 2, :] for at in (0, 2)]
    odd = jnp.full((2, count), z % 2, jnp.int32) == 1
    upper = jnp.full((2, count), z // 2, jnp.int32) == 1
    for pair in (own, other):
        pair[:] = [jnp.where(odd, pair[1], pair[0]), jnp.where(odd, pair[0], pair[1])]
    for i in range(2):
        change[2 * i : 2 * i + 2, :] = jnp.where(upper, other[i], own[i])
        change[4 + 2 * i : 6 + 2 * i, :] = jnp.where(upper, own[i], other[i])
    loads[0].wait()
    across[0].wait_recv()

    def middle_step():
        folds[2].inward()
        folds[0].total(up_low)
        twins[0].start()

    def late_step():
        folds[3].inward()
        folds[1].total(down_low)
        twins[1].start()

    retreat_kernel(
        experts,
        (folds[1].inward, middle_step, late_step),
        tokens,
        cotangent,
        hidden,
        normed,
        qkv,
        mixed,
        probs,
        change,
        packed,
        rows_near,
        rows_far,
        token_grad,
        grads,
        first,
        hidden_grad,
        branch_grad,
        joined_grad,
        small,
        sums,
        totals,
    )
    tail = folds[4]
    tail.start()
    tail.outward()
    tail.inward()
    tail.total(grads_low)
    twins[2].start()

    loads[1].wait()
    across[2].wait_recv()

    def output(start, size):
        part = pl.ds(start, size)
        total = hidden[part, :] + mixture_near[part, :].astype(F32)
        return (total + mixture_far[part, :].astype(F32)).astype(BF)

    def output_loop(j, carry):
        start = pl.multiple_of(j * STRIP, STRIP)
        block_out[pl.ds(start, STRIP), :] = output(start, STRIP)
        return carry

    lax.fori_loop(0, real // STRIP, output_loop, 0)
    done = real // STRIP * STRIP
    if done < real:
        block_out[done:real, :] = output(done, crossing - done)[: real - done]

    twins[2].wait_recv()
    for half in range(2):
        add_up(grads_middle.at[half], grads_low.at[half], grads_twin.at[half])
    last.start()
    twins[0].wait_recv()
    folds[2].total(up_total, up_far)
    twins[1].wait_recv()
    folds[3].total(down_total, down_far)
    last.wait_recv()
    size = triple_total.shape[0] // 2
    for half in range(2):
        part = slice(half * size, half * size + size)
        total = grads_middle[half].astype(F32) + grads_far[half].astype(F32)
        triple_total[part, :] = total[:, : 3 * width]
        merge_total[part, :] = total[:, 3 * width : 4 * width]
        small_total[part, :] = total[:, 4 * width :]
    for fold in folds:
        fold.finish()
    for copy in across + twins + [last]:
        copy.wait_send()


def back(
    tokens, cotangent, hidden, normed, qkv, mixed, probs, packed, gates, rows, mixture, up, down, real
):
    count, width = tokens.shape
    experts = probs.shape[0]
    shape = jax.ShapeDtypeStruct
    halves = [up.shape[3:], down.shape[3:]] * 2 + [packed.shape[2:]]
    size = 2 * packed.shape[2]
    crossing = ceil_to(real, 16)
    scratch = [pltpu.VMEM((8, count), F32)]
    scratch += [pltpu.VMEM((count, width), BF)] * 2
    scratch += [pltpu.VMEM((crossing, width), BF)] * 2
    scratch += [
        pltpu.VMEM((experts, count), F32),
        pltpu.VMEM((count, width), BF),
        pltpu.VMEM((count, width), F32),
        pltpu.VMEM((count, width), BF),
        pltpu.VMEM((count, 3 * width), BF),
        pltpu.VMEM((LANES, width), F32),
        pltpu.VMEM((LANES, width), F32),
        pltpu.VMEM((4, 8, width), F32),
        pltpu.VMEM(packed.shape, BF),
    ]
    scratch += [pltpu.VMEM(packed.shape[1:], BF)] * 4
    scratch += [pltpu.VMEM((2, *half), BF) for half in halves[:4]]
    scratch += [pltpu.SemaphoreType.DMA((7,))] * 2 + [pltpu.SemaphoreType.DMA((2,))]
    for half in halves:
        scratch += fold_scratch(half)
    return pl.pallas_call(
        partial(back_kernel, experts),
        out_shape=(
            shape((real, width), BF),
            shape((real, width), F32),
            shape((size, 3 * width), F32),
            shape((size, width), F32),
            shape((size, LANES), F32),
            shape(up.shape[2:], F32),
            shape(down.shape[2:], F32),
        ),
        in_specs=[VMEM] * 9 + [ANY] * 4,
        out_specs=[VMEM] * 7,
        scratch_shapes=scratch,
        compiler_params=comm_params(3),
        name="back",
    )(tokens, cotangent, hidden, normed, qkv, mixed, probs, packed, gates, rows, mixture, up, down)


def pack(triple, merge, router, gain_one, bias_one, gain_two, bias_two):
    rest = pack_small(router, gain_one, bias_one, gain_two, bias_two)
    return jnp.concatenate([triple, merge, rest], 1).astype(BF)


def pack_small(router, *vectors):
    total = jnp.pad(router, ((0, 0), (0, LANES - router.shape[1])))
    for i, vector in enumerate(vectors):
        at = router.shape[1] + i
        total += jnp.pad(vector[:, None], ((0, 0), (at, LANES - at - 1)))
    return total


def unpack(grads, width, experts):
    rest = grads[:, 4 * width :]
    return (
        rest[:, experts],
        rest[:, experts + 1],
        grads[:, : 3 * width],
        grads[:, 3 * width : 4 * width],
        rest[:, experts + 2],
        rest[:, experts + 3],
        rest[:, :experts],
    )


def local_any(
    tokens,
    routes,
    cotangent,
    attend_gain,
    attend_bias,
    triple_weight,
    merge_weight,
    mixture_gain,
    mixture_bias,
    router_weight,
    expert_up,
    expert_down,
):
    real, width = tokens.shape
    experts = router_weight.shape[1]
    owners = lax.axis_size("expert")
    capacity = 2 * TOP * real // experts
    padded = ceil_to(real, STRIP)
    here = lax.axis_index("expert")

    packed = pack(
        triple_weight,
        merge_weight,
        router_weight,
        attend_gain,
        attend_bias,
        mixture_gain,
        mixture_bias,
    )
    packed = lax.all_gather(packed, "fsdp", axis=0, tiled=True)
    packed = packed.reshape(-1, 2, STRIP // 2, packed.shape[1])
    up_full = lax.all_gather(expert_up.astype(BF), "fsdp", axis=0)
    down_full = lax.all_gather(expert_down.astype(BF), "fsdp", axis=0)

    token_rows = jnp.pad(tokens, ((0, padded - real), (0, 0)))
    upstream = jnp.pad(cotangent, ((0, padded - real), (0, 0)))
    route_rows = jnp.pad(routes.T, ((0, 0), (0, padded - real)), constant_values=-1)
    all_routes = lax.all_gather(route_rows, "expert", axis=0)
    order, meta = plan_rows(all_routes, here * 2 + jnp.arange(2, dtype=jnp.int32))
    tiles = owners * padded // TILE
    all_upstream = lax.all_gather(upstream, "expert", axis=0, tiled=True)

    qkv, mixed, hidden, normed, probs, gates = attend(token_rows, route_rows, packed, experts)
    all_rows = lax.all_gather(normed, "expert", axis=0, tiled=True)
    all_gates = lax.all_gather(gates, "expert", axis=0)
    own_gates = lax.dynamic_slice_in_dim(all_gates, here * 2, 2, 1)
    own_gates = own_gates.transpose(1, 0, 2).reshape(2, tiles, TILE)
    info = table_of(order, own_gates)

    mixture, row_grad, gate_grad, up_grad, down_grad = expert_block(
        meta, info, up_full[None], down_full[None], all_rows, all_upstream, owners * capacity
    )
    gate_grad = gate_grad[:2].reshape(2, owners, padded).transpose(1, 0, 2)
    gate_grad = lax.all_to_all(gate_grad, "expert", 0, 0).reshape(experts, padded)
    row_grad = lax.psum_scatter(
        row_grad.reshape(owners, padded, width), "expert", scatter_dimension=0, tiled=True
    )
    mixture = lax.psum_scatter(
        mixture.reshape(owners, padded, width), "expert", scatter_dimension=0, tiled=True
    )
    block_out = (hidden[:real] + mixture[0, :real].astype(F32)).astype(BF)
    up_grad = lax.psum_scatter(up_grad[0], "fsdp", scatter_dimension=0, tiled=True)
    down_grad = lax.psum_scatter(down_grad[0], "fsdp", scatter_dimension=0, tiled=True)

    token_grad, grads = retreat(
        token_rows,
        upstream,
        hidden,
        normed,
        qkv,
        mixed,
        probs,
        gate_grad,
        tuple(row_grad),
        packed,
        real,
    )
    grads = grads.reshape(width, packed.shape[-1])
    grads = lax.psum_scatter(grads, "fsdp", scatter_dimension=0, tiled=True)
    grads = lax.psum(grads, "expert").astype(F32)
    return (block_out, token_grad) + unpack(grads, width, experts) + (
        up_grad[0].astype(F32),
        down_grad[0].astype(F32),
    )


def swapped(pair, flag, axis):
    return jnp.where(flag, jnp.flip(pair, axis), pair)


def local_square(
    tokens,
    routes,
    cotangent,
    attend_gain,
    attend_bias,
    triple_weight,
    merge_weight,
    mixture_gain,
    mixture_bias,
    router_weight,
    expert_up,
    expert_down,
):
    real, width = tokens.shape
    experts = router_weight.shape[1]
    capacity = 2 * TOP * real // experts
    padded = ceil_to(real, LANES)
    tiles = 2 * padded // TILE
    z = lax.axis_index("expert")
    odd, upper = z % 2 == 1, z >= 2

    route_rows = jnp.pad(routes.T, ((0, 0), (0, padded - real)), constant_values=-1)
    far_routes = lax.ppermute(route_rows, "expert", [(i, (i + 2) % 4) for i in range(4)])
    mine = jnp.arange(2, dtype=jnp.int32)
    mine = jnp.concatenate([2 * z + mine, 2 * (z + 1 - 2 * (z % 2)) + mine])
    order, meta = plan_rows(jnp.stack([route_rows, far_routes]), mine)
    rest = pack_small(router_weight, attend_gain, attend_bias, mixture_gain, mixture_bias)
    (
        token_rows,
        upstream,
        packed,
        qkv,
        mixed,
        hidden,
        normed,
        probs,
        up_full,
        down_full,
        all_rows,
        all_upstream,
        all_gates,
    ) = front(
        tokens,
        cotangent,
        route_rows,
        triple_weight,
        merge_weight,
        rest,
        expert_up,
        expert_down,
        experts,
    )
    own_gates = all_gates.reshape(2, 2, 2, 2, padded)
    own_gates = jnp.where(upper, own_gates[:, 1], own_gates[:, 0])
    own_gates = swapped(own_gates, odd, 1).transpose(1, 2, 0, 3)
    info = table_of(order, own_gates.reshape(4, tiles, TILE))

    mixture, row_grad, gate_grad, up_grad, down_grad = expert_block(
        meta,
        info,
        up_full,
        down_full,
        all_rows.reshape(2 * padded, width),
        all_upstream.reshape(2 * padded, width),
        2 * capacity,
    )
    block_out, token_grad, triple_grad, merge_grad, rest, up_grad, down_grad = back(
        token_rows,
        upstream,
        hidden,
        normed,
        qkv,
        mixed,
        probs,
        packed,
        gate_grad,
        row_grad,
        mixture,
        up_grad,
        down_grad,
        real,
    )
    return (
        block_out,
        token_grad,
        rest[:, experts],
        rest[:, experts + 1],
        triple_grad,
        merge_grad,
        rest[:, experts + 2],
        rest[:, experts + 3],
        rest[:, :experts],
        up_grad,
        down_grad,
    )


def solution(mesh):
    square = dict(mesh.shape) == {"expert": 4, "fsdp": 8}
    return jax.shard_map(
        local_square if square else local_any,
        mesh=mesh,
        in_specs=(
            P(("expert", "fsdp"), None),
            P(("expert", "fsdp"), None),
            P(("expert", "fsdp"), None),
            P("fsdp"),
            P("fsdp"),
            P("fsdp", None),
            P("fsdp", None),
            P("fsdp"),
            P("fsdp"),
            P("fsdp", None),
            P("expert", "fsdp", None),
            P("expert", "fsdp", None),
        ),
        out_specs=(
            P(("expert", "fsdp"), None),
            P(("expert", "fsdp"), None),
            P("fsdp"),
            P("fsdp"),
            P("fsdp", None),
            P("fsdp", None),
            P("fsdp"),
            P("fsdp"),
            P("fsdp", None),
            P("expert", "fsdp", None),
            P("expert", "fsdp", None),
        ),
        check_vma=False,
    )
```

```python
from functools import partial

import jax
import jax.numpy as jnp
from jax import lax
from jax.experimental import pallas as pl
from jax.experimental.pallas import tpu as pltpu
from jax.sharding import PartitionSpec as P

HEAD_DIM = 64
TOP = 2
SEQ = 197
EPSILON = 1e-06
LANES = 128
TILE = 256
STRIP = 64
SUB = 128
FAR = -1e30
BF = jnp.bfloat16
F32 = jnp.float32
VMEM_LIMIT = 63 * 1024 * 1024

ERFC = (
    0.2820843458175659,
    0.282412052154541,
    0.24283546209335327,
    0.2037508189678192,
    -0.029143672436475754,
    0.2817249596118927,
    -0.49039793014526367,
    0.2861193120479584,
    -0.05938538536429405,
)


def ceil_to(value, unit):
    return -(-value // unit) * unit


def dot_nn(a, b):
    return lax.dot_general(a, b, (((1,), (0,)), ((), ())), preferred_element_type=F32)


def dot_nt(a, b):
    return lax.dot_general(a, b, (((1,), (1,)), ((), ())), preferred_element_type=F32)


def dot_tn(a, b):
    return lax.dot_general(a, b, (((0,), (0,)), ((), ())), preferred_element_type=F32)


def gelu_both(hidden):
    bell = jnp.exp(hidden * hidden * -0.5)
    t = 1.0 / (1.0 + jnp.abs(hidden) * (0.5 * 0.5**0.5))
    series = jnp.full_like(t, ERFC[-1])
    for factor in ERFC[-2::-1]:
        series = series * t + factor
    tail = (0.5 * t) * series * bell
    share = jnp.where(hidden >= 0, 1.0 - tail, tail)
    return hidden * share, share + hidden * bell * 0.3989422804014327


def normalize(values):
    center = values - jnp.mean(values, -1, keepdims=True)
    spread = jnp.mean(center * center, -1, keepdims=True)
    inverse = lax.rsqrt(spread + EPSILON)
    return center * inverse, inverse


def weight(packed, columns):
    part = packed[:, :, :, columns]
    return part.reshape(-1, part.shape[-1])


def set_weight(grads, columns, value):
    spot = grads.shape[:3]
    grads[:, :, :, columns] = value.astype(BF).reshape(*spot, value.shape[1])


def window(image):
    start = image * SEQ // 16 * 16
    offset = image * SEQ - start
    return pl.multiple_of(start, 16), offset


WINDOW = ceil_to(SEQ + 15, 32)


def attend_kernel(
    experts, tokens, routes, packed, qkv, mixed, hidden, normed, probs, gates, first, small
):
    rows, width = tokens.shape
    images = rows // SEQ
    half = rows // 2
    small[...] = weight(packed, slice(4 * width, None)).astype(F32).T
    gain_one, bias_one = small[experts : experts + 1, :], small[experts + 1 : experts + 2, :]
    gain_two, bias_two = small[experts + 2 : experts + 3, :], small[experts + 3 : experts + 4, :]

    def norm_one(j, carry):
        part = pl.ds(pl.multiple_of(j * STRIP, STRIP), STRIP)
        unit, _ = normalize(tokens[part, :].astype(F32))
        first[part, :] = (unit * gain_one + bias_one).astype(BF)
        mixed[part, :] = jnp.zeros((STRIP, width), BF)
        return carry

    lax.fori_loop(0, rows // STRIP, norm_one, 0)
    for third in range(3):
        columns = slice(third * width, (third + 1) * width)

        def project(j, carry):
            part = pl.ds(pl.multiple_of(j * half, 16), half)
            qkv[part, columns] = dot_nn(first[part, :], weight(packed, columns)).astype(BF)
            return carry

        lax.fori_loop(0, 2, project, 0)

    lane = lax.broadcasted_iota(jnp.int32, (1, LANES), 1)
    low = lane < HEAD_DIM
    scale = 1.0 / HEAD_DIM**0.5

    def attend(image, carry):
        start, offset = window(image)
        part = pl.ds(start, WINDOW)
        place = lax.broadcasted_iota(jnp.int32, (WINDOW, 1), 0) - offset
        mine = (place >= 0) & (place < SEQ)
        across = lax.broadcasted_iota(jnp.int32, (1, WINDOW), 1) - offset
        keys_mine = (across >= 0) & (across < SEQ)
        for pair in range(width // LANES):
            at = pair * LANES
            query = qkv[part, at : at + LANES]
            key = qkv[part, width + at : width + at + LANES]
            value = qkv[part, 2 * width + at : 2 * width + at + LANES]
            both = []
            for side in (low, ~low):
                chosen = jnp.where(side, query, jnp.zeros_like(query))
                scores = jnp.where(keys_mine, dot_nt(chosen, key) * scale, FAR)
                top = jnp.max(scores, -1, keepdims=True)
                raised = jnp.exp(scores - top)
                weights = raised * (1.0 / jnp.sum(raised, -1, keepdims=True))
                both.append(dot_nn(weights.astype(BF), value))
            out = jnp.where(low, both[0], both[1]).astype(BF)
            mixed[part, at : at + LANES] = jnp.where(mine, out, mixed[part, at : at + LANES])
        return carry

    lax.fori_loop(0, images, attend, 0)

    def merge(j, carry):
        part = pl.ds(pl.multiple_of(j * half, 16), half)
        hidden[part, :] = dot_nn(mixed[part, :], weight(packed, slice(3 * width, 4 * width)))
        return carry

    lax.fori_loop(0, 2, merge, 0)

    def norm_two(j, carry):
        part = pl.ds(pl.multiple_of(j * STRIP, STRIP), STRIP)
        total = tokens[part, :].astype(F32) + hidden[part, :]
        hidden[part, :] = total
        unit, _ = normalize(total)
        normed[part, :] = (unit * gain_two + bias_two).astype(BF)
        return carry

    lax.fori_loop(0, rows // STRIP, norm_two, 0)
    router = small[0 : max(experts, 16), :].astype(BF)
    logits = dot_nt(router, normed[...])[:experts]
    raised = jnp.exp(logits - jnp.max(logits, 0, keepdims=True))
    share = raised / jnp.sum(raised, 0, keepdims=True)
    probs[...] = share
    ids = lax.broadcasted_iota(jnp.int32, (experts, rows), 0)
    picked = (routes[0:1, :] == ids) | (routes[1:2, :] == ids)
    gates[...] = jnp.where(picked, share, 0.0)


def attend(tokens, routes, packed, experts):
    rows, width = tokens.shape
    shape = jax.ShapeDtypeStruct
    return pl.pallas_call(
        partial(attend_kernel, experts),
        out_shape=(
            shape((rows, 3 * width), BF),
            shape((rows, width), BF),
            shape((rows, width), F32),
            shape((rows, width), BF),
            shape((experts, rows), F32),
            shape((experts, rows), F32),
        ),
        in_specs=[pl.BlockSpec(memory_space=pltpu.VMEM)] * 3,
        out_specs=[pl.BlockSpec(memory_space=pltpu.VMEM)] * 6,
        scratch_shapes=[pltpu.VMEM((rows, width), BF), pltpu.VMEM((LANES, width), F32)],
        compiler_params=pltpu.CompilerParams(vmem_limit_bytes=VMEM_LIMIT),
        name="attend",
    )(tokens, routes, packed)


def expert_kernel(
    tiles,
    parts,
    room,
    meta,
    info,
    up,
    down,
    rows,
    upstream,
    mixture,
    row_grad,
    gate_grad,
    up_grad,
    down_grad,
    slot_gate,
    out_sum,
    back_sum,
    packed,
    up_sum,
    down_sum,
):
    width = rows.shape[1]
    step = pl.program_id(0)
    owned = packed.shape[0]
    member = jnp.minimum(step // parts, owned - 1)
    part = step - member * parts
    span = up_sum.shape[1]
    stride = meta.shape[0] // owned

    def windows(tile):
        bases, count = [], 0
        for which in range(owned):
            begin = meta[which * stride + tile]
            end = meta[which * stride + tile + 1]
            bases.append(begin // 16 * 16)
            used = jnp.where(end > begin, (end - bases[-1] + SUB - 1) // SUB, 0)
            count = jnp.maximum(count, used)
        return bases, count

    @pl.when(step == 0)
    def _():
        def clear(j, carry):
            at = pl.ds(pl.multiple_of(j * TILE, TILE), TILE)
            for which in range(owned):
                packed[which, at, :] = jnp.zeros((TILE, packed.shape[2]), BF)
                slot_gate[which, at, :] = jnp.zeros((TILE, LANES), F32)
            return carry

        lax.fori_loop(0, room // TILE, clear, 0)

        def gather(tile, carry):
            bases, count = windows(tile)
            at = pl.ds(pl.multiple_of(tile * TILE, TILE), TILE)
            known = info[tile]

            def place(j, inner):
                spots, chosen = [], []
                for which in range(owned):
                    origin = pl.multiple_of(bases[which] + j * SUB, 16)
                    wanted = lax.broadcasted_iota(jnp.int32, (SUB, 1), 0) + origin
                    hit = known[which : which + 1, :] == wanted.astype(F32)
                    gate = jnp.where(hit, known[owned + which : owned + which + 1, :], 0.0)
                    to = pl.ds(origin, SUB)
                    slot_gate[which, to, :] += jnp.sum(gate, -1, keepdims=True)
                    spots.append(to)
                    chosen.append(jnp.where(hit, 1.0, 0.0).astype(BF))
                chosen = jnp.concatenate(chosen, 0)
                for at_column, source in ((0, rows), (width, upstream)):
                    picked = dot_nn(chosen, source[at, :]).astype(BF)
                    columns = slice(at_column, at_column + width)
                    for which, to in enumerate(spots):
                        packed[which, to, columns] += picked[which * SUB : (which + 1) * SUB]
                return inner

            return lax.fori_loop(0, count, place, carry)

        lax.fori_loop(0, tiles, gather, 0)

    @pl.when(step < owned * parts)
    def _():
        up_part = up[...].reshape(width, span)
        down_part = down[...].reshape(span, width)
        held = (meta[member * stride + tiles] + SUB - 1) // SUB
        chunks = held // 2
        up_sum[...] = jnp.zeros(up_sum.shape, F32)
        down_sum[...] = jnp.zeros(down_sum.shape, F32)

        def chunk(j, carry, size=TILE):
            at = pl.ds(pl.multiple_of(j * TILE, TILE), size)
            source = packed[member, at, :width]
            change = packed[member, at, width : 2 * width].astype(F32)
            gate = slot_gate[member, at, 0:1]
            grads = (change * gate).astype(BF)
            pieces = []
            for start in range(0, span, TILE):
                piece = slice(start, start + TILE)
                active, slope = gelu_both(dot_nn(source, up_part[:, piece]))
                change = dot_nt(grads, down_part[piece])
                pieces.append((active.astype(BF), (change * slope).astype(BF)))
            active, pre_grad = [jnp.concatenate(piece, 1) for piece in zip(*pieces)]
            out = dot_nn(active, down_part)
            back = dot_nt(pre_grad, up_part)

            @pl.when(part == 0)
            def _():
                out_sum[at, :] = out
                back_sum[at, :] = back

            @pl.when((part > 0) & (part < parts - 1))
            def _():
                out_sum[at, :] += out
                back_sum[at, :] += back

            @pl.when(part == parts - 1)
            def _():
                total = (out_sum[at, :] + out).astype(BF).astype(F32)
                change = packed[member, at, width : 2 * width].astype(F32)
                dots = jnp.sum(total * change, -1, keepdims=True)
                packed[member, at, :width] = (total * gate).astype(BF)
                packed[member, at, width : 2 * width] = (back_sum[at, :] + back).astype(BF)
                high = dots.astype(BF).astype(F32)
                lane = lax.broadcasted_iota(jnp.int32, (1, LANES), 1)
                both = jnp.where(lane == member, high, 0.0)
                both += jnp.where(lane == member + owned, dots - high, 0.0)
                packed[member, at, 2 * width :] = both.astype(BF)

            down_sum[...] += dot_tn(active, grads)
            up_sum[...] += dot_tn(source, pre_grad)
            return carry

        lax.fori_loop(0, chunks, chunk, 0)

        @pl.when(held % 2 == 1)
        def _():
            chunk(chunks, 0, SUB)

        up_grad[...] = up_sum[...].astype(BF).reshape(up_grad.shape)
        down_grad[...] = down_sum[...].astype(BF).reshape(down_grad.shape)

    @pl.when(step >= owned * parts)
    def _():
        tile = step - owned * parts
        bases, count = windows(tile)
        columns = info[tile].T

        def fetch(j, total):
            chosen, source = [], []
            for which in range(owned):
                origin = pl.multiple_of(bases[which] + j * SUB, 16)
                wanted = lax.broadcasted_iota(jnp.int32, (1, SUB), 1) + origin
                hit = columns[:, which : which + 1] == wanted.astype(F32)
                chosen.append(jnp.where(hit, 1.0, 0.0).astype(BF))
                source.append(packed[which, pl.ds(origin, SUB), :])
            return total + dot_nn(jnp.concatenate(chosen, 1), jnp.concatenate(source, 0))

        total = lax.fori_loop(0, count, fetch, jnp.zeros((TILE, packed.shape[2]), F32))
        mixture[...] = total[:, :width].astype(BF)
        row_grad[...] = total[:, width : 2 * width].astype(BF)
        dots = total[:, 2 * width :].T
        dots = dots[:owned] + dots[owned : 2 * owned]
        gate_grad[...] = jnp.zeros(gate_grad.shape, F32)
        gate_grad[:owned, :] = dots


def expert_block(meta, info, up, down, rows, upstream, most):
    groups, shards, members, rows_up, hidden_units = up.shape
    rows_down = down.shape[3]
    owned = groups * members
    count, width = rows.shape
    tiles = count // TILE
    parts = hidden_units // (1024 if count <= 4096 else 512)
    span = hidden_units // parts
    held = ceil_to(most, TILE)
    room = ceil_to(most + 3 * SUB, TILE)
    shape = jax.ShapeDtypeStruct
    last = owned * parts - 1

    def member_of(i):
        return jnp.minimum(i, last) // parts

    def part_of(i):
        return jnp.minimum(i, last) % parts

    up_spec = pl.BlockSpec(
        (1, shards, 1, rows_up, span),
        lambda i, *_: (member_of(i) // members, 0, member_of(i) % members, 0, part_of(i)),
    )
    down_spec = pl.BlockSpec(
        (1, span // rows_down, 1, rows_down, width),
        lambda i, *_: (member_of(i) // members, part_of(i), member_of(i) % members, 0, 0),
    )
    tile_spec = pl.BlockSpec((TILE, width), lambda i, *_: (jnp.maximum(i - last - 1, 0), 0))
    whole = pl.BlockSpec(memory_space=pltpu.VMEM)
    return pl.pallas_call(
        partial(expert_kernel, tiles, parts, room),
        grid_spec=pltpu.PrefetchScalarGridSpec(
            num_scalar_prefetch=1,
            grid=(owned * parts + tiles,),
            in_specs=[whole, up_spec, down_spec, whole, whole],
            out_specs=[
                tile_spec,
                tile_spec,
                pl.BlockSpec((8, TILE), lambda i, *_: (0, jnp.maximum(i - last - 1, 0))),
                up_spec,
                down_spec,
            ],
            scratch_shapes=[
                pltpu.VMEM((owned, room, LANES), F32),
                pltpu.VMEM((held, width), F32),
                pltpu.VMEM((held, width), F32),
                pltpu.VMEM((owned, room, 2 * width + LANES), BF),
                pltpu.VMEM((width, span), F32),
                pltpu.VMEM((span, width), F32),
            ],
        ),
        out_shape=(
            shape((count, width), BF),
            shape((count, width), BF),
            shape((8, count), F32),
            shape(up.shape, BF),
            shape(down.shape, BF),
        ),
        compiler_params=pltpu.CompilerParams(
            vmem_limit_bytes=VMEM_LIMIT, dimension_semantics=("arbitrary",)
        ),
        name="experts",
    )(meta, info, up, down, rows, upstream)


def retreat_kernel(
    experts,
    steps,
    tokens,
    cotangent,
    hidden,
    normed,
    qkv,
    mixed,
    probs,
    gate_grad,
    packed,
    *rest,
):
    returned, rest = rest[:-9], rest[-9:]
    token_grad, grads, first, hidden_grad, branch_grad, joined_grad, small, sums, totals = rest
    rows, width = tokens.shape
    real = token_grad.shape[0]
    images = rows // SEQ
    half = rows // 2
    small[...] = weight(packed, slice(4 * width, None)).astype(F32).T
    gain_one, bias_one = small[experts : experts + 1, :], small[experts + 1 : experts + 2, :]
    gain_two = small[experts + 2 : experts + 3, :]
    sums[...] = jnp.zeros(sums.shape, F32)
    totals[...] = jnp.zeros(totals.shape, F32)

    share = probs[...]
    change = gate_grad[...]
    tilt = share * (change - jnp.sum(share * change, 0, keepdims=True))
    if experts < 16:
        tilt = jnp.concatenate([tilt, jnp.zeros((16 - experts, rows), F32)], 0)
    tilt = tilt.astype(BF)
    router = small[0 : tilt.shape[0], :].astype(BF)
    keep = lax.broadcasted_iota(jnp.int32, (tilt.shape[0], 1), 0) < experts
    router = jnp.where(keep, router, jnp.zeros_like(router))
    sums[0 : tilt.shape[0], :] = dot_nn(tilt, normed[...])
    hidden_grad[...] = dot_tn(tilt, router)

    def norm_two(j, carry):
        part = pl.ds(pl.multiple_of(j * STRIP, STRIP), STRIP)
        change = hidden_grad[part, :]
        for arrived in returned:
            change += arrived[part, :].astype(F32)
        unit, inverse = normalize(hidden[part, :])
        tail = change * unit
        totals[0] += jnp.sum(tail.reshape(STRIP // 8, 8, width), 0)
        totals[1] += jnp.sum(change.reshape(STRIP // 8, 8, width), 0)
        change = change * gain_two
        mean = jnp.mean(change, -1, keepdims=True)
        lean = jnp.mean(change * unit, -1, keepdims=True)
        total = cotangent[part, :].astype(F32) + inverse * (change - mean - unit * lean)
        hidden_grad[part, :] = total
        branch_grad[part, :] = total.astype(BF)
        unit, _ = normalize(tokens[part, :].astype(F32))
        first[part, :] = (unit * gain_one + bias_one).astype(BF)
        joined_grad[part, :] = jnp.zeros((STRIP, 3 * width), BF)
        return carry

    lax.fori_loop(0, rows // STRIP, norm_two, 0)
    merge = slice(3 * width, 4 * width)
    set_weight(grads, merge, dot_tn(mixed[...], branch_grad[...]))

    def project(j, carry):
        part = pl.ds(pl.multiple_of(j * half, 16), half)
        branch_grad[part, :] = dot_nt(branch_grad[part, :], weight(packed, merge)).astype(BF)
        return carry

    lax.fori_loop(0, 2, project, 0)
    steps[0]()

    lane = lax.broadcasted_iota(jnp.int32, (1, LANES), 1)
    low = lane < HEAD_DIM
    scale = 1.0 / HEAD_DIM**0.5

    def attend(image, carry):
        start, offset = window(image)
        part = pl.ds(start, WINDOW)
        place = lax.broadcasted_iota(jnp.int32, (WINDOW, 1), 0) - offset
        mine = (place >= 0) & (place < SEQ)
        for pair in range(width // LANES):
            at = pair * LANES
            query = qkv[part, at : at + LANES]
            key = qkv[part, width + at : width + at + LANES]
            value = qkv[part, 2 * width + at : 2 * width + at + LANES]
            change = branch_grad[part, at : at + LANES]
            change = jnp.where(mine, change, jnp.zeros_like(change))
            sides = []
            for side in (low, ~low):
                chosen = jnp.where(side, query, jnp.zeros_like(query))
                scores = jnp.where(mine, dot_nt(key, chosen) * scale, FAR)
                raised = jnp.exp(scores - jnp.max(scores, 0, keepdims=True))
                weights = raised * (1.0 / jnp.sum(raised, 0, keepdims=True))
                slope = dot_nt(value, jnp.where(side, change, jnp.zeros_like(change)))
                lean = jnp.sum(weights * slope, 0, keepdims=True)
                slope = (weights * (slope - lean)).astype(BF)
                sides.append(
                    (
                        dot_tn(slope, key) * scale,
                        dot_nn(slope, query) * scale,
                        dot_nn(weights.astype(BF), change),
                    )
                )
            for third in range(3):
                to = third * width + at
                joined_grad[part, to : to + LANES] += jnp.where(
                    low, sides[0][third], sides[1][third]
                ).astype(BF)
        return carry

    lax.fori_loop(0, images, attend, 0)
    steps[1]()
    for third in range(3):
        columns = slice(third * width, (third + 1) * width)
        set_weight(grads, columns, dot_tn(first[...], joined_grad[:, columns]))
    steps[2]()

    def finish(start, size):
        part = pl.ds(start, size)
        change = dot_nt(joined_grad[part, :], weight(packed, slice(0, 3 * width)))
        unit, inverse = normalize(tokens[part, :].astype(F32))
        tail = change * unit
        totals[2] += jnp.sum(tail.reshape(size // 8, 8, width), 0)
        totals[3] += jnp.sum(change.reshape(size // 8, 8, width), 0)
        change = change * gain_one
        mean = jnp.mean(change, -1, keepdims=True)
        lean = jnp.mean(change * unit, -1, keepdims=True)
        return hidden_grad[part, :] + inverse * (change - mean - unit * lean)

    block = 2 * STRIP

    def finish_loop(j, carry):
        start = pl.multiple_of(j * block, block)
        token_grad[pl.ds(start, block), :] = finish(start, block)
        return carry

    lax.fori_loop(0, real // block, finish_loop, 0)
    done = real // block * block
    if done < real:
        token_grad[done:real, :] = finish(done, ceil_to(real - done, 16))[: real - done]
    for which, row in ((2, experts), (3, experts + 1), (0, experts + 2), (1, experts + 3)):
        sums[row : row + 1, :] = jnp.sum(totals[which], 0, keepdims=True)
    set_weight(grads, slice(4 * width, None), sums[...].T)


def retreat(
    tokens, cotangent, hidden, normed, qkv, mixed, probs, gate_grad, returned, packed, real
):
    rows, width = tokens.shape
    experts = probs.shape[0]
    shape = jax.ShapeDtypeStruct
    return pl.pallas_call(
        partial(retreat_kernel, experts, (lambda: None,) * 3),
        out_shape=(shape((real, width), F32), shape(packed.shape, BF)),
        in_specs=[pl.BlockSpec(memory_space=pltpu.VMEM)] * (9 + len(returned)),
        out_specs=[pl.BlockSpec(memory_space=pltpu.VMEM)] * 2,
        scratch_shapes=[
            pltpu.VMEM((rows, width), BF),
            pltpu.VMEM((rows, width), F32),
            pltpu.VMEM((rows, width), BF),
            pltpu.VMEM((rows, 3 * width), BF),
            pltpu.VMEM((LANES, width), F32),
            pltpu.VMEM((LANES, width), F32),
            pltpu.VMEM((4, 8, width), F32),
        ],
        compiler_params=pltpu.CompilerParams(vmem_limit_bytes=VMEM_LIMIT),
        name="retreat",
    )(tokens, cotangent, hidden, normed, qkv, mixed, probs, gate_grad, packed, *returned)


def plan_rows(routes, mine):
    owned = mine.shape[0]
    tiles = routes.shape[0] * routes.shape[2] // TILE
    mine = mine[:, None, None]
    chosen = (routes[None, :, 0] == mine) | (routes[None, :, 1] == mine)
    chosen = chosen.reshape(owned, tiles, TILE)
    flags = chosen.astype(BF)
    upper = jnp.triu(jnp.ones((TILE, TILE), BF))
    within = jnp.dot(flags.reshape(owned * tiles, TILE), upper, preferred_element_type=F32)
    within = within.reshape(owned, tiles, TILE)
    counts = within[:, :, -1]
    below = jnp.tril(jnp.ones((tiles + 1, tiles), F32), -1)
    begins = jnp.sum(below[None] * counts[:, None, :], 2)
    order = jnp.where(chosen, begins[:, :tiles, None] + within - 1.0, -1.0)
    return order, begins.astype(jnp.int32).reshape(-1)


def table_of(order, gates):
    owned, tiles, _ = order.shape
    parts = [order, gates]
    if 2 * owned < 8:
        parts.append(jnp.zeros((8 - 2 * owned, tiles, TILE), F32))
    return jnp.concatenate(parts, 0).transpose(1, 0, 2)


MESH = pl.DeviceIdType.MESH
ANY = pl.BlockSpec(memory_space=pl.ANY)
VMEM = pl.BlockSpec(memory_space=pltpu.VMEM)
PATHS = 10


class Place:
    def __init__(self):
        z, me = lax.axis_index("expert"), lax.axis_index("fsdp")
        self.me = me
        self.x = me + 2 - 4 * ((me // 2) % 2)
        turn = 4 - 8 * (me // 4)
        self.y = me + turn
        self.corner = self.x + turn
        self.swap = 1 - 2 * (me % 2)
        self.to_x, self.to_y = {"fsdp": self.x}, {"fsdp": self.y}
        self.to_core = {"fsdp": me + self.swap}
        self.to_twin = {"expert": z + 1 - 2 * (z % 2)}
        self.to_far = {"expert": (z + 2) % 4}

    def meet(self, partners):
        barrier = pltpu.get_barrier_semaphore()
        for partner in partners:
            pl.semaphore_signal(barrier, inc=1, device_id=partner, device_id_type=MESH)
        pl.semaphore_wait(barrier, len(partners))


def send_to(source, target, sent, arrived, partner):
    return pltpu.make_async_remote_copy(
        src_ref=source,
        dst_ref=target,
        send_sem=sent,
        recv_sem=arrived,
        device_id=partner,
        device_id_type=MESH,
    )


class Spread:
    def __init__(self, place, source, target, sent, arrived):
        def copy(path, piece, spot, partner):
            return send_to(piece, spot, sent.at[path], arrived.at[path], partner)

        def relay(path, spot, partner):
            return copy(path, spot, spot, partner)

        own = target.at[place.me]
        self.own_x = copy(0, source, own, place.to_x)
        self.own_y = copy(1, source, own, place.to_y)
        self.own_core = copy(2, source, own, place.to_core)
        self.x_on = relay(3, target.at[place.x, 0], place.to_y)
        self.x_core = relay(4, target.at[place.x], place.to_core)
        self.y_on = relay(5, target.at[place.y, 1], place.to_x)
        self.y_core = relay(6, target.at[place.y], place.to_core)
        self.low_core = relay(7, target.at[place.corner, 0], place.to_core)
        self.high_core = relay(8, target.at[place.corner, 1], place.to_core)
        self.last = (self.own_core, self.x_core, self.y_core, self.low_core, self.high_core)

    def start(self):
        for copy in (self.own_x, self.own_y, self.own_core):
            copy.start()

    def pass_on(self):
        self.own_x.wait_recv()
        self.x_on.start()
        self.x_core.start()
        self.own_y.wait_recv()
        self.y_on.start()
        self.y_core.start()

    def share(self):
        self.x_on.wait_recv()
        self.low_core.start()
        self.y_on.wait_recv()
        self.high_core.start()

    def finish(self):
        for copy in self.last:
            copy.wait_recv()
        for copy in self.last + (self.own_x, self.own_y, self.x_on, self.y_on):
            copy.wait_send()


def add_up(target, *terms):
    rows, columns = target.shape
    strip = max(16, 16384 // columns // 16 * 16)
    strip = min(strip, rows)

    def body(j, carry):
        part = pl.ds(pl.multiple_of(j * strip, strip), strip)
        total = terms[0][part, :].astype(F32)
        for term in terms[1:]:
            total += term[part, :].astype(F32)
        target[part, :] = total.astype(target.dtype)
        return carry

    lax.fori_loop(0, rows // strip, body, 0)


class Fold:
    def __init__(self, place, source, mine, got, bend, from_x, from_y, sent, arrived, loaded):
        def copy(path, piece, spot, partner):
            return send_to(piece, spot, sent.at[path], arrived.at[path], partner)

        slots = (place.me, place.x, place.y, place.corner)
        self.loads = [
            pltpu.make_async_copy(source.at[slot], mine.at[i], loaded.at[i])
            for i, slot in enumerate(slots)
        ]
        self.swaps = [
            copy(i, source.at[slot + place.swap], got.at[i], place.to_core)
            for i, slot in enumerate(slots)
        ]
        self.bend_y = copy(4, mine.at[3, 0], bend.at[0], place.to_y)
        self.bend_x = copy(5, mine.at[3, 1], bend.at[1], place.to_x)
        self.early_x = copy(6, mine.at[1, 1], from_x.at[1], place.to_x)
        self.early_y = copy(7, mine.at[2, 0], from_y.at[0], place.to_y)
        self.late_x = copy(8, mine.at[1, 0], from_x.at[0], place.to_x)
        self.late_y = copy(9, mine.at[2, 1], from_y.at[1], place.to_y)
        self.mine, self.got, self.bend = mine, got, bend
        self.from_x, self.from_y = from_x, from_y

    def start(self):
        for i in (3, 1, 2, 0):
            self.swaps[i].start()
            self.loads[i].start()

    def join(self, i):
        self.loads[i].wait()
        self.swaps[i].wait_recv()
        for half in range(2):
            mine = self.mine.at[i, half]
            add_up(mine, mine, self.got.at[i, half])

    def outward(self):
        self.join(3)
        self.bend_y.start()
        self.bend_x.start()
        self.join(1)
        self.early_x.start()
        self.join(2)
        self.early_y.start()

    def inward(self):
        self.bend_y.wait_recv()
        mine = self.mine.at[1, 0]
        add_up(mine, mine, self.bend.at[0])
        self.late_x.start()
        self.bend_x.wait_recv()
        mine = self.mine.at[2, 1]
        add_up(mine, mine, self.bend.at[1])
        self.late_y.start()

    def total(self, target, *more):
        self.loads[0].wait()
        self.swaps[0].wait_recv()
        for copy in (self.early_x, self.early_y, self.late_x, self.late_y):
            copy.wait_recv()
        for half in range(2):
            terms = [self.mine.at[0, half], self.got.at[0, half]]
            terms += [self.from_x.at[half], self.from_y.at[half]]
            add_up(target.at[half], *terms, *[term.at[half] for term in more])

    def finish(self):
        for copy in self.swaps:
            copy.wait_send()
        for copy in (self.bend_y, self.bend_x, self.early_x, self.early_y):
            copy.wait_send()
        self.late_x.wait_send()
        self.late_y.wait_send()


def fold_scratch(half):
    return [
        pltpu.VMEM((4, 2, *half), BF),
        pltpu.VMEM((4, 2, *half), BF),
        pltpu.VMEM((2, *half), BF),
        pltpu.VMEM((2, *half), BF),
        pltpu.VMEM((2, *half), BF),
        pltpu.SemaphoreType.DMA((PATHS,)),
        pltpu.SemaphoreType.DMA((PATHS,)),
        pltpu.SemaphoreType.DMA((4,)),
    ]


def comm_params(number):
    return pltpu.CompilerParams(
        collective_id=number, has_side_effects=True, vmem_limit_bytes=VMEM_LIMIT
    )


def front_kernel(
    experts,
    tokens,
    cotangent,
    routes,
    triple,
    merge,
    rest,
    up_shard,
    down_shard,
    token_rows,
    upstream,
    packed,
    qkv,
    mixed,
    hidden,
    normed,
    probs,
    up_full,
    down_full,
    rows_full,
    upstream_full,
    gates_full,
    shard,
    up,
    down,
    gates,
    first,
    small,
    sent,
    arrived,
    z_sent,
    z_arrived,
    kept,
):
    real, width = tokens.shape
    count = token_rows.shape[0]
    crossing = ceil_to(real, 16)
    place = Place()
    place.meet([place.to_x, place.to_y, place.to_core, place.to_twin, place.to_far])
    for half in range(2):
        part = slice(half * triple.shape[0] // 2, (half + 1) * triple.shape[0] // 2)
        shard[half, :, : 3 * width] = triple[part, :].astype(BF)
        shard[half, :, 3 * width : 4 * width] = merge[part, :].astype(BF)
        shard[half, :, 4 * width :] = rest[part, :].astype(BF)
    spread = Spread(place, shard, packed, sent.at[0], arrived.at[0])
    spread.start()
    keeps = [pltpu.make_async_copy(shard, packed.at[place.me], kept.at[0])]
    keeps[0].start()

    for half in range(2):
        add_up(up.at[half], up_shard.at[half])
        add_up(down.at[half], down_shard.at[half])
    twins, near, far = [], [], []
    for i, (source, full) in enumerate(((up, up_full), (down, down_full))):
        spot = full.at[1, place.me]
        twins.append(send_to(source, spot, z_sent.at[i], z_arrived.at[i], place.to_twin))
        near.append(Spread(place, source, full.at[0], sent.at[1 + i], arrived.at[1 + i]))
        far.append(Spread(place, spot, full.at[1], sent.at[3 + i], arrived.at[3 + i]))
        keeps.append(pltpu.make_async_copy(source, full.at[0, place.me], kept.at[1 + i]))
    for copy in twins:
        copy.start()
    pad_rows(cotangent, upstream)
    across = []

    def cross(source, full, whole):
        at = 2 + len(across)
        count = source.shape[0] if whole else crossing
        part = source.at[pl.ds(0, count)]
        target = full.at[1, pl.ds(0, count)]
        across.append(send_to(part, target, z_sent.at[at], z_arrived.at[at], place.to_far))
        across[-1].start()
        keeps.append(pltpu.make_async_copy(source, full.at[0], kept.at[len(keeps)]))
        keeps[-1].start()
        if not whole:
            left = pl.ds(crossing, source.shape[0] - crossing)
            copy = pltpu.make_async_copy(source.at[left], full.at[1, left], kept.at[len(keeps)])
            copy.start()
            keeps.append(copy)

    cross_first = len(keeps)
    for copy in keeps[1:cross_first]:
        copy.start()
    cross(upstream, upstream_full, False)
    pad_rows(tokens, token_rows)
    spread.pass_on()
    for other in near:
        other.start()
    spread.share()
    keeps[0].wait()
    spread.finish()

    attend_kernel(
        experts, token_rows, routes, packed, qkv, mixed, hidden, normed, probs, gates, first, small
    )
    cross(normed, rows_full, False)
    cross(gates, gates_full, True)
    for i in range(2):
        near[i].pass_on()
        twins[i].wait_recv()
        far[i].start()
    for i in range(2):
        near[i].share()
        far[i].pass_on()
    for i in range(2):
        far[i].share()
    for other in near + far:
        other.finish()
    for copy in twins:
        copy.wait_send()
    for copy in across + keeps[1:]:
        copy.wait()


def pad_rows(source, target):
    real, width = source.shape
    whole = real // STRIP * STRIP

    def body(j, carry):
        part = pl.ds(pl.multiple_of(j * STRIP, STRIP), STRIP)
        target[part, :] = source[part, :]
        return carry

    lax.fori_loop(0, whole // STRIP, body, 0)
    if whole < target.shape[0]:
        target[whole:, :] = jnp.zeros((target.shape[0] - whole, width), target.dtype)
    if whole < real:
        target[whole:real, :] = source[whole:real, :]


def front(tokens, cotangent, routes, triple, merge, rest, up, down, experts):
    real, width = tokens.shape
    rows = routes.shape[1]
    shape = jax.ShapeDtypeStruct
    columns = 4 * width + LANES
    half = triple.shape[0] // 2
    return pl.pallas_call(
        partial(front_kernel, experts),
        out_shape=(
            shape((rows, width), BF),
            shape((rows, width), BF),
            shape((8, 2, half, columns), BF),
            shape((rows, 3 * width), BF),
            shape((rows, width), BF),
            shape((rows, width), F32),
            shape((rows, width), BF),
            shape((experts, rows), F32),
            shape((2, 8, *up.shape), BF),
            shape((2, 8, *down.shape), BF),
            shape((2, rows, width), BF),
            shape((2, rows, width), BF),
            shape((2, experts, rows), F32),
        ),
        in_specs=[VMEM] * 8,
        out_specs=[VMEM] * 8 + [ANY] * 5,
        scratch_shapes=[
            pltpu.VMEM((2, half, columns), BF),
            pltpu.VMEM(up.shape, BF),
            pltpu.VMEM(down.shape, BF),
            pltpu.VMEM((experts, rows), F32),
            pltpu.VMEM((rows, width), BF),
            pltpu.VMEM((LANES, width), F32),
            pltpu.SemaphoreType.DMA((5, PATHS)),
            pltpu.SemaphoreType.DMA((5, PATHS)),
            pltpu.SemaphoreType.DMA((5,)),
            pltpu.SemaphoreType.DMA((5,)),
            pltpu.SemaphoreType.DMA((8,)),
        ],
        compiler_params=comm_params(1),
        name="front",
    )(tokens, cotangent, routes, triple, merge, rest, up, down)


def back_kernel(
    experts,
    tokens,
    cotangent,
    hidden,
    normed,
    qkv,
    mixed,
    probs,
    packed,
    gates,
    rows,
    mixture,
    up,
    down,
    block_out,
    token_grad,
    triple_total,
    merge_total,
    small_total,
    up_total,
    down_total,
    gates_far,
    rows_near,
    rows_far,
    mixture_near,
    mixture_far,
    change,
    first,
    hidden_grad,
    branch_grad,
    joined_grad,
    small,
    sums,
    totals,
    grads,
    grads_low,
    grads_twin,
    grads_middle,
    grads_far,
    up_low,
    down_low,
    up_far,
    down_far,
    z_sent,
    z_arrived,
    loaded,
    *buffers,
):
    real, width = token_grad.shape
    count = tokens.shape[0]
    crossing = ceil_to(real, 16)
    place = Place()
    place.meet([place.to_x, place.to_y, place.to_core, place.to_twin, place.to_far])
    near, far = pl.ds(0, crossing), pl.ds(count, crossing)
    pairs = (
        (rows.at[far], rows_far.at[near]),
        (gates.at[:, pl.ds(count, count)], gates_far),
        (mixture.at[far], mixture_far),
    )
    across = [
        send_to(source, target, z_sent.at[i], z_arrived.at[i], place.to_far)
        for i, (source, target) in enumerate(pairs)
    ]
    for copy in across[:2]:
        copy.start()
    sources = (up.at[1], down.at[1], up.at[0], down.at[0], grads)
    folds = [
        Fold(place, source, *buffers[8 * i : 8 * i + 8]) for i, source in enumerate(sources)
    ]
    twins = [
        send_to(low, other, z_sent.at[4 + i], z_arrived.at[4 + i], place.to_twin)
        for i, (low, other) in enumerate(
            ((up_low, up_far), (down_low, down_far), (grads_low, grads_twin))
        )
    ]
    last = send_to(grads_middle, grads_far, z_sent.at[7], z_arrived.at[7], place.to_far)
    for fold in folds[:4]:
        fold.start()
    loads = (
        pltpu.make_async_copy(rows.at[pl.ds(0, count)], rows_near, loaded.at[0]),
        pltpu.make_async_copy(mixture.at[near], mixture_near, loaded.at[1]),
    )
    for copy in loads:
        copy.start()
    rows_far[crossing:, :] = jnp.zeros((count - crossing, width), BF)
    folds[0].outward()
    folds[1].outward()
    folds[0].inward()
    folds[1].inward()
    folds[2].outward()
    folds[3].outward()

    across[1].wait_recv()
    z = lax.axis_index("expert")
    own = [gates[at : at + 2, :count] for at in (0, 2)]
    other = [gates_far[at : at + 2, :] for at in (0, 2)]
    odd = jnp.full((2, count), z % 2, jnp.int32) == 1
    upper = jnp.full((2, count), z // 2, jnp.int32) == 1
    for pair in (own, other):
        pair[:] = [jnp.where(odd, pair[1], pair[0]), jnp.where(odd, pair[0], pair[1])]
    for i in range(2):
        change[2 * i : 2 * i + 2, :] = jnp.where(upper, other[i], own[i])
        change[4 + 2 * i : 6 + 2 * i, :] = jnp.where(upper, own[i], other[i])
    loads[0].wait()
    across[0].wait_recv()

    def early_step():
        folds[0].total(up_low)
        twins[0].start()

    def middle_step():
        folds[1].total(down_low)
        twins[1].start()
        across[2].start()
        folds[2].inward()

    retreat_kernel(
        experts,
        (early_step, middle_step, lambda: None),
        tokens,
        cotangent,
        hidden,
        normed,
        qkv,
        mixed,
        probs,
        change,
        packed,
        rows_near,
        rows_far,
        token_grad,
        grads,
        first,
        hidden_grad,
        branch_grad,
        joined_grad,
        small,
        sums,
        totals,
    )
    tail = folds[4]
    tail.start()
    tail.outward()
    tail.inward()
    folds[3].inward()
    tail.total(grads_low)
    twins[2].start()

    twins[2].wait_recv()
    for half in range(2):
        add_up(grads_middle.at[half], grads_low.at[half], grads_twin.at[half])
    last.start()
    twins[0].wait_recv()
    folds[2].total(up_total, up_far)
    loads[1].wait()
    across[2].wait_recv()

    def output(start, size):
        part = pl.ds(start, size)
        total = hidden[part, :] + mixture_near[part, :].astype(F32)
        return (total + mixture_far[part, :].astype(F32)).astype(BF)

    def output_loop(j, carry):
        start = pl.multiple_of(j * STRIP, STRIP)
        block_out[pl.ds(start, STRIP), :] = output(start, STRIP)
        return carry

    lax.fori_loop(0, real // STRIP, output_loop, 0)
    done = real // STRIP * STRIP
    if done < real:
        block_out[done:real, :] = output(done, crossing - done)[: real - done]
    twins[1].wait_recv()
    folds[3].total(down_total, down_far)
    last.wait_recv()
    size = triple_total.shape[0] // 2
    for half in range(2):
        part = slice(half * size, half * size + size)
        total = grads_middle[half].astype(F32) + grads_far[half].astype(F32)
        triple_total[part, :] = total[:, : 3 * width]
        merge_total[part, :] = total[:, 3 * width : 4 * width]
        small_total[part, :] = total[:, 4 * width :]
    for fold in folds:
        fold.finish()
    for copy in across + twins + [last]:
        copy.wait_send()


def back(
    tokens, cotangent, hidden, normed, qkv, mixed, probs, packed, gates, rows, mixture, up, down, real
):
    count, width = tokens.shape
    experts = probs.shape[0]
    shape = jax.ShapeDtypeStruct
    halves = [up.shape[3:], down.shape[3:]] * 2 + [packed.shape[2:]]
    size = 2 * packed.shape[2]
    crossing = ceil_to(real, 16)
    scratch = [pltpu.VMEM((8, count), F32)]
    scratch += [pltpu.VMEM((count, width), BF)] * 2
    scratch += [pltpu.VMEM((crossing, width), BF)] * 2
    scratch += [
        pltpu.VMEM((experts, count), F32),
        pltpu.VMEM((count, width), BF),
        pltpu.VMEM((count, width), F32),
        pltpu.VMEM((count, width), BF),
        pltpu.VMEM((count, 3 * width), BF),
        pltpu.VMEM((LANES, width), F32),
        pltpu.VMEM((LANES, width), F32),
        pltpu.VMEM((4, 8, width), F32),
        pltpu.VMEM(packed.shape, BF),
    ]
    scratch += [pltpu.VMEM(packed.shape[1:], BF)] * 4
    scratch += [pltpu.VMEM((2, *half), BF) for half in halves[:4]]
    scratch += [pltpu.SemaphoreType.DMA((8,))] * 2 + [pltpu.SemaphoreType.DMA((2,))]
    for half in halves:
        scratch += fold_scratch(half)
    return pl.pallas_call(
        partial(back_kernel, experts),
        out_shape=(
            shape((real, width), BF),
            shape((real, width), F32),
            shape((size, 3 * width), F32),
            shape((size, width), F32),
            shape((size, LANES), F32),
            shape(up.shape[2:], F32),
            shape(down.shape[2:], F32),
        ),
        in_specs=[VMEM] * 9 + [ANY] * 4,
        out_specs=[VMEM] * 7,
        scratch_shapes=scratch,
        compiler_params=comm_params(3),
        name="back",
    )(tokens, cotangent, hidden, normed, qkv, mixed, probs, packed, gates, rows, mixture, up, down)


def pack(triple, merge, router, gain_one, bias_one, gain_two, bias_two):
    rest = pack_small(router, gain_one, bias_one, gain_two, bias_two)
    return jnp.concatenate([triple, merge, rest], 1).astype(BF)


def pack_small(router, *vectors):
    total = jnp.pad(router, ((0, 0), (0, LANES - router.shape[1])))
    for i, vector in enumerate(vectors):
        at = router.shape[1] + i
        total += jnp.pad(vector[:, None], ((0, 0), (at, LANES - at - 1)))
    return total


def unpack(grads, width, experts):
    rest = grads[:, 4 * width :]
    return (
        rest[:, experts],
        rest[:, experts + 1],
        grads[:, : 3 * width],
        grads[:, 3 * width : 4 * width],
        rest[:, experts + 2],
        rest[:, experts + 3],
        rest[:, :experts],
    )


def local_any(
    tokens,
    routes,
    cotangent,
    attend_gain,
    attend_bias,
    triple_weight,
    merge_weight,
    mixture_gain,
    mixture_bias,
    router_weight,
    expert_up,
    expert_down,
):
    real, width = tokens.shape
    experts = router_weight.shape[1]
    owners = lax.axis_size("expert")
    capacity = 2 * TOP * real // experts
    padded = ceil_to(real, STRIP)
    here = lax.axis_index("expert")

    packed = pack(
        triple_weight,
        merge_weight,
        router_weight,
        attend_gain,
        attend_bias,
        mixture_gain,
        mixture_bias,
    )
    packed = lax.all_gather(packed, "fsdp", axis=0, tiled=True)
    packed = packed.reshape(-1, 2, STRIP // 2, packed.shape[1])
    up_full = lax.all_gather(expert_up.astype(BF), "fsdp", axis=0)
    down_full = lax.all_gather(expert_down.astype(BF), "fsdp", axis=0)

    token_rows = jnp.pad(tokens, ((0, padded - real), (0, 0)))
    upstream = jnp.pad(cotangent, ((0, padded - real), (0, 0)))
    route_rows = jnp.pad(routes.T, ((0, 0), (0, padded - real)), constant_values=-1)
    all_routes = lax.all_gather(route_rows, "expert", axis=0)
    order, meta = plan_rows(all_routes, here * 2 + jnp.arange(2, dtype=jnp.int32))
    tiles = owners * padded // TILE
    all_upstream = lax.all_gather(upstream, "expert", axis=0, tiled=True)

    qkv, mixed, hidden, normed, probs, gates = attend(token_rows, route_rows, packed, experts)
    all_rows = lax.all_gather(normed, "expert", axis=0, tiled=True)
    all_gates = lax.all_gather(gates, "expert", axis=0)
    own_gates = lax.dynamic_slice_in_dim(all_gates, here * 2, 2, 1)
    own_gates = own_gates.transpose(1, 0, 2).reshape(2, tiles, TILE)
    info = table_of(order, own_gates)

    mixture, row_grad, gate_grad, up_grad, down_grad = expert_block(
        meta, info, up_full[None], down_full[None], all_rows, all_upstream, owners * capacity
    )
    gate_grad = gate_grad[:2].reshape(2, owners, padded).transpose(1, 0, 2)
    gate_grad = lax.all_to_all(gate_grad, "expert", 0, 0).reshape(experts, padded)
    row_grad = lax.psum_scatter(
        row_grad.reshape(owners, padded, width), "expert", scatter_dimension=0, tiled=True
    )
    mixture = lax.psum_scatter(
        mixture.reshape(owners, padded, width), "expert", scatter_dimension=0, tiled=True
    )
    block_out = (hidden[:real] + mixture[0, :real].astype(F32)).astype(BF)
    up_grad = lax.psum_scatter(up_grad[0], "fsdp", scatter_dimension=0, tiled=True)
    down_grad = lax.psum_scatter(down_grad[0], "fsdp", scatter_dimension=0, tiled=True)

    token_grad, grads = retreat(
        token_rows,
        upstream,
        hidden,
        normed,
        qkv,
        mixed,
        probs,
        gate_grad,
        tuple(row_grad),
        packed,
        real,
    )
    grads = grads.reshape(width, packed.shape[-1])
    grads = lax.psum_scatter(grads, "fsdp", scatter_dimension=0, tiled=True)
    grads = lax.psum(grads, "expert").astype(F32)
    return (block_out, token_grad) + unpack(grads, width, experts) + (
        up_grad[0].astype(F32),
        down_grad[0].astype(F32),
    )


def swapped(pair, flag, axis):
    return jnp.where(flag, jnp.flip(pair, axis), pair)


def local_square(
    tokens,
    routes,
    cotangent,
    attend_gain,
    attend_bias,
    triple_weight,
    merge_weight,
    mixture_gain,
    mixture_bias,
    router_weight,
    expert_up,
    expert_down,
):
    real, width = tokens.shape
    experts = router_weight.shape[1]
    capacity = 2 * TOP * real // experts
    padded = ceil_to(real, LANES)
    tiles = 2 * padded // TILE
    z = lax.axis_index("expert")
    odd, upper = z % 2 == 1, z >= 2

    route_rows = jnp.pad(routes.T, ((0, 0), (0, padded - real)), constant_values=-1)
    far_routes = lax.ppermute(route_rows, "expert", [(i, (i + 2) % 4) for i in range(4)])
    mine = jnp.arange(2, dtype=jnp.int32)
    mine = jnp.concatenate([2 * z + mine, 2 * (z + 1 - 2 * (z % 2)) + mine])
    order, meta = plan_rows(jnp.stack([route_rows, far_routes]), mine)
    rest = pack_small(router_weight, attend_gain, attend_bias, mixture_gain, mixture_bias)
    (
        token_rows,
        upstream,
        packed,
        qkv,
        mixed,
        hidden,
        normed,
        probs,
        up_full,
        down_full,
        all_rows,
        all_upstream,
        all_gates,
    ) = front(
        tokens,
        cotangent,
        route_rows,
        triple_weight,
        merge_weight,
        rest,
        expert_up,
        expert_down,
        experts,
    )
    own_gates = all_gates.reshape(2, 2, 2, 2, padded)
    own_gates = jnp.where(upper, own_gates[:, 1], own_gates[:, 0])
    own_gates = swapped(own_gates, odd, 1).transpose(1, 2, 0, 3)
    info = table_of(order, own_gates.reshape(4, tiles, TILE))

    mixture, row_grad, gate_grad, up_grad, down_grad = expert_block(
        meta,
        info,
        up_full,
        down_full,
        all_rows.reshape(2 * padded, width),
        all_upstream.reshape(2 * padded, width),
        2 * capacity,
    )
    block_out, token_grad, triple_grad, merge_grad, rest, up_grad, down_grad = back(
        token_rows,
        upstream,
        hidden,
        normed,
        qkv,
        mixed,
        probs,
        packed,
        gate_grad,
        row_grad,
        mixture,
        up_grad,
        down_grad,
        real,
    )
    return (
        block_out,
        token_grad,
        rest[:, experts],
        rest[:, experts + 1],
        triple_grad,
        merge_grad,
        rest[:, experts + 2],
        rest[:, experts + 3],
        rest[:, :experts],
        up_grad,
        down_grad,
    )


def solution(mesh):
    square = dict(mesh.shape) == {"expert": 4, "fsdp": 8}
    return jax.shard_map(
        local_square if square else local_any,
        mesh=mesh,
        in_specs=(
            P(("expert", "fsdp"), None),
            P(("expert", "fsdp"), None),
            P(("expert", "fsdp"), None),
            P("fsdp"),
            P("fsdp"),
            P("fsdp", None),
            P("fsdp", None),
            P("fsdp"),
            P("fsdp"),
            P("fsdp", None),
            P("expert", "fsdp", None),
            P("expert", "fsdp", None),
        ),
        out_specs=(
            P(("expert", "fsdp"), None),
            P(("expert", "fsdp"), None),
            P("fsdp"),
            P("fsdp"),
            P("fsdp", None),
            P("fsdp", None),
            P("fsdp"),
            P("fsdp"),
            P("fsdp", None),
            P("expert", "fsdp", None),
            P("expert", "fsdp", None),
        ),
        check_vma=False,
    )
```
